32 devices in a mesh: grp: 4 (over y, core), rows: 8 (over z, x).
Axes of the slice: x: 2, y: 2, z: 4, core: 2. Of those that a mesh axis runs over, the one named last changes fastest.
Arguments:
- feature_c2: bfloat16 [1024, 256, 256], P(('grp', 'rows')), may hold values from -6 to 6
- feature_c3: bfloat16 [512, 128, 512], P(('grp', 'rows')), may hold values from -6 to 6
- feature_c4: bfloat16 [256, 64, 1024], P(('grp', 'rows')), may hold values from -6 to 6
- feature_c5: bfloat16 [128, 32, 2048], P(('grp', 'rows')), may hold values from -6 to 6
- cotangent_p2: bfloat16 [1024, 256, 256], P(('grp', 'rows')), may hold values from -6 to 6
- cotangent_p3: bfloat16 [512, 128, 256], P(('grp', 'rows')), may hold values from -6 to 6
- cotangent_p4: bfloat16 [256, 64, 256], P(('grp', 'rows')), may hold values from -6 to 6
- cotangent_p5: bfloat16 [128, 32, 256], P(('grp', 'rows')), may hold values from -6 to 6
- cotangent_p6: bfloat16 [64, 16, 256], P(('grp', 'rows')), may hold values from -6 to 6
- image_heights: int32 [4, 3], P('grp'), may hold values from 1 to 8, 16 in all within a row
- lateral_weight: float32 [3840, 256], P('rows')
- conv_weight: float32 [9216, 256], P('rows'), may hold values from -0.125 to 0.125
- bias_all: float32 [2048], P('rows'), may hold values from -1.75 to 1.75
- lateral_momentum: float32 [3840, 256], P('rows')
- conv_momentum: float32 [9216, 256], P('rows')
- bias_momentum: float32 [2048], P('rows')
- lateral_ema: float32 [3840, 256], P('rows')
- conv_ema: float32 [9216, 256], P('rows'), may hold values from -0.125 to 0.125
- bias_ema: float32 [2048], P('rows'), may hold values from -1.75 to 1.75
Outputs:
- pyramid_p2: bfloat16 [1024, 256, 256], P(('grp', 'rows'))
- pyramid_p3: bfloat16 [512, 128, 256], P(('grp', 'rows'))
- pyramid_p4: bfloat16 [256, 64, 256], P(('grp', 'rows'))
- pyramid_p5: bfloat16 [128, 32, 256], P(('grp', 'rows'))
- pyramid_p6: bfloat16 [64, 16, 256], P(('grp', 'rows'))
- feature_grad_c2: bfloat16 [1024, 256, 256], P(('grp', 'rows'))
- feature_grad_c3: bfloat16 [512, 128, 512], P(('grp', 'rows'))
- feature_grad_c4: bfloat16 [256, 64, 1024], P(('grp', 'rows'))
- feature_grad_c5: bfloat16 [128, 32, 2048], P(('grp', 'rows'))
- lateral_updated: float32 [3840, 256], P('rows')
- conv_updated: float32 [9216, 256], P('rows')
- bias_updated: float32 [2048], P('rows')
- lateral_velocity: float32 [3840, 256], P('rows')
- conv_velocity: float32 [9216, 256], P('rows')
- bias_velocity: float32 [2048], P('rows')
- lateral_average: float32 [3840, 256], P('rows')
- conv_average: float32 [9216, 256], P('rows')
- bias_average: float32 [2048], P('rows')
The draws below stay inside these ranges and needn't reach their ends.
Inputs may be any that keep to these rules, and one draw needn't show every extreme that they name: `image_heights`: row g lists group g's image heights top to bottom in blocks of 64 pixel rows; each row sums to 16.
All inputs are finite; a program needn't handle non-finite values.
Results may differ from the reference program's by a relative error of at most 0.008.
Values may be sent and summed in bfloat16 or wider, within the bound.
A program may use at most 320 MiB of HBM per device.

```python
import math
import jax
import jax.numpy as jnp
import numpy as np
from jax import lax

FPN_CH = 256
C2_CH = 256
C3_CH = 512
C4_CH = 1024
C5_CH = 2048
IMG_W = 256
STEP = 10
ROWS_P5 = 128
ROWS_P4 = 256
ROWS_P3 = 512
ROWS_P2 = 1024
ROWS_P6 = 64
UNITS = 16
MOST = 8
IMGS = 3
CIN = 3840
N_GRP = 4


def lateral_rows(key):
    scales = jnp.concatenate([jnp.full((C2_CH,), C2_CH ** (-0.5), jnp.float32), jnp.full((C3_CH,), C3_CH ** (-0.5), jnp.float32), jnp.full((C4_CH,), C4_CH ** (-0.5), jnp.float32), jnp.full((C5_CH,), C5_CH ** (-0.5), jnp.float32)])
    values = jnp.clip(jax.random.normal(key, (CIN, FPN_CH), jnp.float32), -6.0, 6.0)
    return values * scales[:, None]


def draw_lateral_weight(key, part):
    return lateral_rows(jax.random.fold_in(key, 11))


def draw_lateral_ema(key, part):
    return lateral_rows(jax.random.fold_in(key, 23))


def draw_lateral_momentum(key, part):
    values = jnp.clip(jax.random.normal(jax.random.fold_in(key, 31), (CIN, FPN_CH), jnp.float32), -6.0, 6.0)
    return values * math.sqrt(ROWS_P2 * IMG_W)


def draw_conv_momentum(key, part):
    base = math.sqrt(ROWS_P2 * IMG_W)
    factors = (2.0, math.sqrt(3.0) / 2.0, math.sqrt(2.0) / 4.0, 0.125)
    scales = jnp.concatenate([jnp.full((9 * FPN_CH,), base * factor, jnp.float32) for factor in factors])
    values = jnp.clip(jax.random.normal(jax.random.fold_in(key, 41), (36 * FPN_CH, FPN_CH), jnp.float32), -6.0, 6.0)
    return values * scales[:, None]


def draw_bias_momentum(key, part):
    base = math.sqrt(ROWS_P2 * IMG_W)
    factors = (1.0, math.sqrt(5.0) / 2.0, math.sqrt(21.0) / 4.0, math.sqrt(85.0) / 8.0, 1.0, 0.5, 0.25, 0.125)
    scales = jnp.concatenate([jnp.full((FPN_CH,), base * factor, jnp.float32) for factor in factors])
    values = jnp.clip(jax.random.normal(jax.random.fold_in(key, 53), (8 * FPN_CH,), jnp.float32), -6.0, 6.0)
    return values * scales


def block_scale(stream_key, shape, shards, smallest, top_value):
    loudness = 1.0
    for position, parts in shards:
        heights = jax.random.uniform(jax.random.fold_in(jax.random.fold_in(stream_key, 6), position), (parts,), jnp.float32, smallest / len(shards), top_value / len(shards))
        loudness = loudness * jnp.repeat(jnp.exp(heights), shape[position] // parts).reshape((-1,) + (1,) * (len(shape) - 1 - position))
    return loudness


def length_profile(amount, total, most, lean):
    loads = [(1 << 20) // math.isqrt(grade ** lean) + 1 for grade in range(2, amount + 1)]
    spare, counts = total - most - (amount - 1), [1] * (amount - 1)
    while spare > 0:
        free = [i for i in range(amount - 1) if counts[i] < most]
        mass, left = sum([loads[i] for i in free]), spare
        for i in free:
            extra = min(most - counts[i], max(1, left * loads[i] // mass), spare)
            counts[i] = counts[i] + extra
            spare = spare - extra
    return np.array([most] + counts)


def ragged_sizes(key, count, total, limit, skew):
    if count == 2:
        one = jax.random.randint(key, (), max(1, total - limit), min(limit, total - 1) + 1)
        return jnp.stack([one, total - one])
    tallies = jnp.asarray(length_profile(count, total, limit, skew), jnp.int32)
    twos = (count - 1) // 2
    donor, receiver = tallies[1:1 + 2 * twos:2], tallies[2:2 + 2 * twos:2]
    room = jnp.minimum(donor - 1, limit - receiver)
    passed = jax.random.randint(jax.random.fold_in(key, 1), (twos,), 0, 1 << 20) % (room + 1)
    tallies = tallies.at[1:1 + 2 * twos:2].set(donor - passed).at[2:2 + 2 * twos:2].set(receiver + passed)
    return tallies[jax.random.permutation(jax.random.fold_in(key, 2), count)]


def centred(key, dims, deviation, limit, shards=(), kind=jnp.bfloat16):
    values = deviation * jax.random.normal(key, dims, jnp.float32)
    if shards:
        values = values * block_scale(key, dims, shards, -0.22, 0.18)
    return jnp.clip(values, -limit, limit).astype(kind)


def setup_inputs(seed: int = 0) -> dict:
    keys = jax.random.split(jax.random.key(seed), 20)
    return {
        "feature_c2": centred(keys[0], (ROWS_P2, IMG_W, C2_CH), 1.0, 6.0, ((0, 32),)),
        "feature_c3": centred(keys[1], (ROWS_P3, IMG_W // 2, C3_CH), 1.0, 6.0, ((0, 32),)),
        "feature_c4": centred(keys[2], (ROWS_P4, IMG_W // 4, C4_CH), 1.0, 6.0, ((0, 32),)),
        "feature_c5": centred(keys[3], (ROWS_P5, IMG_W // 8, C5_CH), 1.0, 6.0, ((0, 32),)),
        "cotangent_p2": centred(keys[4], (ROWS_P2, IMG_W, FPN_CH), 1.0, 6.0, ((0, 32),)),
        "cotangent_p3": centred(keys[5], (ROWS_P3, IMG_W // 2, FPN_CH), 1.0, 6.0, ((0, 32),)),
        "cotangent_p4": centred(keys[6], (ROWS_P4, IMG_W // 4, FPN_CH), 1.0, 6.0, ((0, 32),)),
        "cotangent_p5": centred(keys[7], (ROWS_P5, IMG_W // 8, FPN_CH), 1.0, 6.0, ((0, 32),)),
        "cotangent_p6": centred(keys[8], (ROWS_P6, IMG_W // 16, FPN_CH), 1.0, 6.0, ((0, 32),)),
        "image_heights": jax.vmap(lambda own: ragged_sizes(own, IMGS, UNITS, MOST, 2))(jax.random.split(keys[9], N_GRP)).reshape((N_GRP, IMGS)).astype(jnp.int32),
        "lateral_weight": draw_lateral_weight(jax.random.fold_in(keys[19], 71), 0),
        "conv_weight": centred(keys[11], (36 * FPN_CH, FPN_CH), (9 * FPN_CH) ** -0.5, 0.125, ((0, 8),), jnp.float32),
        "bias_all": centred(keys[12], (8 * FPN_CH,), 0.3, 1.75, ((0, 8),), jnp.float32),
        "lateral_momentum": draw_lateral_momentum(jax.random.fold_in(keys[19], 71), 0),
        "conv_momentum": draw_conv_momentum(jax.random.fold_in(keys[19], 71), 0),
        "bias_momentum": draw_bias_momentum(jax.random.fold_in(keys[19], 71), 0),
        "lateral_ema": draw_lateral_ema(jax.random.fold_in(keys[19], 71), 0),
        "conv_ema": centred(keys[17], (36 * FPN_CH, FPN_CH), (9 * FPN_CH) ** -0.5, 0.125, ((0, 8),), jnp.float32),
        "bias_ema": centred(keys[18], (8 * FPN_CH,), 0.3, 1.75, ((0, 8),), jnp.float32),
    }


@jax.custom_vjp
def low(v):
    return lax.optimization_barrier(v.astype(jnp.bfloat16)).astype(jnp.float32)

@jax.custom_vjp
def low_back(v):
    return v

def low_keep(v):
    return (low(v), None)

def low_pass(kept, grad):
    return (grad,)

def back_keep(v):
    return (v, None)

def back_low(kept, grad):
    return (low(grad),)
low.defvjp(low_keep, low_pass)
low_back.defvjp(back_keep, back_low)
precise = lax.Precision.HIGHEST
momentum_rate = 0.9
decay_rate = 0.0001
lateral_rate = 1.2e-05
conv_rate = 8e-06
bias_rate = 0.00013

def upsample(field):
    return jnp.repeat(jnp.repeat(field, 2, axis=0), 2, axis=1)

def edge_keep(image_heights, total, unit):
    canvas = total // N_GRP
    place = jnp.arange(total, dtype=jnp.int32)
    group = place // canvas
    inside = place % canvas
    starts = (jnp.cumsum(image_heights, axis=1) - image_heights).astype(jnp.int32)
    opening = jnp.logical_and(inside % unit == 0, jnp.any((inside // unit)[:, None] == starts[group], axis=1))
    keep = jnp.where(opening, 0.0, 1.0).astype(jnp.float32)
    keep_down = jnp.concatenate([keep[1:], jnp.ones((1,), jnp.float32)])
    return (keep, keep_down)

def conv_level(field, taps, keep_up, keep_down):
    zero_row = jnp.zeros_like(field[:1])
    above = jnp.concatenate([zero_row, field[:-1]], 0) * keep_up[:, None, None]
    below = jnp.concatenate([field[1:], zero_row], 0) * keep_down[:, None, None]
    width = field.shape[1]
    result = jnp.zeros((field.shape[0], width, taps.shape[2]), jnp.float32)
    for row_shift, source in enumerate((above, field, below)):
        widened = jnp.pad(source, ((0, 0), (1, 1), (0, 0)))
        for col_shift in range(3):
            result = result + jnp.einsum('hwc,cd->hwd', widened[:, col_shift:col_shift + width], taps[3 * row_shift + col_shift], precision=precise)
    return result
checked_conv = jax.checkpoint(conv_level)

def nesterov(weight, grad, moment, average, rate, decay):
    ema_keep = min(0.999, (1.0 + STEP) / (10.0 + STEP))
    step_grad = grad + decay * weight
    moment_new = momentum_rate * moment + step_grad
    weight_new = weight - rate * (step_grad + momentum_rate * moment_new)
    average_new = ema_keep * average + (1.0 - ema_keep) * weight_new
    return (weight_new, moment_new, average_new)

def reference(feature_c2, feature_c3, feature_c4, feature_c5, cotangent_p2, cotangent_p3, cotangent_p4, cotangent_p5, cotangent_p6, image_heights, lateral_weight, conv_weight, bias_all, lateral_momentum, conv_momentum, bias_momentum, lateral_ema, conv_ema, bias_ema):
    features = tuple((f.astype(jnp.float32) for f in (feature_c2, feature_c3, feature_c4, feature_c5)))
    edges = [edge_keep(image_heights, total, 16 >> level) for level, total in enumerate((ROWS_P2, ROWS_P3, ROWS_P4, ROWS_P5))]
    bounds = (0, C2_CH, C2_CH + C3_CH, C2_CH + C3_CH + C4_CH, CIN)

    def forward(level_c2, level_c3, level_c4, level_c5, lateral_full, conv_full, bias_full):
        lateral_low = low(lateral_full)
        conv_low = low(conv_full).reshape(4, 9, FPN_CH, FPN_CH)
        bias_low = low(bias_full).reshape(8, FPN_CH)
        laterals = []
        for level, feature in enumerate((level_c2, level_c3, level_c4, level_c5)):
            weight_rows = lateral_low[bounds[level]:bounds[level + 1]]
            laterals.append(low_back(jnp.einsum('hwc,cd->hwd', feature, weight_rows, precision=precise) + bias_low[level]))
        top_down = list(laterals)
        for level in (2, 1, 0):
            top_down[level] = laterals[level] + upsample(top_down[level + 1])
        pyramid = []
        for level in range(4):
            keep_up, keep_down = edges[level]
            pyramid.append(checked_conv(low(top_down[level]), conv_low[level], keep_up, keep_down) + bias_low[4 + level])
        pyramid[3] = low_back(pyramid[3])
        coarse = pyramid[3].reshape(ROWS_P6, 2, IMG_W // 16, 2, FPN_CH).mean(axis=(1, 3))
        return (pyramid[0], pyramid[1], pyramid[2], pyramid[3], coarse)
    outputs, pullback = jax.vjp(forward, features[0], features[1], features[2], features[3], lateral_weight, conv_weight, bias_all)
    cotangents = tuple((c.astype(jnp.float32) for c in (cotangent_p2, cotangent_p3, cotangent_p4, cotangent_p5, cotangent_p6)))
    grads = pullback(cotangents)
    lateral_new, lateral_moment, lateral_avg = nesterov(lateral_weight, grads[4], lateral_momentum, lateral_ema, lateral_rate, decay_rate)
    conv_new, conv_moment, conv_avg = nesterov(conv_weight, grads[5], conv_momentum, conv_ema, conv_rate, decay_rate)
    bias_new, bias_moment, bias_avg = nesterov(bias_all, grads[6], bias_momentum, bias_ema, bias_rate, 0.0)
    return (outputs[0].astype(jnp.bfloat16), outputs[1].astype(jnp.bfloat16), outputs[2].astype(jnp.bfloat16), outputs[3].astype(jnp.bfloat16), outputs[4].astype(jnp.bfloat16), grads[0].astype(jnp.bfloat16), grads[1].astype(jnp.bfloat16), grads[2].astype(jnp.bfloat16), grads[3].astype(jnp.bfloat16), lateral_new, conv_new, bias_new, lateral_moment, conv_moment, bias_moment, lateral_avg, conv_avg, bias_avg)
```

```python
import jax
import jax.numpy as jnp
from jax import lax
from jax.sharding import PartitionSpec as P

FPN_CH = 256
C2_CH = 256
C3_CH = 512
C4_CH = 1024
C5_CH = 2048
STEP = 10


momentum_rate = 0.9
decay_rate = 0.0001
lateral_rate = 1.2e-05
conv_rate = 8e-06
bias_rate = 0.00013


def with_halo(cells, sides, width):
    for axis, dim in sides:
        count = lax.axis_size(axis)
        ends = count - 1
        head = lax.slice_in_dim(cells, 0, width, axis=dim)
        tail = lax.slice_in_dim(cells, cells.shape[dim] - width, cells.shape[dim], axis=dim)
        cells = jnp.concatenate(
            [
                lax.ppermute(tail, axis, [(i, (i + 1) % count) for i in range(ends)]),
                cells,
                lax.ppermute(head, axis, [((i + 1) % count, i) for i in range(ends)]),
            ],
            axis=dim,
        )
    return cells


def upsample(field):
    return jnp.repeat(jnp.repeat(field, 2, axis=0), 2, axis=1)


def downsum(field):
    return field.reshape(field.shape[0] // 2, 2, field.shape[1] // 2, 2, field.shape[2]).sum(
        axis=(1, 3)
    )


def block_keep(image_heights, count, base):
    lengths = image_heights[0]
    order = jnp.arange(lengths.shape[0])
    starts = jnp.sum(jnp.where(order[None, :] < order[:, None], lengths[None, :], 0), axis=1)
    place = base + jnp.arange(count, dtype=jnp.int32)
    opening = jnp.any(place[:, None] == starts[None, :], axis=1)
    return jnp.where(opening, 0.0, 1.0).astype(jnp.bfloat16)


def with_rims(field):
    return with_halo(field, (("rows", 0),), 1)


def in_blocks(padded, keep, unit):
    blocks = []
    for block in range((padded.shape[0] - 2) // unit):
        piece = padded[block * unit : block * unit + unit + 2]
        blocks.append(
            jnp.concatenate(
                [piece[:1] * keep[block], piece[1:-1], piece[-1:] * keep[block + 1]], axis=0
            )
        )
    return jnp.stack(blocks)


def nesterov(weight, grad, moment, average, rate, decay):
    ema_keep = min(0.999, (1.0 + STEP) / (10.0 + STEP))
    step_grad = grad + decay * weight
    moment_new = momentum_rate * moment + step_grad
    weight_new = weight - rate * (step_grad + momentum_rate * moment_new)
    average_new = ema_keep * average + (1.0 - ema_keep) * weight_new
    return (weight_new, moment_new, average_new)


def shards(
    feature_c2,
    feature_c3,
    feature_c4,
    feature_c5,
    cotangent_p2,
    cotangent_p3,
    cotangent_p4,
    cotangent_p5,
    cotangent_p6,
    image_heights,
    lateral_weight,
    conv_weight,
    bias_all,
    lateral_momentum,
    conv_momentum,
    bias_momentum,
    lateral_ema,
    conv_ema,
    bias_ema,
):
    lateral_low, conv_low, bias_low = (
        lax.all_gather(lateral_weight.astype(jnp.bfloat16), "rows", axis=0, tiled=True),
        lax.all_gather(conv_weight.astype(jnp.bfloat16), "rows", axis=0, tiled=True),
        lax.all_gather(bias_all.astype(jnp.bfloat16), "rows", axis=0, tiled=True),
    )
    conv_taps = conv_low.reshape(4, 3, 3, FPN_CH, FPN_CH)
    bias_rows = bias_low.astype(jnp.float32).reshape(8, FPN_CH)
    bounds = (0, C2_CH, C2_CH + C3_CH, C2_CH + C3_CH + C4_CH, C2_CH + C3_CH + C4_CH + C5_CH)
    features = (feature_c2, feature_c3, feature_c4, feature_c5)
    strip = lax.axis_index("rows")
    laterals = []
    for level in range(4):
        weight_rows = lateral_low[bounds[level] : bounds[level + 1]]
        laterals.append(
            jnp.dot(features[level], weight_rows, preferred_element_type=jnp.float32)
            + bias_rows[level]
        )
    top_down = list(laterals)
    for level in (2, 1, 0):
        top_down[level] = laterals[level] + upsample(top_down[level + 1])
    units = [16 >> level for level in range(4)]
    blocks = features[0].shape[0] // units[0]
    keep = block_keep(image_heights, blocks + 1, strip * blocks)
    columns = []
    pyramid = []
    for level in range(4):
        shape = top_down[level].shape
        stacked = in_blocks(with_rims(top_down[level].astype(jnp.bfloat16)), keep, units[level])
        columns.append(stacked)
        pyramid.append(
            lax.conv_general_dilated(
                stacked,
                conv_taps[level],
                (1, 1),
                ((0, 0), (1, 1)),
                dimension_numbers=("NHWC", "HWIO", "NHWC"),
                preferred_element_type=jnp.float32,
            ).reshape(shape)
            + bias_rows[4 + level]
        )
    finest = pyramid[3]
    coarse = finest.reshape(finest.shape[0] // 2, 2, finest.shape[1] // 2, 2, finest.shape[2]).mean(
        axis=(1, 3)
    )
    grad_levels = [
        cotangent_p2,
        cotangent_p3,
        cotangent_p4,
        (
            cotangent_p5.astype(jnp.float32) + 0.25 * upsample(cotangent_p6.astype(jnp.float32))
        ).astype(jnp.bfloat16),
    ]
    conv_grads = []
    output_bias_grads = []
    top_grads = []
    for level in range(4):
        count, width, depth = grad_levels[level].shape
        conv_grads.append(
            lax.conv_general_dilated(
                columns[level],
                grad_levels[level].reshape(blocks, units[level], width, depth),
                (1, 1),
                ((0, 0), (1, 1)),
                dimension_numbers=("CHWN", "IHWO", "HWNC"),
                preferred_element_type=jnp.float32,
            ).reshape(9, FPN_CH, FPN_CH)
        )
        output_bias_grads.append(jnp.sum(grad_levels[level], axis=(0, 1), dtype=jnp.float32))
        back = in_blocks(with_rims(grad_levels[level]), keep, units[level])
        top_grads.append(
            lax.conv_general_dilated(
                back,
                jnp.flip(conv_taps[level], (0, 1)),
                (1, 1),
                ((0, 0), (1, 1)),
                dimension_numbers=("NHWC", "HWOI", "NHWC"),
                preferred_element_type=jnp.float32,
            ).reshape(count, width, depth)
        )
    for level in (1, 2, 3):
        top_grads[level] = top_grads[level] + downsum(top_grads[level - 1])
    lateral_grads = []
    lateral_bias_grads = []
    feature_grads = []
    for level in range(4):
        lowered = top_grads[level].astype(jnp.bfloat16)
        weight_rows = lateral_low[bounds[level] : bounds[level + 1]]
        lateral_grads.append(
            jnp.einsum("rwc,rwd->cd", features[level], lowered, preferred_element_type=jnp.float32)
        )
        lateral_bias_grads.append(jnp.sum(lowered, axis=(0, 1), dtype=jnp.float32))
        feature_grads.append(
            jnp.einsum(
                "rwd,cd->rwc", lowered, weight_rows, preferred_element_type=jnp.float32
            ).astype(jnp.bfloat16)
        )
    grad_lateral = jnp.concatenate(lateral_grads, axis=0)
    grad_conv = jnp.stack(conv_grads).reshape(36 * FPN_CH, FPN_CH)
    grad_bias = jnp.concatenate(lateral_bias_grads + output_bias_grads, axis=0)
    strip_lateral, strip_conv, strip_bias = (
        lax.psum_scatter(grad_lateral.astype(jnp.bfloat16), "rows", scatter_dimension=0, tiled=True),
        lax.psum_scatter(grad_conv.astype(jnp.bfloat16), "rows", scatter_dimension=0, tiled=True),
        lax.psum_scatter(grad_bias, "rows", scatter_dimension=0, tiled=True),
    )
    sum_lateral, sum_conv, sum_bias = (
        lax.psum(strip_lateral.astype(jnp.bfloat16), "grp").astype(jnp.float32),
        lax.psum(strip_conv.astype(jnp.bfloat16), "grp").astype(jnp.float32),
        lax.psum(strip_bias.astype(jnp.bfloat16), "grp").astype(jnp.float32),
    )
    lateral_new, lateral_moment, lateral_avg = nesterov(
        lateral_weight, sum_lateral, lateral_momentum, lateral_ema, lateral_rate, decay_rate
    )
    conv_new, conv_moment, conv_avg = nesterov(
        conv_weight, sum_conv, conv_momentum, conv_ema, conv_rate, decay_rate
    )
    bias_new, bias_moment, bias_avg = nesterov(
        bias_all, sum_bias, bias_momentum, bias_ema, bias_rate, 0.0
    )
    return (
        pyramid[0].astype(jnp.bfloat16),
        pyramid[1].astype(jnp.bfloat16),
        pyramid[2].astype(jnp.bfloat16),
        pyramid[3].astype(jnp.bfloat16),
        coarse.astype(jnp.bfloat16),
        feature_grads[0],
        feature_grads[1],
        feature_grads[2],
        feature_grads[3],
        lateral_new,
        conv_new,
        bias_new,
        lateral_moment,
        conv_moment,
        bias_moment,
        lateral_avg,
        conv_avg,
        bias_avg,
    )


def solution(mesh):
    in_specs = (
        P(("grp", "rows"), None, None),
        P(("grp", "rows"), None, None),
        P(("grp", "rows"), None, None),
        P(("grp", "rows"), None, None),
        P(("grp", "rows"), None, None),
        P(("grp", "rows"), None, None),
        P(("grp", "rows"), None, None),
        P(("grp", "rows"), None, None),
        P(("grp", "rows"), None, None),
        P("grp", None),
        P("rows", None),
        P("rows", None),
        P("rows"),
        P("rows", None),
        P("rows", None),
        P("rows"),
        P("rows", None),
        P("rows", None),
        P("rows"),
    )
    out_specs = (
        P(("grp", "rows"), None, None),
        P(("grp", "rows"), None, None),
        P(("grp", "rows"), None, None),
        P(("grp", "rows"), None, None),
        P(("grp", "rows"), None, None),
        P(("grp", "rows"), None, None),
        P(("grp", "rows"), None, None),
        P(("grp", "rows"), None, None),
        P(("grp", "rows"), None, None),
        P("rows", None),
        P("rows", None),
        P("rows"),
        P("rows", None),
        P("rows", None),
        P("rows"),
        P("rows", None),
        P("rows", None),
        P("rows"),
    )
    return jax.shard_map(shards, mesh=mesh, in_specs=in_specs, out_specs=out_specs, check_vma=False)
```

```python
import functools

import jax
import jax.numpy as jnp
from jax import lax
from jax.experimental import pallas as pl
from jax.experimental.pallas import tpu as pltpu
from jax.sharding import PartitionSpec as P

FPN_CH = 256
C2_CH = 256
C3_CH = 512
C4_CH = 1024
C5_CH = 2048
STEP = 10
LEVELS = 4
TAPS = 9 * FPN_CH
HALF = FPN_CH // 2

momentum_rate = 0.9
decay_rate = 0.0001
lateral_rate = 1.2e-05
conv_rate = 8e-06
bias_rate = 0.00013

MESH = pl.DeviceIdType.MESH
ANY = pl.BlockSpec(memory_space=pl.ANY)
VMEM = pl.BlockSpec(memory_space=pltpu.VMEM)
f32 = jnp.float32
bf16 = jnp.bfloat16
ROOM = 61 << 20


def nesterov(weight, grad, moment, average, rate, decay):
    ema_keep = min(0.999, (1.0 + STEP) / (10.0 + STEP))
    step_grad = grad + decay * weight
    moment_new = momentum_rate * moment + step_grad
    weight_new = weight - rate * (step_grad + momentum_rate * moment_new)
    average_new = ema_keep * average + (1.0 - ema_keep) * weight_new
    return (weight_new, moment_new, average_new)


def block_keep(image_heights, blocks, base, total):
    lengths = image_heights[0]
    order = jnp.arange(lengths.shape[0])
    starts = jnp.sum(jnp.where(order[None, :] < order[:, None], lengths[None, :], 0), axis=1)
    place = base + jnp.arange(blocks + 1, dtype=jnp.int32)
    opening = jnp.logical_or(
        place == total, jnp.any(place[:, None] == starts[None, :], axis=1)
    )
    keep = jnp.where(opening, 0.0, 1.0).astype(f32)
    return jnp.broadcast_to(keep[:, None, None], (blocks + 1, 1, FPN_CH))


class Plan:
    def __init__(self, features, rows_count, lateral_rows, conv_rows):
        self.count = rows_count
        self.rows = [f.shape[0] for f in features]
        self.width = [f.shape[1] for f in features]
        self.depth = [f.shape[2] for f in features]
        self.unit = [16 >> k for k in range(LEVELS)]
        self.blocks = self.rows[0] // self.unit[0]
        self.lateral_rows = lateral_rows
        self.conv_rows = conv_rows
        self.bounds = [sum(self.depth[:k]) for k in range(LEVELS + 1)]


def put_shifted(target, value):
    wide = value.astype(f32)
    width = wide.shape[0]
    at = lax.broadcasted_iota(jnp.int32, wide.shape, 0)
    zero = jnp.zeros_like(wide)
    target[:, 0:FPN_CH] = jnp.where(at == 0, zero, pltpu.roll(wide, 1, 0)).astype(bf16)
    target[:, FPN_CH : 2 * FPN_CH] = value
    target[:, 2 * FPN_CH : 3 * FPN_CH] = jnp.where(
        at == width - 1, zero, pltpu.roll(wide, width - 1, 0)
    ).astype(bf16)


def masked(value, keep):
    return (value.astype(f32) * keep).astype(bf16)


def row_sum(value):
    wide = value.astype(f32)
    return jnp.sum(wide.reshape(wide.shape[0] // 8, 8, wide.shape[1]), axis=0)


def doubled(pairs, base, value):
    count = value.shape[0]
    sides = []
    for side in range(FPN_CH // HALF):
        part = value[:, side * HALF : (side + 1) * HALF]
        pairs[side, pl.ds(base, count, stride=2), :] = part
        pairs[side, pl.ds(base + 1, count, stride=2), :] = part
        sides.append(pairs[side, base : base + 2 * count, :])
    return jnp.concatenate(sides, axis=1)


def halved(pairs, base, value):
    count = value.shape[0] // 2
    sides = []
    for side in range(FPN_CH // HALF):
        pairs[side, base : base + 2 * count, :] = value[:, side * HALF : (side + 1) * HALF]
        sides.append(
            pairs[side, pl.ds(base, count, stride=2), :]
            + pairs[side, pl.ds(base + 1, count, stride=2), :]
        )
    return jnp.concatenate(sides, axis=1)


class Copies:
    def __init__(self, sends, locals_):
        self.sends = sends
        self.locals_ = locals_
        self.sent = []
        self.begun = 0
        self.used = 0

    def remote(self, source, target, arrival, device):
        copy = pltpu.make_async_remote_copy(
            src_ref=source,
            dst_ref=target,
            send_sem=self.sends.at[self.begun],
            recv_sem=arrival,
            device_id=device,
            device_id_type=MESH,
        )
        copy.start()
        self.begun += 1
        self.sent.append(copy)
        return copy

    def settle(self, copy):
        copy.wait_send()
        self.sent = [other for other in self.sent if other is not copy]

    def local(self, source, target):
        copy = pltpu.make_async_copy(source, target, self.locals_.at[self.used])
        self.used += 1
        copy.start()
        return copy

    def drain(self):
        for copy in self.sent:
            copy.wait_send()


def arrived(target, semaphore, device):
    pltpu.make_async_remote_copy(
        src_ref=target,
        dst_ref=target,
        send_sem=semaphore,
        recv_sem=semaphore,
        device_id=device,
        device_id_type=MESH,
    ).wait_recv()


class Place:
    def __init__(self, count):
        self.count = count
        self.spans = count // 2
        self.strip = lax.axis_index("rows")
        self.group = lax.axis_index("grp")
        self.a = self.strip // 2
        self.b = self.strip % 2
        self.y = self.group // 2
        self.c = self.group % 2
        self.core = (self.y * 2 + 1 - self.c, self.strip)
        self.across = ((1 - self.y) * 2 + self.c, self.strip)
        self.beside = (self.group, self.a * 2 + 1 - self.b)

    def span(self, step):
        return lax.rem(self.a + step, self.spans)

    def along(self, step):
        return (self.group, self.span(step) * 2 + self.b)

    def strips(self):
        return [(self.group, lax.rem(self.strip + k, self.count)) for k in range(1, self.count)]


def enter(devices):
    barrier = pltpu.get_barrier_semaphore()
    for device in devices:
        pl.semaphore_signal(barrier, inc=1, device_id=device, device_id_type=MESH)
    pl.semaphore_wait(barrier, len(devices))


class Gather:
    def __init__(self, full, share, place, copies, arrivals):
        self.full = full
        self.share = share
        self.place = place
        self.copies = copies
        self.arrivals = arrivals

    def piece(self, owner, upper, lane):
        half = self.share // 2
        start = pl.multiple_of(owner * self.share + upper * half, 16 if half % 16 == 0 else 8)
        return self.full.at[pl.ds(start, half), pl.ds(pl.multiple_of(lane * HALF, HALF), HALF)]

    def send(self, owner, upper, lane, device):
        part = self.piece(owner, upper, lane)
        self.copies.remote(part, part, self.arrivals.at[owner, upper, lane], device)

    def take(self, owner, upper, lane, device):
        arrived(self.piece(owner, upper, lane), self.arrivals.at[owner, upper, lane], device)

    def start(self):
        at = self.place
        for step in range(1, at.spans):
            self.send(at.strip, at.y, at.c, at.along(step))
        self.send(at.strip, at.y, at.c, at.beside)

    def from_spans(self):
        at = self.place
        for step in range(1, at.spans):
            owner = at.span(step) * 2 + at.b
            self.take(owner, at.y, at.c, at.along(step))
            for device in (at.across, at.beside, at.core):
                self.send(owner, at.y, at.c, device)

    def from_beside(self):
        at = self.place
        for step in range(at.spans):
            owner = at.span(step) * 2 + 1 - at.b
            self.take(owner, at.y, at.c, at.beside)
            for device in (at.across, at.core):
                self.send(owner, at.y, at.c, device)

    def owners(self):
        at = self.place
        own = [at.span(step) * 2 + at.b for step in range(1, at.spans)]
        other = [at.span(step) * 2 + 1 - at.b for step in range(at.spans)]
        return own + other

    def from_across(self):
        at = self.place
        for owner in self.owners():
            self.take(owner, 1 - at.y, at.c, at.across)
            self.send(owner, 1 - at.y, at.c, at.core)

    def from_core(self):
        at = self.place
        for upper in (at.y, 1 - at.y):
            for owner in self.owners():
                self.take(owner, upper, 1 - at.c, at.core)


def backward_kernel(plan, own_lateral, *refs):
    refs = list(refs)

    def take(number):
        taken = refs[:number]
        del refs[:number]
        return taken

    features = take(4)
    grads = take(4)
    (coarse_grad, keep, lateral_in, conv_in, bias_in) = take(5)
    (conv_out, lateral_out, bias_out) = take(3)
    tops_out = take(4)
    lows_out = take(4)
    (conv_grad_out, lateral_grad_out, bias_grad_out) = take(3)
    c_v = take(4)
    g_v = take(4)
    (p6_v,) = take(1)
    wide = take(4)
    x_v = take(4)
    (t1, t2, t3) = take(3)
    (conv_v, lateral_v, bias_v, conv_own, lateral_own) = take(5)
    (acc, stage, pairs, bias_acc) = take(4)
    g_halo = take(4)
    x_halo = take(4)
    (send_sems, local_sems, conv_sems, lateral_sems, bias_sems, halo_sems) = take(6)
    sums = [None, t1, t2, t3]
    rows, width, depth, unit, blocks = plan.rows, plan.width, plan.depth, plan.unit, plan.blocks

    at = Place(plan.count)
    copies = Copies(send_sems, local_sems)
    if own_lateral:
        lateral_load = copies.local(lateral_in, lateral_own)
    else:
        lateral_load = copies.local(lateral_in, lateral_v)
    conv_load = copies.local(conv_in, conv_own)
    grad_loads = [copies.local(grads[k], g_v[k]) for k in (3, 2, 1, 0)][::-1]
    coarse_load = copies.local(coarse_grad, p6_v)
    feature_loads = [copies.local(features[k], c_v[k]) for k in (3, 2, 1, 0)][::-1]
    strips = at.strips()
    enter(strips + [at.core, at.across])

    conv = Gather(conv_v, plan.conv_rows, at, copies, conv_sems)
    lateral = Gather(lateral_v, plan.lateral_rows, at, copies, lateral_sems)
    lateral_load.wait()
    if own_lateral:
        start = pl.multiple_of(at.strip * plan.lateral_rows, 16)
        lateral_v[pl.ds(start, plan.lateral_rows), :] = lateral_own[...].astype(bf16)
        lateral.start()
    bias_v[at.strip] = bias_in[...]
    for device in strips:
        copies.remote(bias_in, bias_v.at[at.strip], bias_sems.at[at.strip], device)
    conv_load.wait()
    start = pl.multiple_of(at.strip * plan.conv_rows, 16)
    conv_v[pl.ds(start, plan.conv_rows), :] = conv_own[...].astype(bf16)
    conv.start()

    grad_loads[3].wait()
    coarse_load.wait()
    for r in range(rows[3] // 2):
        quarter = doubled(pairs, 0, 0.25 * p6_v[r].astype(f32))
        for s in range(2):
            whole = g_v[3][2 * r + s].astype(f32) + quarter
            g_v[3][2 * r + s] = whole.astype(bf16)

    above = (at.group, lax.rem(at.strip + at.count - 1, at.count))
    below = (at.group, lax.rem(at.strip + 1, at.count))

    def send_rims(first, last, halo, index):
        return [
            copies.remote(first, halo.at[1], halo_sems.at[index, 1], above),
            copies.remote(last, halo.at[0], halo_sems.at[index, 0], below),
        ]

    def take_rims(halo, index):
        arrived(halo.at[0], halo_sems.at[index, 0], above)
        arrived(halo.at[1], halo_sems.at[index, 1], below)

    rims = []
    for k in (3, 2, 1, 0):
        if k < 3:
            grad_loads[k].wait()
        rims += send_rims(g_v[k].at[0], g_v[k].at[rows[k] - 1], g_halo[k], k)

    bias_acc[...] = jnp.zeros_like(bias_acc)

    def spread(k):
        for j in range(blocks):

            def body(i, carry):
                value = g_v[k][j * unit[k] + i]
                put_shifted(wide[k].at[j, i + 1], value)
                bias_acc[LEVELS + k] += row_sum(value)
                return carry

            lax.fori_loop(0, unit[k], body, 0)
            if j > 0:
                put_shifted(wide[k].at[j, 0], masked(g_v[k][j * unit[k] - 1], keep[j]))
            if j < blocks - 1:
                put_shifted(
                    wide[k].at[j, unit[k] + 1], masked(g_v[k][(j + 1) * unit[k]], keep[j + 1])
                )

    for k in range(LEVELS):
        spread(k)
    if own_lateral:
        lateral.from_spans()
    for k in range(LEVELS):
        take_rims(g_halo[k], k)
        put_shifted(wide[k].at[0, 0], masked(g_halo[k][0], keep[0]))
        put_shifted(wide[k].at[blocks - 1, unit[k] + 1], masked(g_halo[k][1], keep[blocks]))
    if own_lateral:
        lateral.from_beside()
        lateral.from_across()
        lateral.from_core()
    outs = [copies.local(lateral_v, lateral_out)]
    for k, device in enumerate(strips):
        owner = lax.rem(at.strip + k + 1, at.count)
        arrived(bias_v.at[owner], bias_sems.at[owner], device)
    per = plan.count // 8
    for j in range(8):
        total = bias_v[j * per]
        for other in range(1, per):
            total = total + bias_v[j * per + other]
        bias_out[j] = total

    def lateral_rows(k, r, count):
        pixels = count * width[k]
        value = jnp.dot(
            c_v[k][pl.ds(r, count)].reshape(pixels, depth[k]),
            lateral_v[plan.bounds[k] : plan.bounds[k + 1], :],
            preferred_element_type=f32,
        )
        value = (value + bias_out[k][0:1, :]).reshape(count, width[k], FPN_CH)
        if k == 3:
            tops = [value[s] for s in range(count)]
        else:
            tops = []
            for s in range(count // 2):
                raised = doubled(pairs, s * width[k], sums[k + 1][r // 2 + s])
                tops += [value[2 * s] + raised, value[2 * s + 1] + raised]
        return tops

    def lateral_block(k, j, count):
        def body(i, carry):
            tops = lateral_rows(k, j * unit[k] + i * count, count)
            for s in range(count):
                if k:
                    sums[k][j * unit[k] + i * count + s] = tops[s]
                x_v[k][j, i * count + s + 1] = tops[s].astype(bf16)
            return carry

        lax.fori_loop(0, unit[k] // count, body, 0)

    for k in (3, 2, 1, 0):
        feature_loads[k].wait()
        for j in range(blocks):
            lateral_block(k, j, min(4, unit[k]))
        send_rims(x_v[k].at[0, 1], x_v[k].at[blocks - 1, unit[k]], x_halo[k], LEVELS + k)
        for j in range(1, blocks):
            x_v[k][j - 1, unit[k] + 1] = masked(x_v[k][j, 1], keep[j])
            x_v[k][j, 0] = masked(x_v[k][j - 1, unit[k]], keep[j])
    conv.from_spans()

    flushes = [None, None]
    flushed = [0]

    def flush(count, target):
        slot = flushed[0] % 2
        flushes[slot] = copies.local(stage.at[slot, pl.ds(0, count)], target)
        flushed[0] += 1

    def stage_slot():
        slot = flushed[0] % 2
        if flushes[slot] is not None:
            flushes[slot].wait()
        return slot

    def tap_dots(k, chunks):
        for dy in range(3):
            x = jnp.concatenate(
                [x_v[k][j, pl.ds(i + 1, n)].reshape(n * width[k], FPN_CH) for j, i, n in chunks],
                axis=0,
            )
            g = jnp.concatenate(
                [
                    wide[k][j, pl.ds(i + dy, n)].reshape(n * width[k], 3 * FPN_CH)
                    for j, i, n in chunks
                ],
                axis=0,
            )
            dot = lax.dot_general(x, g, (((0,), (0,)), ((), ())), preferred_element_type=f32)
            yield dy, dot

    def finish_taps(k):
        slot = stage_slot()
        for tap in range(9):
            part = acc[:, (8 - tap) * FPN_CH : (9 - tap) * FPN_CH]
            stage[slot, tap * FPN_CH : (tap + 1) * FPN_CH, :] = part.astype(bf16)
        flush(TAPS, conv_grad_out.at[pl.ds(k * TAPS, TAPS)])

    def tap_grads(k):
        for dy, dot in tap_dots(k, [(j, 0, unit[k]) for j in range(blocks)]):
            acc[:, dy * 3 * FPN_CH : (dy + 1) * 3 * FPN_CH] = dot
        finish_taps(k)

    def tap_block(k, j, count):
        def body(i, carry):
            for dy, dot in tap_dots(k, [(j, i * count, count)]):
                acc[:, dy * 3 * FPN_CH : (dy + 1) * 3 * FPN_CH] += dot
            return carry

        lax.fori_loop(0, unit[k] // count, body, 0)

    for k in (3, 2, 1):
        tap_grads(k)
    conv.from_beside()
    acc[...] = jnp.zeros_like(acc)
    for j in range(blocks):
        tap_block(0, j, 8)
        if j == 0:
            conv.from_across()
    finish_taps(0)
    conv.from_core()
    outs.append(copies.local(conv_v, conv_out))

    def top_rows(k, j, i, count):
        pixels = count * width[k]
        value = None
        for dy in range(3):
            for dx in range(3):
                tap = 8 - (3 * dy + dx)
                start = k * TAPS + tap * FPN_CH
                dot = lax.dot_general(
                    wide[k][j, pl.ds(i + dy, count), :, dx * FPN_CH : (dx + 1) * FPN_CH].reshape(
                        pixels, FPN_CH
                    ),
                    conv_v[start : start + FPN_CH, :],
                    (((1,), (1,)), ((), ())),
                    preferred_element_type=f32,
                )
                value = dot if value is None else value + dot
        value = value.reshape(count, width[k], FPN_CH)
        first = j * unit[k] + i
        if k:
            value = value + sums[k][pl.ds(first, count)]
        low = value.astype(bf16)
        g_v[k][pl.ds(first, count)] = low
        bias_acc[k] += row_sum(low.reshape(pixels, FPN_CH))
        if k < 3:
            for s in range(count // 2):
                sums[k + 1][first // 2 + s] = halved(
                    pairs, s * width[k], value[2 * s] + value[2 * s + 1]
                )

    for copy in rims:
        copies.settle(copy)
    for k in range(LEVELS):
        count = min(4, unit[k])
        for j in range(blocks):

            def body(i, carry, k=k, j=j, count=count):
                top_rows(k, j, i * count, count)
                return carry

            lax.fori_loop(0, unit[k] // count, body, 0)
        outs.append(copies.local(g_v[k], lows_out[k]))

    for k in range(LEVELS):
        slot = stage_slot()
        if k == 0:
            count = min(8, rows[0])
            acc[:, 0 : depth[0]] = jnp.zeros((FPN_CH, depth[0]), f32)

            def body(i, carry, count=count):
                acc[:, 0 : depth[0]] += lax.dot_general(
                    c_v[0][pl.ds(i * count, count)].reshape(count * width[0], depth[0]),
                    g_v[0][pl.ds(i * count, count)].reshape(count * width[0], FPN_CH),
                    (((0,), (0,)), ((), ())),
                    preferred_element_type=f32,
                )
                return carry

            lax.fori_loop(0, rows[0] // count, body, 0)
            value = acc[:, 0 : depth[0]]
        else:
            value = lax.dot_general(
                c_v[k][...].reshape(rows[k] * width[k], depth[k]),
                g_v[k][...].reshape(rows[k] * width[k], FPN_CH),
                (((0,), (0,)), ((), ())),
                preferred_element_type=f32,
            )
        stage[slot, 0 : depth[k], :] = value.astype(bf16)
        flush(depth[k], lateral_grad_out.at[pl.ds(plan.bounds[k], depth[k])])

    for j in range(8):
        bias_grad_out[j] = jnp.broadcast_to(
            jnp.sum(bias_acc[j], axis=0, keepdims=True), bias_acc[j].shape
        )
    for k in range(LEVELS):
        take_rims(x_halo[k], LEVELS + k)
        x_v[k][0, 0] = masked(x_halo[k][0], keep[0])
        x_v[k][blocks - 1, unit[k] + 1] = masked(x_halo[k][1], keep[blocks])
        outs.append(copies.local(x_v[k], tops_out[k]))
    for copy in outs:
        copy.wait()
    for copy in flushes:
        copy.wait()
    copies.drain()


def backward(plan, own_lateral, features, grads, coarse_grad, keep, lateral, conv, bias):
    rows, width, depth, unit, blocks = plan.rows, plan.width, plan.depth, plan.unit, plan.blocks
    shape = jax.ShapeDtypeStruct
    padded = [(blocks, unit[k] + 2, width[k]) for k in range(LEVELS)]
    total = plan.bounds[LEVELS]
    out_shape = (
        [shape((LEVELS * TAPS, FPN_CH), bf16), shape((total, FPN_CH), bf16)]
        + [shape((8, 8, FPN_CH), f32)]
        + [shape((*padded[k], FPN_CH), bf16) for k in range(LEVELS)]
        + [shape((rows[k], width[k], FPN_CH), bf16) for k in range(LEVELS)]
        + [shape((LEVELS * TAPS, FPN_CH), bf16), shape((total, FPN_CH), bf16)]
        + [shape((8, 8, FPN_CH), f32)]
    )
    v = pltpu.VMEM
    dma = pltpu.SemaphoreType.DMA
    pieces = 9 * plan.count + 32
    scratch = (
        [v((rows[k], width[k], depth[k]), bf16) for k in range(LEVELS)]
        + [v((rows[k], width[k], FPN_CH), bf16) for k in range(LEVELS)]
        + [v(coarse_grad.shape, bf16)]
        + [v((*padded[k], 3 * FPN_CH), bf16) for k in range(LEVELS)]
        + [v((*padded[k], FPN_CH), bf16) for k in range(LEVELS)]
        + [v((rows[k], width[k], FPN_CH), f32) for k in (1, 2, 3)]
        + [v((LEVELS * TAPS, FPN_CH), bf16), v((total, FPN_CH), bf16), v((plan.count, 8, FPN_CH), f32)]
        + [v(conv.shape, f32), v(lateral.shape if own_lateral else (8, FPN_CH), f32)]
        + [v((FPN_CH, TAPS), f32), v((2, TAPS, FPN_CH), bf16)]
        + [v((FPN_CH // HALF, 2 * width[0], HALF), f32), v((8, 8, FPN_CH), f32)]
        + [v((2, width[k], FPN_CH), bf16) for k in range(LEVELS)] * 2
        + [dma((pieces,)), dma((40,)), dma((plan.count, 2, 2)), dma((plan.count, 2, 2))]
        + [dma((plan.count,)), dma((2 * LEVELS, 2))]
    )
    outs = pl.pallas_call(
        functools.partial(backward_kernel, plan, own_lateral),
        out_shape=out_shape,
        in_specs=[ANY] * 9 + [VMEM, ANY, ANY, VMEM],
        out_specs=[ANY, ANY, VMEM] + [ANY] * 8 + [ANY, ANY, VMEM],
        scratch_shapes=scratch,
        name="backward",
        cost_estimate=pl.CostEstimate(
            flops=30 << 30, bytes_accessed=60 << 20, transcendentals=0
        ),
        compiler_params=pltpu.CompilerParams(
            collective_id=0, has_side_effects=True, vmem_limit_bytes=ROOM
        ),
    )(*features, *grads, coarse_grad, keep, lateral, conv, bias)
    return outs


def pyramid_kernel(plan, number, *refs):
    rows, width, unit, blocks = plan.rows, plan.width, plan.unit, plan.blocks
    levels = list(range(number[0], number[1]))
    refs = list(refs)
    x_v = dict(zip(levels, refs[: len(levels)]))
    taps, bias = refs[len(levels) : len(levels) + 2]
    outs = refs[len(levels) + 2 :]
    p_v = dict(zip(levels, outs[: len(levels)]))
    rest = outs[len(levels) :]
    if 3 in levels:
        coarse_out = rest[0]
        rest = rest[1:]
    wide = dict(zip(levels, rest[: len(levels)]))
    pairs = rest[len(levels)]
    for k in levels:
        for j in range(blocks):

            def widen(i, carry, k=k, j=j):
                put_shifted(wide[k].at[j, i], x_v[k][j, i])
                return carry

            lax.fori_loop(0, unit[k] + 2, widen, 0)
        count = min(4, unit[k])
        for j in range(blocks):

            def body(i, carry, k=k, j=j, count=count):
                pixels = count * width[k]
                tile = jnp.concatenate(
                    [
                        wide[k][j, pl.ds(i * count + dy, count)].reshape(pixels, 3 * FPN_CH)
                        for dy in range(3)
                    ],
                    axis=1,
                )
                start = (k - levels[0]) * TAPS
                value = jnp.dot(tile, taps[start : start + TAPS, :], preferred_element_type=f32)
                value = (value + bias[LEVELS + k][0:1, :]).reshape(count, width[k], FPN_CH)
                p_v[k][pl.ds(j * unit[k] + i * count, count)] = value.astype(bf16)
                if k == 3:
                    for s in range(count // 2):
                        mean = 0.25 * halved(pairs, 0, value[2 * s] + value[2 * s + 1])
                        coarse_out[j * unit[k] // 2 + i * count // 2 + s] = mean.astype(bf16)
                return carry

            lax.fori_loop(0, unit[k] // count, body, 0)


def pyramids(plan, tops, taps, bias, first, last):
    levels = range(first, last)
    rows, width, unit, blocks = plan.rows, plan.width, plan.unit, plan.blocks
    out_shape = [jax.ShapeDtypeStruct((rows[k], width[k], FPN_CH), bf16) for k in levels]
    if last == LEVELS:
        out_shape.append(jax.ShapeDtypeStruct((rows[3] // 2, width[3] // 2, FPN_CH), bf16))
    pixels = sum(rows[k] * width[k] for k in levels)
    return pl.pallas_call(
        functools.partial(pyramid_kernel, plan, (first, last)),
        out_shape=out_shape,
        in_specs=[VMEM] * (len(levels) + 2),
        out_specs=[VMEM] * len(out_shape),
        scratch_shapes=[
            pltpu.VMEM((blocks, unit[k] + 2, width[k], 3 * FPN_CH), bf16) for k in levels
        ]
        + [pltpu.VMEM((FPN_CH // HALF, width[3], HALF), f32)],
        name="pyramid",
        cost_estimate=pl.CostEstimate(
            flops=2 * pixels * TAPS * FPN_CH, bytes_accessed=4 * pixels * FPN_CH, transcendentals=0
        ),
        compiler_params=pltpu.CompilerParams(vmem_limit_bytes=ROOM),
    )(*tops[first:last], taps, bias)


def feature_kernel(plan, *refs):
    lows, lateral, outs = refs[:LEVELS], refs[LEVELS], refs[LEVELS + 1 :]
    for k in range(LEVELS):
        count = max(1, min(plan.rows[k], 1024 // plan.width[k]))

        def body(i, carry, k=k, count=count):
            value = lax.dot_general(
                lows[k][pl.ds(i * count, count)].reshape(count * plan.width[k], FPN_CH),
                lateral[plan.bounds[k] : plan.bounds[k + 1], :],
                (((1,), (1,)), ((), ())),
                preferred_element_type=f32,
            )
            outs[k][pl.ds(i * count, count)] = value.astype(bf16).reshape(
                count, plan.width[k], plan.depth[k]
            )
            return carry

        lax.fori_loop(0, plan.rows[k] // count, body, 0)


def feature_grads(plan, lows, lateral):
    shapes = [(plan.rows[k], plan.width[k], plan.depth[k]) for k in range(LEVELS)]
    return pl.pallas_call(
        functools.partial(feature_kernel, plan),
        out_shape=[jax.ShapeDtypeStruct(s, bf16) for s in shapes],
        in_specs=[VMEM] * (LEVELS + 1),
        out_specs=[VMEM] * LEVELS,
        name="features",
        cost_estimate=pl.CostEstimate(flops=2 << 30, bytes_accessed=15 << 20, transcendentals=0),
        compiler_params=pltpu.CompilerParams(vmem_limit_bytes=ROOM),
    )(*lows, lateral)


class Scatter:
    def __init__(self, share, grad, own, by_core, by_beside, by_across, by_span, total, place, copies, sems):
        self.share = share
        self.half = share // 2
        self.grad, self.own = grad, own
        self.by_core, self.by_beside, self.by_across, self.by_span = by_core, by_beside, by_across, by_span
        self.total = total
        self.place = place
        self.copies = copies
        self.core_sems, self.beside_sems, self.across_sems, self.span_sems, self.last_sems = sems

    def lanes(self, lane):
        return pl.ds(pl.multiple_of(lane * HALF, HALF), HALF)

    def rows_of(self, owner):
        return pl.ds(pl.multiple_of(owner * self.share, 16), self.share)

    def half_rows(self, base, upper):
        step = 16 if self.half % 16 == 0 else 8
        return pl.ds(pl.multiple_of(base + upper * self.half, step), self.half)

    def owners(self, beside):
        at = self.place
        side = 1 - at.b if beside else at.b
        return [at.span(step) * 2 + side for step in range(1, at.spans)] + [at.a * 2 + side]

    def start(self):
        at = self.place
        for beside in (True, False):
            for owner in self.owners(beside):
                self.copies.remote(
                    self.grad.at[self.rows_of(owner), self.lanes(1 - at.c)],
                    self.by_core.at[self.rows_of(owner)],
                    self.core_sems.at[owner],
                    at.core,
                )

    def to_beside(self):
        at = self.place
        for step, owner in enumerate(self.owners(True)):
            rows = self.rows_of(owner)
            arrived(self.by_core.at[rows], self.core_sems.at[owner], at.core)
            value = self.own[rows, self.lanes(at.c)].astype(f32) + self.by_core[rows, :].astype(f32)
            self.by_core[rows, :] = value.astype(bf16)
            slot = pl.ds(pl.multiple_of(owner // 2 * self.share, 16), self.share)
            self.copies.remote(
                self.by_core.at[rows],
                self.by_beside.at[slot],
                self.beside_sems.at[owner // 2],
                at.beside,
            )

    def to_across(self):
        at = self.place
        for owner in self.owners(False):
            rows = self.rows_of(owner)
            span = owner // 2
            slot = pl.ds(pl.multiple_of(span * self.share, 16), self.share)
            arrived(self.by_core.at[rows], self.core_sems.at[owner], at.core)
            arrived(self.by_beside.at[slot], self.beside_sems.at[span], at.beside)
            value = (
                self.own[rows, self.lanes(at.c)].astype(f32)
                + self.by_core[rows, :].astype(f32)
                + self.by_beside[slot, :].astype(f32)
            )
            self.by_core[rows, :] = value.astype(bf16)
            self.copies.remote(
                self.by_core.at[self.half_rows(owner * self.share, 1 - at.y)],
                self.by_across.at[self.half_rows(span * self.half, 0)],
                self.across_sems.at[span],
                at.across,
            )

    def to_spans(self):
        at = self.place
        for step in range(1, at.spans + 1):
            span = at.span(step) if step < at.spans else at.a
            owner = span * 2 + at.b
            slot = self.half_rows(span * self.half, 0)
            mine = self.half_rows(owner * self.share, at.y)
            arrived(self.by_across.at[slot], self.across_sems.at[span], at.across)
            value = self.by_core[mine, :].astype(f32) + self.by_across[slot, :].astype(f32)
            self.by_across[slot, :] = value.astype(bf16)
            if step < at.spans:
                self.copies.remote(
                    self.by_across.at[slot],
                    self.by_span.at[self.half_rows(at.a * self.half, 0)],
                    self.span_sems.at[at.a],
                    at.along(step),
                )

    def finish(self):
        at = self.place
        mine = self.half_rows(at.a * self.half, 0)
        value = self.by_across[mine, :].astype(f32)
        for step in range(1, at.spans):
            span = at.span(step)
            slot = self.half_rows(span * self.half, 0)
            arrived(self.by_span.at[slot], self.span_sems.at[span], at.along(step))
            value = value + self.by_span[slot, :].astype(f32)
        part = self.total.at[self.half_rows(0, at.y), self.lanes(at.c)]
        part[...] = value
        self.copies.remote(part, part, self.last_sems.at[at.y, at.c], at.across)
        self.copies.remote(part, part, self.last_sems.at[at.y, at.c], at.core)

    def join(self):
        at = self.place
        other = self.total.at[self.half_rows(0, 1 - at.y), self.lanes(at.c)]
        arrived(other, self.last_sems.at[1 - at.y, at.c], at.across)
        self.copies.remote(other, other, self.last_sems.at[1 - at.y, at.c], at.core)

    def close(self):
        at = self.place
        for upper in (at.y, 1 - at.y):
            part = self.total.at[self.half_rows(0, upper), self.lanes(1 - at.c)]
            arrived(part, self.last_sems.at[upper, 1 - at.c], at.core)


def scatter_shapes(share, count):
    v = pltpu.VMEM
    dma = pltpu.SemaphoreType.DMA
    spans = count // 2
    return [
        v((share * count, FPN_CH), bf16),
        v((share * count, HALF), bf16),
        v((share * spans, HALF), bf16),
        v((share // 2 * spans, HALF), bf16),
        v((share // 2 * spans, HALF), bf16),
        v((share, FPN_CH), f32),
        dma((count,)),
        dma((spans,)),
        dma((spans,)),
        dma((spans,)),
        dma((2, 2)),
    ]


def sum_kernel(plan, own_lateral, *refs):
    refs = list(refs)
    shares = [plan.conv_rows] + ([plan.lateral_rows] if own_lateral else [])
    number = len(shares)
    grads = refs[:number]
    bias_grad = refs[number]
    totals = refs[number + 1 : 2 * number + 1]
    bias_total = refs[2 * number + 1]
    rest = refs[2 * number + 2 :]
    parts = [rest[11 * i : 11 * i + 11] for i in range(number)]
    bias_v, send_sems, local_sems, bias_sems = rest[11 * number :]
    at = Place(plan.count)
    copies = Copies(send_sems, local_sems)
    loads = [copies.local(grads[i], parts[i][0]) for i in range(number)]
    strips = at.strips()
    enter(strips + [at.core, at.across])
    scatters = []
    for i, share in enumerate(shares):
        part = parts[i]
        scatters.append(
            Scatter(share, grads[i], part[0], *part[1:5], part[5], at, copies, part[6:11])
        )
    for scatter in scatters:
        scatter.start()
    bias_v[at.strip] = bias_grad[...]
    for device in strips:
        copies.remote(bias_grad, bias_v.at[at.strip], bias_sems.at[at.strip], device)
    for load in loads:
        load.wait()
    for scatter in scatters:
        scatter.to_beside()
    for scatter in scatters:
        scatter.to_across()
    for k, device in enumerate(strips):
        owner = lax.rem(at.strip + k + 1, at.count)
        arrived(bias_v.at[owner], bias_sems.at[owner], device)
    total = bias_v[0]
    for k in range(1, plan.count):
        total = total + bias_v[k]
    across, core = plan.count, plan.count + 1
    bias_v[across + 2] = total
    copies.remote(bias_v.at[across + 2], bias_v.at[across], bias_sems.at[across], at.across)
    arrived(bias_v.at[across], bias_sems.at[across], at.across)
    total = total + bias_v[across]
    bias_v[across + 3] = total
    copies.remote(bias_v.at[across + 3], bias_v.at[core], bias_sems.at[core], at.core)
    for scatter in scatters:
        scatter.to_spans()
    for scatter in scatters:
        scatter.finish()
    arrived(bias_v.at[core], bias_sems.at[core], at.core)
    bias_total[...] = total + bias_v[core]
    for scatter in scatters:
        scatter.join()
    for scatter in scatters:
        scatter.close()
    for i in range(number):
        totals[i][...] = parts[i][5][...]
    copies.drain()


def sum_grads(plan, own_lateral, conv, lateral, bias):
    shares = [plan.conv_rows] + ([plan.lateral_rows] if own_lateral else [])
    grads = [conv] + ([lateral] if own_lateral else [])
    dma = pltpu.SemaphoreType.DMA
    scratch = []
    for share in shares:
        scratch += scatter_shapes(share, plan.count)
    scratch += [
        pltpu.VMEM((plan.count + 4, 8, FPN_CH), f32),
        dma((8 * plan.count + 16,)),
        dma((4,)),
        dma((plan.count + 2,)),
    ]
    return pl.pallas_call(
        functools.partial(sum_kernel, plan, own_lateral),
        out_shape=[jax.ShapeDtypeStruct((share, FPN_CH), f32) for share in shares]
        + [jax.ShapeDtypeStruct((8, FPN_CH), f32)],
        in_specs=[ANY] * len(shares) + [VMEM],
        out_specs=[VMEM] * (len(shares) + 1),
        scratch_shapes=scratch,
        name="sums",
        cost_estimate=pl.CostEstimate(flops=1 << 20, bytes_accessed=20 << 20, transcendentals=0),
        compiler_params=pltpu.CompilerParams(
            collective_id=1, has_side_effects=True, vmem_limit_bytes=ROOM
        ),
    )(*grads, bias)


def shards(
    feature_c2,
    feature_c3,
    feature_c4,
    feature_c5,
    cotangent_p2,
    cotangent_p3,
    cotangent_p4,
    cotangent_p5,
    cotangent_p6,
    image_heights,
    lateral_weight,
    conv_weight,
    bias_all,
    lateral_momentum,
    conv_momentum,
    bias_momentum,
    lateral_ema,
    conv_ema,
    bias_ema,
):
    features = (feature_c2, feature_c3, feature_c4, feature_c5)
    grads = (cotangent_p2, cotangent_p3, cotangent_p4, cotangent_p5)
    count = lax.axis_size("rows")
    strip = lax.axis_index("rows")
    plan = Plan(features, count, lateral_weight.shape[0], conv_weight.shape[0])
    own_lateral = plan.lateral_rows % 16 == 0
    keep = block_keep(image_heights, plan.blocks, strip * plan.blocks, plan.blocks * count)
    share = bias_all.shape[0]
    place = lax.rem(strip * share, FPN_CH)
    bias_low = bias_all.astype(bf16).astype(f32)
    bias_row = jnp.tile(bias_low, FPN_CH // share)
    lane = jnp.arange(FPN_CH)
    inside = jnp.logical_and(lane >= place, lane < place + share)
    bias_row = jnp.broadcast_to(jnp.where(inside, bias_row, 0.0)[None, :], (8, FPN_CH))
    if own_lateral:
        lateral_in = lateral_weight
    else:
        lateral_in = lax.all_gather(lateral_weight.astype(bf16), "rows", axis=0, tiled=True)
    results = backward(
        plan, own_lateral, features, grads, cotangent_p6, keep, lateral_in, conv_weight, bias_row
    )
    taps, lateral_low, bias_rows = results[:3]
    tops = results[3:7]
    lows = results[7:11]
    conv_grad, lateral_grad, bias_grad = results[11:]
    finest = pyramids(plan, tops, taps[:TAPS], bias_rows, 0, 1)
    others = pyramids(plan, tops, taps[TAPS:], bias_rows, 1, LEVELS)
    feature_outs = feature_grads(plan, lows, lateral_low)
    sums = sum_grads(plan, own_lateral, conv_grad, lateral_grad, bias_grad[:, 0, :])
    sum_conv, sum_bias = sums[0], sums[-1].reshape(-1)
    if own_lateral:
        sum_lateral = sums[1]
    else:
        sum_lateral = lax.psum(
            lax.psum_scatter(lateral_grad, "rows", scatter_dimension=0, tiled=True), "grp"
        ).astype(f32)
    sum_bias = lax.dynamic_slice_in_dim(sum_bias, strip * share, share)
    lateral_new, lateral_moment, lateral_avg = nesterov(
        lateral_weight, sum_lateral, lateral_momentum, lateral_ema, lateral_rate, decay_rate
    )
    conv_new, conv_moment, conv_avg = nesterov(
        conv_weight, sum_conv, conv_momentum, conv_ema, conv_rate, decay_rate
    )
    bias_new, bias_moment, bias_avg = nesterov(
        bias_all, sum_bias, bias_momentum, bias_ema, bias_rate, 0.0
    )
    return (
        finest[0],
        *others,
        *feature_outs,
        lateral_new,
        conv_new,
        bias_new,
        lateral_moment,
        conv_moment,
        bias_moment,
        lateral_avg,
        conv_avg,
        bias_avg,
    )


def solution(mesh):
    cut = P(("grp", "rows"), None, None)
    wide = P("rows", None)
    in_specs = (cut,) * 9 + (P("grp", None),) + (wide, wide, P("rows")) * 3
    out_specs = (cut,) * 9 + (wide, wide, P("rows")) * 3
    return jax.shard_map(
        shards,
        mesh=mesh,
        in_specs=in_specs,
        out_specs=out_specs,
        check_vma=False,
    )
```

```python
import functools

import jax
import jax.numpy as jnp
from jax import lax
from jax.experimental import pallas as pl
from jax.experimental.pallas import tpu as pltpu
from jax.sharding import PartitionSpec as P

FPN_CH = 256
C2_CH = 256
C3_CH = 512
C4_CH = 1024
C5_CH = 2048
STEP = 10
LEVELS = 4
TAPS = 9 * FPN_CH
HALF = FPN_CH // 2

momentum_rate = 0.9
decay_rate = 0.0001
lateral_rate = 1.2e-05
conv_rate = 8e-06
bias_rate = 0.00013

MESH = pl.DeviceIdType.MESH
ANY = pl.BlockSpec(memory_space=pl.ANY)
VMEM = pl.BlockSpec(memory_space=pltpu.VMEM)
f32 = jnp.float32
bf16 = jnp.bfloat16
ROOM = 63 << 20


def nesterov(weight, grad, moment, average, rate, decay):
    ema_keep = min(0.999, (1.0 + STEP) / (10.0 + STEP))
    step_grad = grad + decay * weight
    moment_new = momentum_rate * moment + step_grad
    weight_new = weight - rate * (step_grad + momentum_rate * moment_new)
    average_new = ema_keep * average + (1.0 - ema_keep) * weight_new
    return (weight_new, moment_new, average_new)


def block_keep(image_heights, blocks, base, total):
    lengths = image_heights[0]
    order = jnp.arange(lengths.shape[0])
    starts = jnp.sum(jnp.where(order[None, :] < order[:, None], lengths[None, :], 0), axis=1)
    place = base + jnp.arange(blocks + 1, dtype=jnp.int32)
    opening = jnp.logical_or(
        place == total, jnp.any(place[:, None] == starts[None, :], axis=1)
    )
    keep = jnp.where(opening, 0.0, 1.0).astype(f32)
    return jnp.broadcast_to(keep[:, None, None], (blocks + 1, 1, FPN_CH))


class Plan:
    def __init__(self, features, rows_count, lateral_rows, conv_rows):
        self.count = rows_count
        self.rows = [f.shape[0] for f in features]
        self.width = [f.shape[1] for f in features]
        self.depth = [f.shape[2] for f in features]
        self.unit = [16 >> k for k in range(LEVELS)]
        self.blocks = self.rows[0] // self.unit[0]
        self.lateral_rows = lateral_rows
        self.conv_rows = conv_rows
        self.bounds = [sum(self.depth[:k]) for k in range(LEVELS + 1)]


def put_shifted(target, value):
    wide = value.astype(f32)
    width = wide.shape[0]
    at = lax.broadcasted_iota(jnp.int32, wide.shape, 0)
    zero = jnp.zeros_like(wide)
    target[:, 0:FPN_CH] = jnp.where(at == 0, zero, pltpu.roll(wide, 1, 0)).astype(bf16)
    target[:, FPN_CH : 2 * FPN_CH] = value
    target[:, 2 * FPN_CH : 3 * FPN_CH] = jnp.where(
        at == width - 1, zero, pltpu.roll(wide, width - 1, 0)
    ).astype(bf16)


def masked(value, keep):
    return (value.astype(f32) * keep).astype(bf16)


def row_sum(value):
    wide = value.astype(f32)
    return jnp.sum(wide.reshape(wide.shape[0] // 8, 8, wide.shape[1]), axis=0)


def doubled(pairs, base, value):
    count = value.shape[0]
    sides = []
    for side in range(FPN_CH // HALF):
        part = value[:, side * HALF : (side + 1) * HALF]
        pairs[side, pl.ds(base, count, stride=2), :] = part
        pairs[side, pl.ds(base + 1, count, stride=2), :] = part
        sides.append(pairs[side, base : base + 2 * count, :])
    return jnp.concatenate(sides, axis=1)


def halved(pairs, base, value):
    count = value.shape[0] // 2
    sides = []
    for side in range(FPN_CH // HALF):
        pairs[side, base : base + 2 * count, :] = value[:, side * HALF : (side + 1) * HALF]
        sides.append(
            pairs[side, pl.ds(base, count, stride=2), :]
            + pairs[side, pl.ds(base + 1, count, stride=2), :]
        )
    return jnp.concatenate(sides, axis=1)


class Copies:
    def __init__(self, sends, locals_):
        self.sends = sends
        self.locals_ = locals_
        self.sent = []
        self.maybe = []
        self.begun = 0
        self.used = 0

    def remote(self, source, target, arrival, device, when=None):
        copy = pltpu.make_async_remote_copy(
            src_ref=source,
            dst_ref=target,
            send_sem=self.sends.at[self.begun],
            recv_sem=arrival,
            device_id=device,
            device_id_type=MESH,
        )
        self.begun += 1
        if when is None:
            copy.start()
            self.sent.append(copy)
        else:
            pl.when(when)(copy.start)
            self.maybe.append((when, copy))
        return copy

    def settle(self, copy):
        copy.wait_send()
        self.sent = [other for other in self.sent if other is not copy]

    def local(self, source, target):
        copy = pltpu.make_async_copy(source, target, self.locals_.at[self.used])
        self.used += 1
        copy.start()
        return copy

    def drain(self):
        for copy in self.sent:
            copy.wait_send()
        for when, copy in self.maybe:
            pl.when(when)(copy.wait_send)


def arrived(target, semaphore, device):
    pltpu.make_async_remote_copy(
        src_ref=target,
        dst_ref=target,
        send_sem=semaphore,
        recv_sem=semaphore,
        device_id=device,
        device_id_type=MESH,
    ).wait_recv()


class Place:
    def __init__(self, count):
        self.count = count
        self.spans = count // 2
        self.strip = lax.axis_index("rows")
        self.group = lax.axis_index("grp")
        self.a = self.strip // 2
        self.b = self.strip % 2
        self.y = self.group // 2
        self.c = self.group % 2
        self.core = (self.y * 2 + 1 - self.c, self.strip)
        self.across = ((1 - self.y) * 2 + self.c, self.strip)
        self.beside = (self.group, self.a * 2 + 1 - self.b)

    def other(self, spot):
        return spot + (spot - self.a + self.spans) // self.spans

    def strips(self):
        return [(self.group, lax.rem(self.strip + k, self.count)) for k in range(1, self.count)]


def enter(devices):
    barrier = pltpu.get_barrier_semaphore()
    for device in devices:
        pl.semaphore_signal(barrier, inc=1, device_id=device, device_id_type=MESH)
    pl.semaphore_wait(barrier, len(devices))


class Gather:
    def __init__(self, full, share, place, copies, arrivals):
        self.full = full
        self.share = share
        self.place = place
        self.copies = copies
        self.arrivals = arrivals

    def piece(self, owner, upper, lane):
        half = self.share // 2
        start = pl.multiple_of(owner * self.share + upper * half, 16 if half % 16 == 0 else 8)
        return self.full.at[pl.ds(start, half), pl.ds(pl.multiple_of(lane * HALF, HALF), HALF)]

    def send(self, owner, upper, lane, device):
        part = self.piece(owner, upper, lane)
        self.copies.remote(part, part, self.arrivals.at[owner, upper, lane], device)

    def take(self, owner, upper, lane, device):
        arrived(self.piece(owner, upper, lane), self.arrivals.at[owner, upper, lane], device)

    def from_core(self, spots):
        at = self.place
        for upper in (at.y, 1 - at.y):
            for owner in self.owners(spots):
                self.take(owner, upper, 1 - at.c, at.core)

    def owners(self, spots):
        at = self.place
        mine = [at.other(spot) * 2 + at.b for spot in spots if spot < at.spans - 1]
        return mine + [spot * 2 + 1 - at.b for spot in spots]


class AcrossLast(Gather):
    def start(self):
        at = self.place
        for spot in range(at.spans - 1):
            self.send(at.strip, at.y, at.c, (at.group, at.other(spot) * 2 + at.b))
        self.send(at.strip, at.y, at.c, at.beside)

    def from_span(self, spot):
        at = self.place
        span = at.other(spot)
        owner = span * 2 + at.b
        self.take(owner, at.y, at.c, (at.group, owner))
        for device in (at.across, at.beside, at.core):
            self.send(owner, at.y, at.c, device)

    def from_beside(self, spot):
        at = self.place
        owner = spot * 2 + 1 - at.b
        self.take(owner, at.y, at.c, at.beside)
        for device in (at.across, at.core):
            self.send(owner, at.y, at.c, device)

    def from_across(self, spots):
        at = self.place
        for owner in self.owners(spots):
            self.take(owner, 1 - at.y, at.c, at.across)
            self.send(owner, 1 - at.y, at.c, at.core)


class BesideLast(Gather):
    def start(self):
        at = self.place
        for spot in range(at.spans - 1):
            self.send(at.strip, at.y, at.c, (at.group, at.other(spot) * 2 + at.b))
        for upper in (at.y, 1 - at.y):
            self.send(at.strip, upper, at.c, at.beside)

    def from_span(self, spot):
        at = self.place
        span = at.other(spot)
        owner = span * 2 + at.b
        self.take(owner, at.y, at.c, (at.group, owner))
        for device in (at.across, at.beside, at.core):
            self.send(owner, at.y, at.c, device)

    def from_across(self, spot):
        at = self.place
        owner = at.other(spot) * 2 + at.b
        self.take(owner, 1 - at.y, at.c, at.across)
        for device in (at.beside, at.core):
            self.send(owner, 1 - at.y, at.c, device)

    def from_beside(self, upper):
        at = self.place
        for spot in range(at.spans):
            owner = spot * 2 + 1 - at.b
            self.take(owner, upper, at.c, at.beside)
            self.send(owner, upper, at.c, at.core)


class Scatter:
    def __init__(self, share, own, by_core, by_beside, by_across, by_span, total, place, copies, sems):
        self.share = share
        self.half = share // 2
        self.own = own
        self.by_core, self.by_beside, self.by_across, self.by_span = by_core, by_beside, by_across, by_span
        self.total = total
        self.place = place
        self.copies = copies
        self.core_sems, self.beside_sems, self.across_sems, self.span_sems, self.last_sems = sems

    def lanes(self, lane):
        return pl.ds(pl.multiple_of(lane * HALF, HALF), HALF)

    def rows_of(self, owner):
        return pl.ds(pl.multiple_of(owner * self.share, 16), self.share)

    def half_rows(self, base, upper):
        step = 16 if self.half % 16 == 0 else 8
        return pl.ds(pl.multiple_of(base + upper * self.half, step), self.half)

    def start(self, span):
        at = self.place
        for owner in (span * 2 + 1 - at.b, span * 2 + at.b):
            self.copies.remote(
                self.own.at[self.rows_of(owner), self.lanes(1 - at.c)],
                self.by_core.at[self.rows_of(owner)],
                self.core_sems.at[owner],
                at.core,
            )

    def to_beside(self, span):
        at = self.place
        owner = span * 2 + 1 - at.b
        rows = self.rows_of(owner)
        arrived(self.by_core.at[rows], self.core_sems.at[owner], at.core)
        value = self.own[rows, self.lanes(at.c)].astype(f32) + self.by_core[rows, :].astype(f32)
        self.by_core[rows, :] = value.astype(bf16)
        slot = pl.ds(span * self.share, self.share)
        self.copies.remote(
            self.by_core.at[rows], self.by_beside.at[slot], self.beside_sems.at[span], at.beside
        )

    def to_across(self, span):
        at = self.place
        owner = span * 2 + at.b
        rows = self.rows_of(owner)
        slot = pl.ds(span * self.share, self.share)
        arrived(self.by_core.at[rows], self.core_sems.at[owner], at.core)
        arrived(self.by_beside.at[slot], self.beside_sems.at[span], at.beside)
        value = (
            self.own[rows, self.lanes(at.c)].astype(f32)
            + self.by_core[rows, :].astype(f32)
            + self.by_beside[slot, :].astype(f32)
        )
        self.by_core[rows, :] = value.astype(bf16)
        self.copies.remote(
            self.by_core.at[self.half_rows(owner * self.share, 1 - at.y)],
            self.by_across.at[pl.ds(span * self.half, self.half)],
            self.across_sems.at[span],
            at.across,
        )

    def to_span(self, span):
        at = self.place
        owner = span * 2 + at.b
        slot = pl.ds(span * self.half, self.half)
        mine = self.half_rows(owner * self.share, at.y)
        arrived(self.by_across.at[slot], self.across_sems.at[span], at.across)
        value = self.by_core[mine, :].astype(f32) + self.by_across[slot, :].astype(f32)
        self.by_across[slot, :] = value.astype(bf16)
        self.copies.remote(
            self.by_across.at[slot],
            self.by_span.at[self.half_rows(at.a * self.half, 0)],
            self.span_sems.at[at.a],
            (at.group, owner),
            at.a != span,
        )

    def finish(self):
        at = self.place
        value = self.by_across[self.half_rows(at.a * self.half, 0), :].astype(f32)
        for spot in range(at.spans - 1):
            span = at.other(spot)
            slot = self.half_rows(span * self.half, 0)
            arrived(self.by_span.at[slot], self.span_sems.at[span], (at.group, span * 2 + at.b))
            value = value + self.by_span[slot, :].astype(f32)
        part = self.total.at[self.half_rows(0, at.y), self.lanes(at.c)]
        part[...] = value
        self.copies.remote(part, part, self.last_sems.at[at.y, at.c], at.across)
        self.copies.remote(part, part, self.last_sems.at[at.y, at.c], at.core)

    def join(self):
        at = self.place
        other = self.total.at[self.half_rows(0, 1 - at.y), self.lanes(at.c)]
        arrived(other, self.last_sems.at[1 - at.y, at.c], at.across)
        self.copies.remote(other, other, self.last_sems.at[1 - at.y, at.c], at.core)

    def close(self):
        at = self.place
        for upper in (at.y, 1 - at.y):
            part = self.total.at[self.half_rows(0, upper), self.lanes(1 - at.c)]
            arrived(part, self.last_sems.at[upper, 1 - at.c], at.core)


def scatter_shapes(share, count):
    v = pltpu.VMEM
    dma = pltpu.SemaphoreType.DMA
    spans = count // 2
    return [
        v((share * count, FPN_CH), bf16),
        v((share * count, HALF), bf16),
        v((share * spans, HALF), bf16),
        v((share // 2 * spans, HALF), bf16),
        v((share // 2 * spans, HALF), bf16),
        v((share, FPN_CH), f32),
        dma((count,)),
        dma((spans,)),
        dma((spans,)),
        dma((spans,)),
        dma((2, 2)),
    ]


def step_kernel(plan, own_lateral, *refs):
    refs = list(refs)

    def take(number):
        taken = refs[:number]
        del refs[:number]
        return taken

    features = take(4)
    grads = take(4)
    (coarse_grad, keep, lateral_in, conv_in, bias_in) = take(5)
    pyramid_out = take(4)
    (coarse_out,) = take(1)
    feature_out = take(4)
    (conv_total, lateral_total, bias_total) = take(3)
    c_v = take(4)
    g_v = take(4)
    (p6_v, p6_new) = take(2)
    wide = take(4)
    x_v = take(4)
    (t1, t2, t3) = take(3)
    (conv_v, lateral_v, bias_v, bias_low) = take(4)
    (acc, pairs, edge, bias_acc) = take(4)
    g_halo = take(4)
    x_halo = take(4)
    (send_sems, local_sems, conv_sems, lateral_sems, bias_sems, halo_sems) = take(6)
    conv_parts = take(11)
    if own_lateral:
        lateral_parts = take(11)
        lateral_grad = lateral_parts[0]
    else:
        (lateral_grad,) = take(1)
    sums = [None, t1, t2, t3]
    rows, width, depth, unit, blocks = plan.rows, plan.width, plan.depth, plan.unit, plan.blocks

    at = Place(plan.count)
    copies = Copies(send_sems, local_sems)
    conv_own = acc.at[pl.ds(0, plan.conv_rows)]
    lateral_own = acc.at[pl.ds(plan.conv_rows, plan.lateral_rows)]
    lateral_load = copies.local(lateral_in, lateral_own if own_lateral else lateral_v)
    conv_load = copies.local(conv_in, conv_own)
    grad_loads = [copies.local(grads[k], g_v[k]) for k in (3, 2, 1, 0)][::-1]
    coarse_load = copies.local(coarse_grad, p6_v)
    feature_loads = [copies.local(features[k], c_v[k]) for k in (3, 2, 1, 0)][::-1]
    strips = at.strips()
    enter(strips + [at.core, at.across])

    conv = AcrossLast(conv_v, plan.conv_rows, at, copies, conv_sems)
    lateral = BesideLast(lateral_v, plan.lateral_rows, at, copies, lateral_sems)
    lateral_load.wait()
    if own_lateral:
        start = pl.multiple_of(at.strip * plan.lateral_rows, 16)
        lateral_v[pl.ds(start, plan.lateral_rows), :] = lateral_own[...].astype(bf16)
        lateral.start()
    bias_v[at.strip] = bias_in[...]
    for device in strips:
        copies.remote(bias_in, bias_v.at[at.strip], bias_sems.at[at.strip], device)
    conv_load.wait()
    start = pl.multiple_of(at.strip * plan.conv_rows, 16)
    conv_v[pl.ds(start, plan.conv_rows), :] = conv_own[...].astype(bf16)
    conv.start()

    grad_loads[3].wait()
    coarse_load.wait()
    for r in range(rows[3] // 2):
        quarter = doubled(pairs, 0, 0.25 * p6_v[r].astype(f32))
        for s in range(2):
            whole = g_v[3][2 * r + s].astype(f32) + quarter
            g_v[3][2 * r + s] = whole.astype(bf16)

    above = (at.group, lax.rem(at.strip + at.count - 1, at.count))
    below = (at.group, lax.rem(at.strip + 1, at.count))

    def send_rims(first, last, halo, index):
        return [
            copies.remote(first, halo.at[1], halo_sems.at[index, 1], above),
            copies.remote(last, halo.at[0], halo_sems.at[index, 0], below),
        ]

    def take_rims(halo, index):
        arrived(halo.at[0], halo_sems.at[index, 0], above)
        arrived(halo.at[1], halo_sems.at[index, 1], below)

    rims = []
    for k in (3, 2, 1, 0):
        if k < 3:
            grad_loads[k].wait()
        rims += send_rims(g_v[k].at[0], g_v[k].at[rows[k] - 1], g_halo[k], k)

    bias_acc[...] = jnp.zeros_like(bias_acc)

    def slot_of(k, j):
        return j if k else 0

    def spread(k, j, first_time):
        tile = wide[k].at[slot_of(k, j)]

        def body(i, carry):
            value = g_v[k][j * unit[k] + i]
            put_shifted(tile.at[i + 1], value)
            if first_time:
                bias_acc[LEVELS + k] += row_sum(value)
            return carry

        lax.fori_loop(0, unit[k], body, 0)

    def spread_rims(k, j, saved):
        tile = wide[k].at[slot_of(k, j)]
        up = g_halo[k][0] if j == 0 else g_v[k][j * unit[k] - 1]
        put_shifted(tile.at[0], masked(up, keep[j]))
        if saved:
            down = edge[...]
        else:
            down = g_halo[k][1] if j == blocks - 1 else g_v[k][(j + 1) * unit[k]]
        put_shifted(tile.at[unit[k] + 1], masked(down, keep[j + 1]))

    spread(0, 0, True)
    for k in (3, 2, 1):
        for j in range(blocks):
            spread(k, j, True)
    if own_lateral:
        for spot in range(at.spans - 1):
            lateral.from_span(spot)
    for k in (3, 2, 1, 0):
        take_rims(g_halo[k], k)
        for j in range(blocks if k else 1):
            spread_rims(k, j, False)
    if own_lateral:
        for spot in range(at.spans - 1):
            lateral.from_across(spot)
        for upper in (at.y, 1 - at.y):
            lateral.from_beside(upper)
        lateral.from_core(range(at.spans))
    for k, device in enumerate(strips):
        owner = lax.rem(at.strip + k + 1, at.count)
        arrived(bias_v.at[owner], bias_sems.at[owner], device)
    per = plan.count // 8
    for j in range(8):
        total = bias_v[j * per]
        for other in range(1, per):
            total = total + bias_v[j * per + other]
        bias_low[j] = total

    def top_values(k, r, count):
        pixels = count * width[k]
        value = jnp.dot(
            c_v[k][pl.ds(r, count)].reshape(pixels, depth[k]),
            lateral_v[plan.bounds[k] : plan.bounds[k + 1], :],
            preferred_element_type=f32,
        )
        value = (value + bias_low[k][0:1, :]).reshape(count, width[k], FPN_CH)
        if k == 3:
            return [value[s] for s in range(count)]
        tops = []
        for s in range(count // 2):
            raised = doubled(pairs, s * width[k], sums[k + 1][r // 2 + s])
            tops += [value[2 * s] + raised, value[2 * s + 1] + raised]
        return tops

    def top_block(k, j, count):
        def body(i, carry):
            tops = top_values(k, j * unit[k] + i * count, count)
            for s in range(count):
                if k:
                    sums[k][j * unit[k] + i * count + s] = tops[s]
                x_v[k][j, i * count + s + 1] = tops[s].astype(bf16)
            return carry

        lax.fori_loop(0, unit[k] // count, body, 0)

    for k in (3, 2, 1, 0):
        feature_loads[k].wait()
        for j in range(blocks):
            top_block(k, j, min(4, unit[k]))
        send_rims(x_v[k].at[0, 1], x_v[k].at[blocks - 1, unit[k]], x_halo[k], LEVELS + k)
        for j in range(1, blocks):
            x_v[k][j - 1, unit[k] + 1] = masked(x_v[k][j, 1], keep[j])
            x_v[k][j, 0] = masked(x_v[k][j - 1, unit[k]], keep[j])
    for spot in range(at.spans - 1):
        conv.from_span(spot)
    conv.from_beside(0)

    conv_sum = Scatter(plan.conv_rows, *conv_parts[0:6], at, copies, conv_parts[6:11])
    conv_grad = conv_parts[0]
    if own_lateral:
        lateral_sum = Scatter(plan.lateral_rows, *lateral_parts[0:6], at, copies, lateral_parts[6:11])
    quarter = at.spans // LEVELS

    def spans_of(k):
        return range(k * quarter, (k + 1) * quarter)

    def for_level(step, k):
        for span in spans_of(k):
            step(span)

    def tap_dots(k, chunks):
        for dy in range(3):
            x = jnp.concatenate(
                [x_v[k][j, pl.ds(i + 1, n)].reshape(n * width[k], FPN_CH) for j, i, n in chunks],
                axis=0,
            )
            g = jnp.concatenate(
                [
                    wide[k][slot_of(k, j), pl.ds(i + dy, n)].reshape(n * width[k], 3 * FPN_CH)
                    for j, i, n in chunks
                ],
                axis=0,
            )
            dot = lax.dot_general(x, g, (((0,), (0,)), ((), ())), preferred_element_type=f32)
            for dx in range(3):
                yield 8 - (3 * dy + dx), dot[:, dx * FPN_CH : (dx + 1) * FPN_CH]

    def tap_grads(k):
        for tap, dot in tap_dots(k, [(j, 0, unit[k]) for j in range(blocks)]):
            start = k * TAPS + tap * FPN_CH
            conv_grad[start : start + FPN_CH, :] = dot.astype(bf16)

    def tap_block(k, j, count):
        def body(i, carry):
            for tap, dot in tap_dots(k, [(j, i * count, count)]):
                acc[tap * FPN_CH : (tap + 1) * FPN_CH, :] += dot
            return carry

        lax.fori_loop(0, unit[k] // count, body, 0)

    tap_grads(3)
    for_level(conv_sum.start, 3)
    tap_grads(2)
    for_level(conv_sum.start, 2)
    for_level(conv_sum.to_beside, 3)
    tap_grads(1)
    for_level(conv_sum.start, 1)
    for_level(conv_sum.to_beside, 2)
    for spot in range(1, at.spans):
        conv.from_beside(spot)
    acc[...] = jnp.zeros_like(acc)
    for j in range(blocks):
        if j:
            spread(0, j, True)
            spread_rims(0, j, False)
        tap_block(0, j, 8)
        if j == 0:
            for_level(conv_sum.to_beside, 1)
            conv.from_across(range(0, quarter))
            for_level(conv_sum.to_across, 3)
            for_level(conv_sum.to_across, 2)
    conv_grad[0:TAPS, :] = acc[...].astype(bf16)
    for_level(conv_sum.start, 0)
    conv.from_across(range(quarter, at.spans))
    for_level(conv_sum.to_across, 1)
    for_level(conv_sum.to_span, 3)
    conv.from_core(range(at.spans))

    def top_rows(k, j, i, count):
        pixels = count * width[k]
        value = None
        for dy in range(3):
            for dx in range(3):
                tap = 8 - (3 * dy + dx)
                start = k * TAPS + tap * FPN_CH
                dot = lax.dot_general(
                    wide[k][
                        slot_of(k, j), pl.ds(i + dy, count), :, dx * FPN_CH : (dx + 1) * FPN_CH
                    ].reshape(pixels, FPN_CH),
                    conv_v[start : start + FPN_CH, :],
                    (((1,), (1,)), ((), ())),
                    preferred_element_type=f32,
                )
                value = dot if value is None else value + dot
        value = value.reshape(count, width[k], FPN_CH)
        first = j * unit[k] + i
        if k:
            value = value + sums[k][pl.ds(first, count)]
        low = value.astype(bf16)
        g_v[k][pl.ds(first, count)] = low
        bias_acc[k] += row_sum(low.reshape(pixels, FPN_CH))
        if k < 3:
            for s in range(count // 2):
                sums[k + 1][first // 2 + s] = halved(
                    pairs, s * width[k], value[2 * s] + value[2 * s + 1]
                )

    def top_grads(k, j):
        count = min(4, unit[k])

        def body(i, carry):
            top_rows(k, j, i * count, count)
            return carry

        lax.fori_loop(0, unit[k] // count, body, 0)

    for copy in rims:
        copies.settle(copy)
    for j in reversed(range(blocks)):
        if j < blocks - 1:
            spread(0, j, False)
            spread_rims(0, j, True)
        if j:
            edge[...] = g_v[0][j * unit[0]]
        top_grads(0, j)
        if j == blocks - 1:
            for_level(conv_sum.to_beside, 0)
            for_level(conv_sum.to_span, 2)
    for_level(conv_sum.to_across, 0)
    for_level(conv_sum.to_span, 1)
    for k in range(1, LEVELS):
        for j in range(blocks):
            top_grads(k, j)

    count = min(8, rows[0])
    acc[0 : depth[0], :] = jnp.zeros((depth[0], FPN_CH), f32)

    def lateral_block(i, carry):
        acc[0 : depth[0], :] += lax.dot_general(
            c_v[0][pl.ds(i * count, count)].reshape(count * width[0], depth[0]),
            g_v[0][pl.ds(i * count, count)].reshape(count * width[0], FPN_CH),
            (((0,), (0,)), ((), ())),
            preferred_element_type=f32,
        )
        return carry

    lax.fori_loop(0, rows[0] // count, lateral_block, 0)
    lateral_grad[0 : depth[0], :] = acc[0 : depth[0], :].astype(bf16)
    for_level(conv_sum.to_span, 0)
    for k in range(1, LEVELS):
        value = lax.dot_general(
            c_v[k][...].reshape(rows[k] * width[k], depth[k]),
            g_v[k][...].reshape(rows[k] * width[k], FPN_CH),
            (((0,), (0,)), ((), ())),
            preferred_element_type=f32,
        )
        lateral_grad[plan.bounds[k] : plan.bounds[k + 1], :] = value.astype(bf16)
    spans = range(at.spans)
    if own_lateral:
        for span in spans:
            lateral_sum.start(span)
    across, core = plan.count, plan.count + 1
    bias_v[across + 4] = jnp.concatenate(
        [jnp.sum(bias_acc[j], axis=0, keepdims=True) for j in range(8)], axis=0
    )
    own_bias = bias_v.at[across + 4]
    for device in strips:
        copies.remote(
            own_bias,
            bias_grad_slot(bias_v, plan, at.strip),
            bias_sems.at[across + 2 + at.strip],
            device,
        )

    outs = []
    for k in range(LEVELS):
        count = max(1, min(rows[k], 1024 // width[k]))

        def feature_block(i, carry, k=k, count=count):
            value = lax.dot_general(
                g_v[k][pl.ds(i * count, count)].reshape(count * width[k], FPN_CH),
                lateral_v[plan.bounds[k] : plan.bounds[k + 1], :],
                (((1,), (1,)), ((), ())),
                preferred_element_type=f32,
            )
            c_v[k][pl.ds(i * count, count)] = value.astype(bf16).reshape(count, width[k], depth[k])
            return carry

        lax.fori_loop(0, rows[k] // count, feature_block, 0)
        outs.append(copies.local(c_v[k], feature_out[k]))
        if k == 0 and own_lateral:
            for span in spans:
                lateral_sum.to_beside(span)
    conv_sum.finish()

    for k in range(LEVELS):
        take_rims(x_halo[k], LEVELS + k)
        x_v[k][0, 0] = masked(x_halo[k][0], keep[0])
        x_v[k][blocks - 1, unit[k] + 1] = masked(x_halo[k][1], keep[blocks])

    def pyramid_block(k, j):
        tile = wide[k].at[slot_of(k, j)]

        def widen(i, carry):
            put_shifted(tile.at[i], x_v[k][j, i])
            return carry

        lax.fori_loop(0, unit[k] + 2, widen, 0)
        count = min(4, unit[k])
        pixels = count * width[k]

        def body(i, carry):
            value = jnp.dot(
                jnp.concatenate(
                    [
                        tile[pl.ds(i * count + dy, count)].reshape(pixels, 3 * FPN_CH)
                        for dy in range(3)
                    ],
                    axis=1,
                ),
                conv_v[k * TAPS : (k + 1) * TAPS, :],
                preferred_element_type=f32,
            )
            value = (value + bias_low[LEVELS + k][0:1, :]).reshape(count, width[k], FPN_CH)
            first = j * unit[k] + i * count
            g_v[k][pl.ds(first, count)] = value.astype(bf16)
            if k == 3:
                for s in range(count // 2):
                    mean = 0.25 * halved(pairs, 0, value[2 * s] + value[2 * s + 1])
                    p6_new[first // 2 + s] = mean.astype(bf16)
            return carry

        lax.fori_loop(0, unit[k] // count, body, 0)
        part = pl.ds(j * unit[k], unit[k])
        outs.append(copies.local(g_v[k].at[part], pyramid_out[k].at[part]))

    for j in range(blocks):
        pyramid_block(0, j)
        if j == 0 and own_lateral:
            for span in spans:
                lateral_sum.to_across(span)
        if j == blocks - 1 and own_lateral:
            for span in spans:
                lateral_sum.to_span(span)
    conv_sum.join()
    for k in range(1, LEVELS):
        for j in range(blocks):
            pyramid_block(k, j)
    outs.append(copies.local(p6_new, coarse_out))
    if own_lateral:
        lateral_sum.finish()
    total = own_bias[...]
    for k, device in enumerate(strips):
        owner = lax.rem(at.strip + k + 1, at.count)
        slot = bias_grad_slot(bias_v, plan, owner)
        arrived(slot, bias_sems.at[across + 2 + owner], device)
    bias_v[across + 5 + at.strip] = total
    total = bias_v[across + 5]
    for k in range(1, plan.count):
        total = total + bias_v[across + 5 + k]
    bias_v[across + 2] = total
    copies.remote(bias_v.at[across + 2], bias_v.at[across], bias_sems.at[across], at.across)
    if own_lateral:
        lateral_sum.join()
    arrived(bias_v.at[across], bias_sems.at[across], at.across)
    total = total + bias_v[across]
    bias_v[across + 3] = total
    copies.remote(bias_v.at[across + 3], bias_v.at[core], bias_sems.at[core], at.core)
    conv_sum.close()
    conv_total[...] = conv_sum.total[...]
    if own_lateral:
        lateral_sum.close()
        lateral_total[...] = lateral_sum.total[...]
    else:
        outs.append(copies.local(lateral_grad, lateral_total))
    arrived(bias_v.at[core], bias_sems.at[core], at.core)
    bias_total[...] = total + bias_v[core]
    for copy in outs:
        copy.wait()
    copies.drain()


def bias_grad_slot(bias_v, plan, owner):
    return bias_v.at[plan.count + 5 + owner]


def whole_step(plan, own_lateral, features, grads, coarse_grad, keep, lateral, conv, bias):
    rows, width, depth, unit, blocks = plan.rows, plan.width, plan.depth, plan.unit, plan.blocks
    shape = jax.ShapeDtypeStruct
    total = plan.bounds[LEVELS]
    coarse = (rows[3] // 2, width[3] // 2, FPN_CH)
    out_shape = (
        [shape((rows[k], width[k], FPN_CH), bf16) for k in range(LEVELS)]
        + [shape(coarse, bf16)]
        + [shape((rows[k], width[k], depth[k]), bf16) for k in range(LEVELS)]
        + [shape((plan.conv_rows, FPN_CH), f32)]
        + [shape((plan.lateral_rows, FPN_CH), f32) if own_lateral else shape((total, FPN_CH), bf16)]
        + [shape((8, FPN_CH), f32)]
    )
    v = pltpu.VMEM
    dma = pltpu.SemaphoreType.DMA
    scratch = (
        [v((rows[k], width[k], depth[k]), bf16) for k in range(LEVELS)]
        + [v((rows[k], width[k], FPN_CH), bf16) for k in range(LEVELS)]
        + [v(coarse, bf16), v(coarse, bf16)]
        + [v((blocks if k else 1, unit[k] + 2, width[k], 3 * FPN_CH), bf16) for k in range(LEVELS)]
        + [v((blocks, unit[k] + 2, width[k], FPN_CH), bf16) for k in range(LEVELS)]
        + [v((rows[k], width[k], FPN_CH), f32) for k in (1, 2, 3)]
        + [v((LEVELS * TAPS, FPN_CH), bf16), v((total, FPN_CH), bf16)]
        + [v((2 * plan.count + 5, 8, FPN_CH), f32), v((8, 8, FPN_CH), f32)]
        + [v((TAPS, FPN_CH), f32), v((FPN_CH // HALF, 2 * width[0], HALF), f32)]
        + [v((width[0], FPN_CH), bf16), v((8, 8, FPN_CH), f32)]
        + [v((2, width[k], FPN_CH), bf16) for k in range(LEVELS)] * 2
        + [dma((20 * plan.count + 64,)), dma((40,))]
        + [dma((plan.count, 2, 2)), dma((plan.count, 2, 2))]
        + [dma((2 * plan.count + 2,)), dma((2 * LEVELS, 2))]
        + scatter_shapes(plan.conv_rows, plan.count)
        + (
            scatter_shapes(plan.lateral_rows, plan.count)
            if own_lateral
            else [v((total, FPN_CH), bf16)]
        )
    )
    return pl.pallas_call(
        functools.partial(step_kernel, plan, own_lateral),
        out_shape=out_shape,
        in_specs=[ANY] * 9 + [VMEM, ANY, ANY, VMEM],
        out_specs=[ANY] * 9 + [VMEM, VMEM if own_lateral else ANY, VMEM],
        scratch_shapes=scratch,
        name="step",
        cost_estimate=pl.CostEstimate(
            flops=45 << 30, bytes_accessed=60 << 20, transcendentals=0
        ),
        compiler_params=pltpu.CompilerParams(
            collective_id=0, has_side_effects=True, vmem_limit_bytes=ROOM
        ),
    )(*features, *grads, coarse_grad, keep, lateral, conv, bias)


def shards(
    feature_c2,
    feature_c3,
    feature_c4,
    feature_c5,
    cotangent_p2,
    cotangent_p3,
    cotangent_p4,
    cotangent_p5,
    cotangent_p6,
    image_heights,
    lateral_weight,
    conv_weight,
    bias_all,
    lateral_momentum,
    conv_momentum,
    bias_momentum,
    lateral_ema,
    conv_ema,
    bias_ema,
):
    features = (feature_c2, feature_c3, feature_c4, feature_c5)
    grads = (cotangent_p2, cotangent_p3, cotangent_p4, cotangent_p5)
    count = lax.axis_size("rows")
    strip = lax.axis_index("rows")
    plan = Plan(features, count, lateral_weight.shape[0], conv_weight.shape[0])
    own_lateral = plan.lateral_rows % 16 == 0
    keep = block_keep(image_heights, plan.blocks, strip * plan.blocks, plan.blocks * count)
    share = bias_all.shape[0]
    place = lax.rem(strip * share, FPN_CH)
    bias_low = bias_all.astype(bf16).astype(f32)
    bias_row = jnp.tile(bias_low, FPN_CH // share)
    lane = jnp.arange(FPN_CH)
    inside = jnp.logical_and(lane >= place, lane < place + share)
    bias_row = jnp.broadcast_to(jnp.where(inside, bias_row, 0.0)[None, :], (8, FPN_CH))
    if own_lateral:
        lateral_in = lateral_weight
    else:
        lateral_in = lax.all_gather(lateral_weight.astype(bf16), "rows", axis=0, tiled=True)
    results = whole_step(
        plan, own_lateral, features, grads, cotangent_p6, keep, lateral_in, conv_weight, bias_row
    )
    sum_conv, sum_lateral = results[9:11]
    sum_bias = results[11].reshape(-1)
    if not own_lateral:
        sum_lateral = lax.psum(
            lax.psum_scatter(sum_lateral, "rows", scatter_dimension=0, tiled=True), "grp"
        ).astype(f32)
    sum_bias = lax.dynamic_slice_in_dim(sum_bias, strip * share, share)
    lateral_new, lateral_moment, lateral_avg = nesterov(
        lateral_weight, sum_lateral, lateral_momentum, lateral_ema, lateral_rate, decay_rate
    )
    conv_new, conv_moment, conv_avg = nesterov(
        conv_weight, sum_conv, conv_momentum, conv_ema, conv_rate, decay_rate
    )
    bias_new, bias_moment, bias_avg = nesterov(
        bias_all, sum_bias, bias_momentum, bias_ema, bias_rate, 0.0
    )
    return (
        *results[:9],
        lateral_new,
        conv_new,
        bias_new,
        lateral_moment,
        conv_moment,
        bias_moment,
        lateral_avg,
        conv_avg,
        bias_avg,
    )


def solution(mesh):
    cut = P(("grp", "rows"), None, None)
    wide = P("rows", None)
    in_specs = (cut,) * 9 + (P("grp", None),) + (wide, wide, P("rows")) * 3
    out_specs = (cut,) * 9 + (wide, wide, P("rows")) * 3
    return jax.shard_map(
        shards,
        mesh=mesh,
        in_specs=in_specs,
        out_specs=out_specs,
        check_vma=False,
    )
```

```python
import functools

import jax
import jax.numpy as jnp
from jax import lax
from jax.experimental import pallas as pl
from jax.experimental.pallas import tpu as pltpu
from jax.sharding import PartitionSpec as P

FPN_CH = 256
C2_CH = 256
C3_CH = 512
C4_CH = 1024
C5_CH = 2048
STEP = 10
LEVELS = 4
TAPS = 9 * FPN_CH
HALF = FPN_CH // 2

momentum_rate = 0.9
decay_rate = 0.0001
lateral_rate = 1.2e-05
conv_rate = 8e-06
bias_rate = 0.00013

MESH = pl.DeviceIdType.MESH
ANY = pl.BlockSpec(memory_space=pl.ANY)
VMEM = pl.BlockSpec(memory_space=pltpu.VMEM)
HBM = pl.BlockSpec(memory_space=pltpu.HBM)
f32 = jnp.float32
bf16 = jnp.bfloat16
ROOM = 49 << 20
WHOLE_ROOM = 63 << 20


def nesterov(weight, grad, moment, average, rate, decay):
    ema_keep = min(0.999, (1.0 + STEP) / (10.0 + STEP))
    step_grad = grad + decay * weight
    moment_new = momentum_rate * moment + step_grad
    weight_new = weight - rate * (step_grad + momentum_rate * moment_new)
    average_new = ema_keep * average + (1.0 - ema_keep) * weight_new
    return (weight_new, moment_new, average_new)


def block_keep(image_heights, blocks, strip, count):
    starts = [0]
    for image in range(image_heights.shape[1] - 1):
        starts.append(starts[-1] + image_heights[0, image])
    keep = []
    for border in range(blocks + 1):
        place = strip * blocks + border
        opening = place == blocks * count
        for start in starts:
            opening = jnp.logical_or(opening, place == start)
        keep.append(jnp.where(opening, 0.0, 1.0).astype(f32))
    return keep


class Plan:
    def __init__(self, features, rows_count, lateral_rows, conv_rows):
        self.count = rows_count
        self.rows = [f.shape[0] for f in features]
        self.width = [f.shape[1] for f in features]
        self.depth = [f.shape[2] for f in features]
        self.unit = [16 >> k for k in range(LEVELS)]
        self.blocks = self.rows[0] // self.unit[0]
        self.lateral_rows = lateral_rows
        self.conv_rows = conv_rows
        self.bounds = [sum(self.depth[:k]) for k in range(LEVELS + 1)]


def put_shifted(target, value):
    wide = value.astype(f32)
    width = wide.shape[0]
    at = lax.broadcasted_iota(jnp.int32, wide.shape, 0)
    zero = jnp.zeros_like(wide)
    target[:, 0:FPN_CH] = jnp.where(at == 0, zero, pltpu.roll(wide, 1, 0)).astype(bf16)
    target[:, FPN_CH : 2 * FPN_CH] = value
    target[:, 2 * FPN_CH : 3 * FPN_CH] = jnp.where(
        at == width - 1, zero, pltpu.roll(wide, width - 1, 0)
    ).astype(bf16)


def masked(value, keep):
    return (value.astype(f32) * keep).astype(bf16)


def row_sum(value):
    wide = value.astype(f32)
    return jnp.sum(wide.reshape(wide.shape[0] // 8, 8, wide.shape[1]), axis=0)


def doubled(pairs, base, value):
    count = value.shape[0]
    sides = []
    for side in range(FPN_CH // HALF):
        part = value[:, side * HALF : (side + 1) * HALF]
        pairs[side, pl.ds(base, count, stride=2), :] = part
        pairs[side, pl.ds(base + 1, count, stride=2), :] = part
        sides.append(pairs[side, base : base + 2 * count, :])
    return jnp.concatenate(sides, axis=1)


def halved(pairs, base, value):
    count = value.shape[0] // 2
    sides = []
    for side in range(FPN_CH // HALF):
        pairs[side, base : base + 2 * count, :] = value[:, side * HALF : (side + 1) * HALF]
        sides.append(
            pairs[side, pl.ds(base, count, stride=2), :]
            + pairs[side, pl.ds(base + 1, count, stride=2), :]
        )
    return jnp.concatenate(sides, axis=1)


class Copies:
    def __init__(self, sends, locals_, ruler):
        self.sends = sends
        self.locals_ = locals_
        self.ruler = ruler
        self.kinds = {}
        self.used = 0

    def remote(self, source, target, arrival, device, kind, when=None, counts=True):
        size = source.dtype.itemsize
        for length in source.shape:
            size *= length
        most = self.ruler.shape[0] * HALF * self.ruler.dtype.itemsize
        while kind in self.kinds and self.kinds[kind][1] + size > most:
            kind = (kind, "more")
        if kind not in self.kinds:
            self.kinds[kind] = [len(self.kinds), 0]
        kept = self.kinds[kind]
        copy = pltpu.make_async_remote_copy(
            src_ref=source,
            dst_ref=target,
            send_sem=self.sends.at[kept[0]],
            recv_sem=arrival,
            device_id=device,
            device_id_type=MESH,
        )
        if counts:
            kept[1] += size
        if when is None:
            copy.start()
        else:
            pl.when(when)(copy.start)

    def settle(self, kind, device, when=None):
        place, size = self.kinds.pop(kind)
        self.kinds[kind, "settled"] = [place, 0]
        wide = size % (16 * FPN_CH) == 0
        lanes = FPN_CH if wide else HALF
        rows = self.ruler.at[pl.ds(0, size // (2 * lanes)), pl.ds(0, lanes)]
        copy = pltpu.make_async_remote_copy(
            src_ref=rows,
            dst_ref=rows,
            send_sem=self.sends.at[place],
            recv_sem=self.sends.at[place],
            device_id=device,
            device_id_type=MESH,
        )
        if when is None:
            copy.wait_send()
        else:
            pl.when(when)(copy.wait_send)

    def local(self, source, target):
        copy = pltpu.make_async_copy(source, target, self.locals_.at[self.used])
        self.used += 1
        copy.start()
        return copy


def arrived(target, semaphore, device):
    pltpu.make_async_remote_copy(
        src_ref=target,
        dst_ref=target,
        send_sem=semaphore,
        recv_sem=semaphore,
        device_id=device,
        device_id_type=MESH,
    ).wait_recv()


class Place:
    def __init__(self, count):
        self.count = count
        self.spans = count // 2
        self.strip = lax.axis_index("rows")
        self.group = lax.axis_index("grp")
        self.a = self.strip // 2
        self.b = self.strip % 2
        self.y = self.group // 2
        self.c = self.group % 2
        self.core = (self.y * 2 + 1 - self.c, self.strip)
        self.across = ((1 - self.y) * 2 + self.c, self.strip)
        self.beside = (self.group, self.a * 2 + 1 - self.b)

    def other(self, spot):
        return spot + (spot - self.a + self.spans) // self.spans

    def strips(self):
        return [(self.group, lax.rem(self.strip + k, self.count)) for k in range(1, self.count)]


def knock(devices):
    for device in devices:
        pl.semaphore_signal(
            pltpu.get_barrier_semaphore(), inc=1, device_id=device, device_id_type=MESH
        )


def answer(devices):
    pl.semaphore_wait(pltpu.get_barrier_semaphore(), len(devices))


class Gather:
    def __init__(self, kind, full, share, place, copies, arrivals, core_arrivals):
        self.kind = kind
        self.full = full
        self.share = share
        self.core_arrivals = core_arrivals
        self.place = place
        self.copies = copies
        self.arrivals = arrivals

    def piece(self, owner, upper, lane):
        half = self.share // 2
        start = pl.multiple_of(owner * self.share + upper * half, 16 if half % 16 == 0 else 8)
        return self.full.at[pl.ds(start, half), pl.ds(pl.multiple_of(lane * HALF, HALF), HALF)]

    def send(self, owner, upper, lane, device):
        part = self.piece(owner, upper, lane)
        arrival = self.core_arrivals if device is self.place.core else self.arrivals.at[owner, upper]
        self.copies.remote(part, part, arrival, device, self.kind)

    def take(self, owner, upper, lane, device):
        arrived(self.piece(owner, upper, lane), self.arrivals.at[owner, upper], device)

    def along(self):
        at = self.place
        for spot in range(at.spans - 1):
            self.send(at.strip, at.y, at.c, (at.group, at.other(spot) * 2 + at.b))

    def aside(self):
        at = self.place
        self.send(at.strip, at.y, at.c, at.beside)

    def from_span(self, spot):
        at = self.place
        owner = at.other(spot) * 2 + at.b
        self.take(owner, at.y, at.c, (at.group, owner))
        for device in (at.across, at.beside, at.core):
            self.send(owner, at.y, at.c, device)

    def mine(self, spot):
        return self.place.other(spot) * 2 + self.place.b

    def facing(self, spot):
        at = self.place
        return (at.a if spot is None else at.other(spot)) * 2 + 1 - at.b

    def from_beside(self, spot):
        at = self.place
        owner = self.facing(spot)
        self.take(owner, at.y, at.c, at.beside)
        for device in (at.across, at.core):
            self.send(owner, at.y, at.c, device)

    def from_across(self, spot):
        at = self.place
        for owner in [self.facing(spot)] if spot is None else [self.mine(spot), self.facing(spot)]:
            self.take(owner, 1 - at.y, at.c, at.across)
            self.send(owner, 1 - at.y, at.c, at.core)

    def from_core(self):
        at = self.place
        rows = (at.count - 1) * self.share // 2
        arrived(self.full.at[pl.ds(0, rows)], self.core_arrivals, at.core)


class Scatter:
    def __init__(self, kind, share, aside, own, by_core, by_across, by_beside, by_span, total, place, copies, sems):
        self.kind = kind
        self.share = share
        self.half = share // 2
        self.aside = aside
        self.apart = share if aside else share // 2
        self.own = own
        self.by_core, self.by_across, self.by_beside, self.by_span = by_core, by_across, by_beside, by_span
        self.total = total
        self.place = place
        self.copies = copies
        self.core_sems, self.across_sems, self.beside_sems, self.span_sems, self.last_sems = sems

    def lanes(self, lane):
        return pl.ds(pl.multiple_of(lane * HALF, HALF), HALF)

    def rows_of(self, owner):
        return pl.ds(pl.multiple_of(owner * self.share, 16), self.share)

    def half_rows(self, base, upper):
        step = 16 if self.half % 16 == 0 else 8
        return pl.ds(pl.multiple_of(base + upper * self.half, step), self.half)

    def start(self, span):
        at = self.place
        for owner in (span * 2 + 1 - at.b, span * 2 + at.b):
            self.copies.remote(
                self.own.at[self.rows_of(owner), self.lanes(1 - at.c)],
                self.by_core.at[self.rows_of(owner)],
                self.core_sems.at[owner],
                at.core,
                (self.kind, "core"),
            )

    def to_across_first(self, span):
        at = self.place
        for owner in (span * 2 + 1 - at.b, span * 2 + at.b):
            rows = self.rows_of(owner)
            arrived(self.by_core.at[rows], self.core_sems.at[owner], at.core)
            value = self.own[rows, self.lanes(at.c)].astype(f32) + self.by_core[rows, :].astype(f32)
            self.by_core[rows, :] = value.astype(bf16)
            self.copies.remote(
                self.by_core.at[self.half_rows(owner * self.share, 1 - at.y)],
                self.by_across.at[self.half_rows(owner * self.half, 0)],
                self.across_sems.at[owner],
                at.across,
                self.kind,
            )

    def both_sides(self, owner):
        at = self.place
        mine = self.half_rows(owner * self.share, at.y)
        slot = self.half_rows(owner * self.half, 0)
        arrived(self.by_across.at[slot], self.across_sems.at[owner], at.across)
        return mine, self.by_core[mine, :].astype(f32) + self.by_across[slot, :].astype(f32)

    def to_beside_second(self, span):
        at = self.place
        mine, value = self.both_sides(span * 2 + 1 - at.b)
        self.by_core[mine, :] = value.astype(bf16)
        self.copies.remote(
            self.by_core.at[mine],
            self.by_beside.at[pl.ds(span * self.apart, self.half)],
            self.beside_sems.at[span],
            at.beside,
            self.kind,
        )

    def to_beside_first(self, span):
        at = self.place
        owner = span * 2 + 1 - at.b
        rows = self.rows_of(owner)
        arrived(self.by_core.at[rows], self.core_sems.at[owner], at.core)
        value = self.own[rows, self.lanes(at.c)].astype(f32) + self.by_core[rows, :].astype(f32)
        self.by_core[rows, :] = value.astype(bf16)
        slot = pl.ds(span * self.share, self.share)
        self.copies.remote(
            self.by_core.at[rows],
            self.by_beside.at[slot],
            self.beside_sems.at[span],
            at.beside,
            self.kind,
        )

    def to_across_second(self, span):
        at = self.place
        owner = span * 2 + at.b
        rows = self.rows_of(owner)
        slot = pl.ds(span * self.share, self.share)
        arrived(self.by_core.at[rows], self.core_sems.at[owner], at.core)
        arrived(self.by_beside.at[slot], self.beside_sems.at[span], at.beside)
        value = (
            self.own[rows, self.lanes(at.c)].astype(f32)
            + self.by_core[rows, :].astype(f32)
            + self.by_beside[slot, :].astype(f32)
        )
        self.by_core[rows, :] = value.astype(bf16)
        self.copies.remote(
            self.by_core.at[self.half_rows(owner * self.share, 1 - at.y)],
            self.by_across.at[self.half_rows(owner * self.half, 0)],
            self.across_sems.at[owner],
            at.across,
            self.kind,
        )

    def first(self, span):
        self.to_beside_first(span) if span in self.aside else self.to_across_first(span)

    def second(self, span):
        self.to_across_second(span) if span in self.aside else self.to_beside_second(span)

    def to_span(self, span):
        at = self.place
        owner = span * 2 + at.b
        mine, value = self.both_sides(owner)
        if span not in self.aside:
            slot = pl.ds(span * self.apart, self.half)
            arrived(self.by_beside.at[slot], self.beside_sems.at[span], at.beside)
            value = value + self.by_beside[slot, :].astype(f32)
        self.by_core[mine, :] = value.astype(bf16)
        self.copies.remote(
            self.by_core.at[mine],
            self.by_span.at[self.half_rows(at.a * self.half, 0)],
            self.span_sems.at[at.a],
            (at.group, owner),
            self.kind,
            at.a != span,
            span > 0,
        )

    def finish(self):
        at = self.place
        value = self.by_core[self.half_rows(at.strip * self.share, at.y), :].astype(f32)
        for spot in range(at.spans - 1):
            span = at.other(spot)
            slot = self.half_rows(span * self.half, 0)
            arrived(self.by_span.at[slot], self.span_sems.at[span], (at.group, span * 2 + at.b))
            value = value + self.by_span[slot, :].astype(f32)
        part = self.total.at[self.half_rows(0, at.y), self.lanes(at.c)]
        part[...] = value.astype(bf16)
        self.copies.remote(part, part, self.last_sems.at[at.y, at.c], at.across, self.kind)
        self.copies.remote(part, part, self.last_sems.at[at.y, at.c], at.core, self.kind)

    def join(self):
        at = self.place
        other = self.total.at[self.half_rows(0, 1 - at.y), self.lanes(at.c)]
        arrived(other, self.last_sems.at[1 - at.y, at.c], at.across)
        self.copies.remote(other, other, self.last_sems.at[1 - at.y, at.c], at.core, self.kind)

    def close(self):
        at = self.place
        for upper in (at.y, 1 - at.y):
            part = self.total.at[self.half_rows(0, upper), self.lanes(1 - at.c)]
            arrived(part, self.last_sems.at[upper, 1 - at.c], at.core)


def scatter_shapes(share, count, mixed):
    v = pltpu.VMEM
    dma = pltpu.SemaphoreType.DMA
    spans = count // 2
    return [
        v((share * count, FPN_CH), bf16),
        v((share * count, HALF), bf16),
        v((share // 2 * count, HALF), bf16),
        v((spans * share // (1 if mixed else 2), HALF), bf16),
        v((share // 2 * spans, HALF), bf16),
        dma((count,)),
        dma((count,)),
        dma((spans,)),
        dma((spans,)),
        dma((2, 2)),
    ]


def step_kernel(plan, own_lateral, pinned, *refs):
    refs = list(refs)

    def take(number):
        taken = refs[:number]
        del refs[:number]
        return taken

    features = take(4)
    grads = take(4)
    (coarse_grad, image_heights, lateral_in, conv_in, bias_in) = take(5)
    held = take(9)
    (conv_total, lateral_total, bias_total) = take(3)
    if pinned:
        g_v, p6_new, c_v = held[:4], held[4], held[5:]
    else:
        g_v, p6_new, c_v = take(4), take(1)[0], take(4)
    (p6_v,) = take(1)
    wide = take(4)
    x_v = take(4)
    (t1, t2, t3) = take(3)
    (conv_v, lateral_v, bias_v, bias_low) = take(4)
    (acc, pairs, edge, bias_acc) = take(4)
    g_halo = take(4)
    x_halo = take(4)
    (send_sems, local_sems, core_sems, conv_sems, lateral_sems, bias_sems, halo_sems) = take(7)
    conv_parts = take(10)
    if own_lateral:
        lateral_parts = take(10)
        lateral_grad = lateral_parts[0]
    else:
        (lateral_grad,) = take(1)
    sums = [None, t1, t2, t3]
    rows, width, depth, unit, blocks = plan.rows, plan.width, plan.depth, plan.unit, plan.blocks

    at = Place(plan.count)
    keep = block_keep(image_heights, blocks, at.strip, plan.count)
    copies = Copies(send_sems, local_sems, conv_v)
    conv_own = acc.at[pl.ds(0, plan.conv_rows)]
    lateral_own = acc.at[pl.ds(plan.conv_rows, plan.lateral_rows)]
    lateral_load = copies.local(lateral_in, lateral_own if own_lateral else lateral_v)
    strips = at.strips()
    partners = strips + [at.core, at.across]
    knock(partners)

    conv = Gather("taps", conv_v, plan.conv_rows, at, copies, conv_sems, core_sems.at[0])
    lateral = Gather(
        "laterals", lateral_v, plan.lateral_rows, at, copies, lateral_sems, core_sems.at[1]
    )
    lateral_load.wait()
    if own_lateral:
        start = pl.multiple_of(at.strip * plan.lateral_rows, 16)
        lateral_v[pl.ds(start, plan.lateral_rows), :] = lateral_own[...].astype(bf16)
    conv_load = copies.local(conv_in, conv_own)
    grad_loads = [copies.local(grads[k], g_v[k]) for k in (3, 2, 1, 0)][::-1]
    coarse_load = copies.local(coarse_grad, p6_v)
    answer(partners)
    if own_lateral:
        lateral.along()
        lateral.aside()
    conv_load.wait()
    start = pl.multiple_of(at.strip * plan.conv_rows, 16)
    conv_v[pl.ds(start, plan.conv_rows), :] = conv_own[...].astype(bf16)
    bias_v[at.strip] = jnp.broadcast_to(bias_in[...].astype(bf16).astype(f32), (8, FPN_CH))
    for device in strips:
        copies.remote(
            bias_v.at[at.strip], bias_v.at[at.strip], bias_sems.at[at.strip], device, "bias"
        )

    grad_loads[3].wait()
    coarse_load.wait()
    for r in range(rows[3] // 2):
        quarter = doubled(pairs, 0, 0.25 * p6_v[r].astype(f32))
        for s in range(2):
            whole = g_v[3][2 * r + s].astype(f32) + quarter
            g_v[3][2 * r + s] = whole.astype(bf16)
    bias_acc[...] = jnp.zeros_like(bias_acc)

    def slot_of(k, j):
        return j if k else 0

    def spread(k, j, first_time):
        tile = wide[k].at[slot_of(k, j)]

        def body(i, carry):
            value = g_v[k][j * unit[k] + i]
            put_shifted(tile.at[i + 1], value)
            if first_time:
                bias_acc[LEVELS + k] += row_sum(value)
            return carry

        lax.fori_loop(0, unit[k], body, 0)

    def spread_rims(k, j, saved):
        tile = wide[k].at[slot_of(k, j)]
        up = g_halo[k][0] if j == 0 else g_v[k][j * unit[k] - 1]
        put_shifted(tile.at[0], masked(up, keep[j]))
        if saved:
            down = edge[...]
        else:
            down = g_halo[k][1] if j == blocks - 1 else g_v[k][(j + 1) * unit[k]]
        put_shifted(tile.at[unit[k] + 1], masked(down, keep[j + 1]))

    near_row = [(1 - at.b) * (rows[k] - 1) for k in range(LEVELS)]
    far_row = [at.b * (rows[k] - 1) for k in range(LEVELS)]
    far = (at.group, at.strip - 1 + 2 * at.b)
    has_far = (at.strip - 1 + 2 * at.b + 1) % (at.count + 1) > 0

    def send_near(row, halo, index):
        kind = ("near", index // LEVELS)
        copies.remote(row, halo.at[at.b], halo_sems.at[index, at.b], at.beside, kind)

    def send_far(row, halo, index):
        kind = ("far", index // LEVELS)
        copies.remote(row, halo.at[1 - at.b], halo_sems.at[index, 1 - at.b], far, kind, has_far)

    def take_rims(halo, index):
        arrived(halo.at[1 - at.b], halo_sems.at[index, 1 - at.b], at.beside)
        pl.when(has_far)(lambda: arrived(halo.at[at.b], halo_sems.at[index, at.b], far))

        def clear():
            halo[at.b] = jnp.zeros(halo.shape[1:], bf16)

        pl.when(jnp.logical_not(has_far))(clear)

    places = [None, *range(at.spans - 1)]
    for k in (2, 1, 0):
        grad_loads[k].wait()
    for k in (3, 2, 1, 0):
        send_far(g_v[k].at[far_row[k]], g_halo[k], k)
    conv.along()
    feature_loads = [copies.local(features[k], c_v[k]) for k in (3, 2, 1, 0)][::-1]
    def spread_level(k):
        def body(r, carry):
            value = g_v[k][r]
            put_shifted(wide[k].at[r // unit[k], lax.rem(r, unit[k]) + 1], value)
            bias_acc[LEVELS + k] += row_sum(value)
            return carry

        lax.fori_loop(0, rows[k], body, 0)

    for k in (3, 2, 1):
        spread_level(k)
    spread(0, 0, True)
    if own_lateral:
        for spot in range(at.spans - 1):
            lateral.from_span(spot)
    for k in (3, 2, 1, 0):
        send_near(g_v[k].at[near_row[k]], g_halo[k], k)
    conv.aside()
    if own_lateral:
        for spot in places:
            lateral.from_beside(spot)
        for spot in places:
            lateral.from_across(spot)
        lateral.from_core()
    for k, device in enumerate(strips):
        owner = lax.rem(at.strip + k + 1, at.count)
        arrived(bias_v.at[owner], bias_sems.at[owner], device)
    per = plan.count // 8
    for j in range(8):
        total = bias_v[j * per]
        for other in range(1, per):
            total = total + bias_v[j * per + other]
        bias_low[j] = total

    def top_values(k, r, count):
        pixels = count * width[k]
        value = jnp.dot(
            c_v[k][pl.ds(r, count)].reshape(pixels, depth[k]),
            lateral_v[plan.bounds[k] : plan.bounds[k + 1], :],
            preferred_element_type=f32,
        )
        value = (value + bias_low[k][0:1, :]).reshape(count, width[k], FPN_CH)
        if k == 3:
            return [value[s] for s in range(count)]
        tops = []
        for s in range(count // 2):
            raised = doubled(pairs, s * width[k], sums[k + 1][r // 2 + s])
            tops += [value[2 * s] + raised, value[2 * s + 1] + raised]
        return tops

    def top_level(k):
        count = min(4, unit[k])
        steps = unit[k] // count

        def body(t, carry):
            tops = top_values(k, t * count, count)
            for s in range(count):
                if k:
                    sums[k][t * count + s] = tops[s]
                x_v[k][t // steps, lax.rem(t, steps) * count + s + 1] = tops[s].astype(bf16)
            return carry

        lax.fori_loop(0, rows[k] // count, body, 0)

    for k in (3, 2, 1, 0):
        feature_loads[k].wait()
        top_level(k)
        for j in range(1, blocks):
            x_v[k][j - 1, unit[k] + 1] = masked(x_v[k][j, 1], keep[j])
            x_v[k][j, 0] = masked(x_v[k][j - 1, unit[k]], keep[j])
        if k == 1:
            conv.from_span(0)
    for k in (3, 2, 1, 0):
        take_rims(g_halo[k], k)
        for j in range(blocks if k else 1):
            spread_rims(k, j, False)

    conv_sum = Scatter(
        "tap sums", plan.conv_rows, (), *conv_parts[0:5], conv_total, at, copies, conv_parts[5:10]
    )
    conv_grad = conv_parts[0]
    if own_lateral:
        lateral_sum = Scatter(
            "lateral sums",
            plan.lateral_rows,
            range(at.spans // 2),
            *lateral_parts[0:5],
            lateral_total,
            at,
            copies,
            lateral_parts[5:10],
        )
    quarter = at.spans // LEVELS

    def spans_of(k):
        return range(k * quarter, (k + 1) * quarter)

    def each(step, items):
        for item in items:
            step(item)

    def for_level(step, k):
        for span in spans_of(k):
            step(span)

    def tap_dots(k, chunks):
        for dy in range(3):
            x = jnp.concatenate(
                [x_v[k][j, pl.ds(i + 1, n)].reshape(n * width[k], FPN_CH) for j, i, n in chunks],
                axis=0,
            )
            g = jnp.concatenate(
                [
                    wide[k][slot_of(k, j), pl.ds(i + dy, n)].reshape(n * width[k], 3 * FPN_CH)
                    for j, i, n in chunks
                ],
                axis=0,
            )
            dot = lax.dot_general(x, g, (((0,), (0,)), ((), ())), preferred_element_type=f32)
            for dx in range(3):
                yield 8 - (3 * dy + dx), dot[:, dx * FPN_CH : (dx + 1) * FPN_CH]

    def tap_grads(k):
        for tap, dot in tap_dots(k, [(j, 0, unit[k]) for j in range(blocks)]):
            start = k * TAPS + tap * FPN_CH
            conv_grad[start : start + FPN_CH, :] = dot.astype(bf16)

    def tap_rows(k, j, first, count):
        for tap, dot in tap_dots(k, [(j, first, count)]):
            acc[tap * FPN_CH : (tap + 1) * FPN_CH, :] += dot

    def x_rims():
        for k in (3, 2, 1, 0):
            send_far(x_v[k].at[at.b * (blocks - 1), 1 + at.b * (unit[k] - 1)], x_halo[k], LEVELS + k)
            send_near(
                x_v[k].at[(1 - at.b) * (blocks - 1), 1 + (1 - at.b) * (unit[k] - 1)],
                x_halo[k],
                LEVELS + k,
            )

    tap_grads(3)
    for_level(conv_sum.start, 3)
    tap_grads(2)
    for_level(conv_sum.start, 2)
    for spot in range(1, at.spans - 1):
        conv.from_span(spot)
    tap_grads(1)
    for_level(conv_sum.start, 1)
    conv.from_beside(None)
    acc[...] = jnp.zeros_like(acc)
    def pass_on(spots):
        return lambda: each(conv.from_beside, [spot for spot in spots if spot < at.spans - 1])

    between = [
        pass_on([0]),
        lambda: each(lambda run: run(), [pass_on([1]), x_rims]),
        lambda: each(
            lambda run: run(),
            [pass_on(range(2, at.spans)), lambda: for_level(conv_sum.first, 3)],
        ),
        lambda: each(lambda k: for_level(conv_sum.first, k), (2, 1)),
    ]
    step = unit[0] // 2

    def tap_half(t, carry):
        j, half = t // 2, lax.rem(t, 2)
        for later in range(1, blocks):

            def renew(later=later):
                spread(0, later, True)
                spread_rims(0, later, False)

            pl.when(t == 2 * later)(renew)
        tap_rows(0, j, half * step, step)
        for place, run in enumerate(between):
            pl.when(t == place)(run)
        return carry

    lax.fori_loop(0, 2 * blocks, tap_half, 0)
    conv_grad[0:TAPS, :] = acc[...].astype(bf16)
    for_level(conv_sum.start, 0)
    for spot in places:
        conv.from_across(spot)
    conv.from_core()

    def top_rows(k, j, i, count):
        pixels = count * width[k]
        value = None
        for dy in range(3):
            for dx in range(3):
                tap = 8 - (3 * dy + dx)
                start = k * TAPS + tap * FPN_CH
                dot = lax.dot_general(
                    wide[k][
                        slot_of(k, j), pl.ds(i + dy, count), :, dx * FPN_CH : (dx + 1) * FPN_CH
                    ].reshape(pixels, FPN_CH),
                    conv_v[start : start + FPN_CH, :],
                    (((1,), (1,)), ((), ())),
                    preferred_element_type=f32,
                )
                value = dot if value is None else value + dot
        value = value.reshape(count, width[k], FPN_CH)
        first = j * unit[k] + i
        if k:
            value = value + sums[k][pl.ds(first, count)]
        low = value.astype(bf16)
        g_v[k][pl.ds(first, count)] = low
        bias_acc[k] += row_sum(low.reshape(pixels, FPN_CH))
        if k < 3:
            for s in range(count // 2):
                sums[k + 1][first // 2 + s] = halved(
                    pairs, s * width[k], value[2 * s] + value[2 * s + 1]
                )

    def top_level_grads(k):
        count = min(4, unit[k])
        steps = unit[k] // count

        def body(t, carry):
            top_rows(k, t // steps, lax.rem(t, steps) * count, count)
            return carry

        lax.fori_loop(0, rows[k] // count, body, 0)

    copies.settle(("near", 0), at.beside)
    copies.settle(("far", 0), far, has_far)
    steps = unit[0] // 4

    def top_four(t, carry):
        for turn in range(blocks):
            j = blocks - 1 - turn

            def renew(j=j):
                if j < blocks - 1:
                    spread(0, j, False)
                    spread_rims(0, j, True)
                if j:
                    edge[...] = g_v[0][j * unit[0]]

            pl.when(t == turn * steps)(renew)
        top_rows(0, blocks - 1 - t // steps, lax.rem(t, steps) * 4, 4)

        pl.when(t == steps - 1)(lambda: for_level(conv_sum.first, 0))
        pl.when(t == steps)(lambda: for_level(conv_sum.second, 3))
        pl.when(t == blocks * steps - 2)(lambda: for_level(conv_sum.second, 2))
        return carry

    lax.fori_loop(0, blocks * steps, top_four, 0)
    for_level(conv_sum.to_span, 3)
    for k in range(1, LEVELS):
        top_level_grads(k)
        if k == 1:
            for_level(conv_sum.second, 1)
            for_level(conv_sum.to_span, 2)

    for k in (3, 2, 1):
        value = lax.dot_general(
            c_v[k][...].reshape(rows[k] * width[k], depth[k]),
            g_v[k][...].reshape(rows[k] * width[k], FPN_CH),
            (((0,), (0,)), ((), ())),
            preferred_element_type=f32,
        )
        lateral_grad[plan.bounds[k] : plan.bounds[k + 1], :] = value.astype(bf16)
    for_level(conv_sum.second, 0)
    for_level(conv_sum.to_span, 1)
    across, core = plan.count, plan.count + 1
    own_bias = jnp.concatenate(
        [jnp.sum(bias_acc[j], axis=0, keepdims=True) for j in range(8)], axis=0
    )
    bias_v[across + 4] = own_bias
    for device in strips:
        copies.remote(
            bias_v.at[across + 4],
            bias_grad_slot(bias_v, plan, at.strip),
            bias_sems.at[across + 2 + at.strip],
            device,
            "bias",
        )
    bias_v[across + 5 + at.strip] = own_bias
    count = min(8, rows[0])
    acc[0 : depth[0], :] = jnp.zeros((depth[0], FPN_CH), f32)

    def lateral_block(i, carry):
        acc[0 : depth[0], :] += lax.dot_general(
            c_v[0][pl.ds(i * count, count)].reshape(count * width[0], depth[0]),
            g_v[0][pl.ds(i * count, count)].reshape(count * width[0], FPN_CH),
            (((0,), (0,)), ((), ())),
            preferred_element_type=f32,
        )
        return carry

    spans = range(at.spans)
    late = [span for span in spans if span * 2 * plan.lateral_rows < depth[0]]
    if own_lateral:
        for span in spans:
            if span not in late:
                lateral_sum.start(span)
    lax.fori_loop(0, rows[0] // count, lateral_block, 0)
    lateral_grad[0 : depth[0], :] = acc[0 : depth[0], :].astype(bf16)
    if own_lateral:
        for span in late:
            lateral_sum.start(span)
        for span in spans:
            if span not in late:
                lateral_sum.first(span)

    outs = []
    for k in range(LEVELS):
        count = max(1, min(rows[k], 1024 // width[k]))

        def feature_block(i, carry, k=k, count=count):
            value = lax.dot_general(
                g_v[k][pl.ds(i * count, count)].reshape(count * width[k], FPN_CH),
                lateral_v[plan.bounds[k] : plan.bounds[k + 1], :],
                (((1,), (1,)), ((), ())),
                preferred_element_type=f32,
            )
            c_v[k][pl.ds(i * count, count)] = value.astype(bf16).reshape(count, width[k], depth[k])
            return carry

        lax.fori_loop(0, rows[k] // count, feature_block, 0)
        if k == 0:
            if own_lateral:
                for span in late:
                    lateral_sum.first(span)
            for_level(conv_sum.to_span, 0)

    for k in range(LEVELS):
        take_rims(x_halo[k], LEVELS + k)
        x_v[k][0, 0] = masked(x_halo[k][0], keep[0])
        x_v[k][blocks - 1, unit[k] + 1] = masked(x_halo[k][1], keep[blocks])

    def widen(k, j):
        tile = wide[k].at[slot_of(k, j)]

        def body(i, carry):
            put_shifted(tile.at[i], x_v[k][j, i])
            return carry

        lax.fori_loop(0, unit[k] + 2, body, 0)

    def pyramid_rows(k, j, i, count):
        pixels = count * width[k]
        value = jnp.dot(
            jnp.concatenate(
                [
                    wide[k][slot_of(k, j), pl.ds(i + dy, count)].reshape(pixels, 3 * FPN_CH)
                    for dy in range(3)
                ],
                axis=1,
            ),
            conv_v[k * TAPS : (k + 1) * TAPS, :],
            preferred_element_type=f32,
        )
        value = (value + bias_low[LEVELS + k][0:1, :]).reshape(count, width[k], FPN_CH)
        first = j * unit[k] + i
        g_v[k][pl.ds(first, count)] = value.astype(bf16)
        if k == 3:
            for s in range(count // 2):
                mean = 0.25 * halved(pairs, 0, value[2 * s] + value[2 * s + 1])
                p6_new[first // 2 + s] = mean.astype(bf16)

    def pyramid_block(k):
        count = min(4, unit[k])
        steps = unit[k] // count

        def widen_block(j, carry):
            widen(k, j)
            return carry

        def body(t, carry):
            pyramid_rows(k, t // steps, lax.rem(t, steps) * count, count)
            return carry

        lax.fori_loop(0, blocks, widen_block, 0)
        lax.fori_loop(0, rows[k] // count, body, 0)

    def end_close():
        conv_sum.close()

    def end_bias():
        arrived(bias_v.at[core], bias_sems.at[core], at.core)
        own = pl.ds(at.strip // per, 1)
        bias_total[...] = bias_v[across + 3, own, :] + bias_v[core, own, :]

    def end_drain():
        if not pinned:
            for source, target in zip([*g_v, p6_new, *c_v], held):
                outs.append(copies.local(source, target))
        for copy in outs:
            copy.wait()
        copies.settle(("far", 1), far, has_far)
        for kind in [kind for kind, (place, size) in copies.kinds.items() if size]:
            copies.settle(kind, at.core)

    pyramid_block(1)
    if own_lateral:
        for span in spans:
            lateral_sum.second(span)
    for k, device in enumerate(strips):
        owner = lax.rem(at.strip + k + 1, at.count)
        arrived(bias_grad_slot(bias_v, plan, owner), bias_sems.at[across + 2 + owner], device)
    total = bias_v[across + 5]
    for k in range(1, plan.count):
        total = total + bias_v[across + 5 + k]
    bias_v[across + 2] = total
    copies.remote(
        bias_v.at[across + 2], bias_v.at[across], bias_sems.at[across], at.across, "bias"
    )
    for k in range(2, LEVELS):
        pyramid_block(k)
    def end_first():
        conv_sum.finish()
        if own_lateral:
            for span in spans:
                lateral_sum.to_span(span)

    def end_second():
        conv_sum.join()
        arrived(bias_v.at[across], bias_sems.at[across], at.across)
        total = bias_v[across + 2] + bias_v[across]
        bias_v[across + 3] = total
        copies.remote(
            bias_v.at[across + 3], bias_v.at[core], bias_sems.at[core], at.core, "bias"
        )

    def end_third():
        if own_lateral:
            lateral_sum.finish()

    def pyramid_four(t, carry):
        j, i = t // steps, lax.rem(t, steps)
        pl.when(i == 0)(lambda: widen(0, j))
        pyramid_rows(0, j, i * 4, 4)
        pl.when(t == 1)(end_first)
        pl.when(t == (blocks - 1) * steps)(end_second)
        pl.when(t == (blocks - 1) * steps + 1)(end_third)
        return carry

    lax.fori_loop(0, blocks * steps, pyramid_four, 0)
    end_close()
    end_bias()
    if own_lateral:
        lateral_sum.join()
        lateral_sum.close()
    else:
        outs.append(copies.local(lateral_grad, lateral_total))
    end_drain()


def bias_grad_slot(bias_v, plan, owner):
    return bias_v.at[plan.count + 5 + owner]


def whole_step(plan, own_lateral, features, grads, coarse_grad, image_heights, lateral, conv, bias):
    rows, width, depth, unit, blocks = plan.rows, plan.width, plan.depth, plan.unit, plan.blocks
    shape = jax.ShapeDtypeStruct
    v = pltpu.VMEM
    total = plan.bounds[LEVELS]
    coarse = (rows[3] // 2, width[3] // 2, FPN_CH)
    pinned = own_lateral
    shapes = [(rows[k], width[k], FPN_CH) for k in range(LEVELS)] + [coarse]
    shapes += [(rows[k], width[k], depth[k]) for k in range(LEVELS)]
    out_shape = (
        [(v if pinned else shape)(s, bf16) for s in shapes]
        + [(v if pinned else shape)((plan.conv_rows, FPN_CH), bf16)]
        + [v((plan.lateral_rows, FPN_CH), bf16) if pinned else shape((total, FPN_CH), bf16)]
        + [shape((1, FPN_CH), f32)]
    )
    dma = pltpu.SemaphoreType.DMA
    scratch = (
        ([] if pinned else [v(s, bf16) for s in shapes])
        + [v(coarse, bf16)]
        + [v((blocks if k else 1, unit[k] + 2, width[k], 3 * FPN_CH), bf16) for k in range(LEVELS)]
        + [v((blocks, unit[k] + 2, width[k], FPN_CH), bf16) for k in range(LEVELS)]
        + [v((rows[k], width[k], FPN_CH), f32) for k in (1, 2, 3)]
        + [v((LEVELS * TAPS, FPN_CH), bf16), v((total, FPN_CH), bf16)]
        + [v((2 * plan.count + 5, 8, FPN_CH), f32), v((8, 8, FPN_CH), f32)]
        + [v((TAPS, FPN_CH), f32), v((FPN_CH // HALF, 2 * width[0], HALF), f32)]
        + [v((width[0], FPN_CH), bf16), v((8, 8, FPN_CH), f32)]
        + [v((2, width[k], FPN_CH), bf16) for k in range(LEVELS)] * 2
        + [dma((16 + plan.count // 2,)), dma((24,)), dma((2,))]
        + [dma((plan.count, 2)), dma((plan.count, 2))]
        + [dma((2 * plan.count + 2,)), dma((2 * LEVELS, 2))]
        + scatter_shapes(plan.conv_rows, plan.count, False)
        + (
            scatter_shapes(plan.lateral_rows, plan.count, True)
            if own_lateral
            else [v((total, FPN_CH), bf16)]
        )
    )
    return pl.pallas_call(
        functools.partial(step_kernel, plan, own_lateral, pinned),
        out_shape=out_shape,
        in_specs=[ANY] * 9 + [pl.BlockSpec(memory_space=pltpu.SMEM), ANY, ANY, VMEM],
        out_specs=[VMEM if pinned else ANY] * 9 + [VMEM, VMEM if own_lateral else ANY, VMEM],
        scratch_shapes=scratch,
        name="step",
        cost_estimate=pl.CostEstimate(
            flops=45 << 30, bytes_accessed=60 << 20, transcendentals=0
        ),
        compiler_params=pltpu.CompilerParams(
            collective_id=0, has_side_effects=True, vmem_limit_bytes=ROOM if pinned else WHOLE_ROOM
        ),
    )(*features, *grads, coarse_grad, image_heights, lateral, conv, bias)


def update_kernel(count, *refs):
    refs = list(refs)

    def take(number):
        taken = refs[:number]
        del refs[:number]
        return taken

    held = take(count)
    sums = take(3)
    given = [take(3), take(3), take(3)]
    held_out = take(count)
    results = [take(3), take(3), take(3)]
    work = [take(3), take(3)]
    (sems,) = take(1)
    used = [0]

    def begin(source, target):
        copy = pltpu.make_async_copy(source, target, sems.at[used[0]])
        used[0] += 1
        copy.start()
        return copy

    loads = [[begin(given[i][j], work[i][j]) for j in range(3)] for i in range(2)]
    outs = [begin(source, target) for source, target in zip(held, held_out)]
    rates = ((conv_rate, decay_rate), (lateral_rate, decay_rate), (bias_rate, 0.0))
    for i in range(2):
        for load in loads[i]:
            load.wait()
        rows = work[i][0].shape[0]
        step = next(size for size in (96, 48, 16, rows) if rows % size == 0)

        def update(r, carry, i=i, step=step):
            part = pl.ds(r * step, step)
            weight, moment, average = (work[i][j][part, :] for j in range(3))
            total = sums[i][part, :].astype(f32)
            new = nesterov(weight, total, moment, average, *rates[i])
            for j in range(3):
                work[i][j][part, :] = new[j]
            return carry

        lax.fori_loop(0, rows // step, update, 0)
        outs += [begin(work[i][j], results[i][j]) for j in range(3)]
    weight, moment, average = (given[2][j][...] for j in range(3))
    new = nesterov(weight, sums[2][...], moment, average, *rates[2])
    for j in range(3):
        results[2][j][...] = new[j]
    for copy in outs:
        copy.wait()


def update(held, sums, given):
    shape = jax.ShapeDtypeStruct
    place = pltpu.with_memory_space_constraint
    kept = [place(x, pltpu.VMEM) for x in held]
    far = [place(x, pltpu.HBM) for g in given[:2] for x in g]
    results = [shape(g[0].shape, f32) for g in given for _ in range(3)]
    return pl.pallas_call(
        functools.partial(update_kernel, len(held)),
        out_shape=[shape(x.shape, x.dtype) for x in held] + results,
        in_specs=[ANY] * len(held) + [VMEM] * 3 + [HBM] * 6 + [VMEM] * 3,
        out_specs=[HBM] * (len(held) + 6) + [VMEM] * 3,
        scratch_shapes=[pltpu.VMEM(g[0].shape, f32) for g in given[:2] for _ in range(3)]
        + [pltpu.SemaphoreType.DMA((len(held) + 12,))],
        name="update",
        cost_estimate=pl.CostEstimate(flops=8 << 20, bytes_accessed=25 << 20, transcendentals=0),
        compiler_params=pltpu.CompilerParams(vmem_limit_bytes=24 << 20),
    )(*kept, *sums, *far, *given[2])


def shards(
    feature_c2,
    feature_c3,
    feature_c4,
    feature_c5,
    cotangent_p2,
    cotangent_p3,
    cotangent_p4,
    cotangent_p5,
    cotangent_p6,
    image_heights,
    lateral_weight,
    conv_weight,
    bias_all,
    lateral_momentum,
    conv_momentum,
    bias_momentum,
    lateral_ema,
    conv_ema,
    bias_ema,
):
    features = (feature_c2, feature_c3, feature_c4, feature_c5)
    grads = (cotangent_p2, cotangent_p3, cotangent_p4, cotangent_p5)
    count = lax.axis_size("rows")
    strip = lax.axis_index("rows")
    plan = Plan(features, count, lateral_weight.shape[0], conv_weight.shape[0])
    own_lateral = plan.lateral_rows % 16 == 0
    share = bias_all.shape[0]
    if share == FPN_CH:
        bias_row = bias_all.reshape(1, FPN_CH)
    else:
        place = lax.rem(strip * share, FPN_CH)
        lane = jnp.arange(FPN_CH)
        inside = jnp.logical_and(lane >= place, lane < place + share)
        bias_row = jnp.where(inside, jnp.tile(bias_all, FPN_CH // share), 0.0)[None, :]
    if own_lateral:
        lateral_in = lateral_weight
    else:
        lateral_in = lax.all_gather(lateral_weight.astype(bf16), "rows", axis=0, tiled=True)
    results = whole_step(
        plan,
        own_lateral,
        features,
        grads,
        cotangent_p6,
        image_heights,
        lateral_in,
        conv_weight,
        bias_row,
    )
    sum_conv, sum_lateral, sum_bias = results[9:]
    if not own_lateral:
        sum_lateral = lax.psum(
            lax.psum_scatter(sum_lateral, "rows", scatter_dimension=0, tiled=True), "grp"
        ).astype(f32)
    row = (1, share)
    if share < FPN_CH:
        sum_bias = lax.dynamic_slice_in_dim(sum_bias, place, share, axis=1)
    held = results[:9] if own_lateral else []
    new = update(
        held,
        (sum_conv, sum_lateral, sum_bias),
        (
            (conv_weight, conv_momentum, conv_ema),
            (lateral_weight, lateral_momentum, lateral_ema),
            (bias_all.reshape(row), bias_momentum.reshape(row), bias_ema.reshape(row)),
        ),
    )
    held = new[: len(held)] or results[:9]
    first = len(new) - 9
    conv_new, lateral_new, bias_new = (new[first + i : first + i + 3] for i in (0, 3, 6))
    return (
        *held,
        lateral_new[0],
        conv_new[0],
        bias_new[0].reshape(share),
        lateral_new[1],
        conv_new[1],
        bias_new[1].reshape(share),
        lateral_new[2],
        conv_new[2],
        bias_new[2].reshape(share),
    )


def solution(mesh):
    cut = P(("grp", "rows"), None, None)
    wide = P("rows", None)
    in_specs = (cut,) * 9 + (P("grp", None),) + (wide, wide, P("rows")) * 3
    out_specs = (cut,) * 9 + (wide, wide, P("rows")) * 3
    return jax.shard_map(
        shards,
        mesh=mesh,
        in_specs=in_specs,
        out_specs=out_specs,
        check_vma=False,
    )
```

```python
import functools

import jax
import jax.numpy as jnp
from jax import lax
from jax.experimental import pallas as pl
from jax.experimental.pallas import tpu as pltpu
from jax.sharding import PartitionSpec as P

FPN_CH = 256
C2_CH = 256
C3_CH = 512
C4_CH = 1024
C5_CH = 2048
STEP = 10
LEVELS = 4
TAPS = 9 * FPN_CH
HALF = FPN_CH // 2

momentum_rate = 0.9
decay_rate = 0.0001
lateral_rate = 1.2e-05
conv_rate = 8e-06
bias_rate = 0.00013

MESH = pl.DeviceIdType.MESH
ANY = pl.BlockSpec(memory_space=pl.ANY)
VMEM = pl.BlockSpec(memory_space=pltpu.VMEM)
HBM = pl.BlockSpec(memory_space=pltpu.HBM)
f32 = jnp.float32
bf16 = jnp.bfloat16
ROOM = 49 << 20
WHOLE_ROOM = 63 << 20


def nesterov(weight, grad, moment, average, rate, decay):
    ema_keep = min(0.999, (1.0 + STEP) / (10.0 + STEP))
    step_grad = grad + decay * weight
    moment_new = momentum_rate * moment + step_grad
    weight_new = weight - rate * (step_grad + momentum_rate * moment_new)
    average_new = ema_keep * average + (1.0 - ema_keep) * weight_new
    return (weight_new, moment_new, average_new)


def block_keep(image_heights, blocks, strip, count):
    starts = [0]
    for image in range(image_heights.shape[1] - 1):
        starts.append(starts[-1] + image_heights[0, image])
    keep = []
    for border in range(blocks + 1):
        place = strip * blocks + border
        opening = place == blocks * count
        for start in starts:
            opening = jnp.logical_or(opening, place == start)
        keep.append(jnp.where(opening, 0.0, 1.0).astype(f32))
    return keep


class Plan:
    def __init__(self, features, rows_count, lateral_rows, conv_rows):
        self.count = rows_count
        self.rows = [f.shape[0] for f in features]
        self.width = [f.shape[1] for f in features]
        self.depth = [f.shape[2] for f in features]
        self.unit = [16 >> k for k in range(LEVELS)]
        self.blocks = self.rows[0] // self.unit[0]
        self.lateral_rows = lateral_rows
        self.conv_rows = conv_rows
        self.bounds = [sum(self.depth[:k]) for k in range(LEVELS + 1)]


def put_shifted(target, value):
    wide = value.astype(f32)
    width = wide.shape[0]
    at = lax.broadcasted_iota(jnp.int32, wide.shape, 0)
    zero = jnp.zeros_like(wide)
    target[:, 0:FPN_CH] = jnp.where(at == 0, zero, pltpu.roll(wide, 1, 0)).astype(bf16)
    target[:, FPN_CH : 2 * FPN_CH] = value
    target[:, 2 * FPN_CH : 3 * FPN_CH] = jnp.where(
        at == width - 1, zero, pltpu.roll(wide, width - 1, 0)
    ).astype(bf16)


def masked(value, keep):
    return (value.astype(f32) * keep).astype(bf16)


def row_sum(value):
    wide = value.astype(f32)
    return jnp.sum(wide.reshape(wide.shape[0] // 8, 8, wide.shape[1]), axis=0)


def doubled(pairs, base, value):
    count = value.shape[0]
    sides = []
    for side in range(FPN_CH // HALF):
        part = value[:, side * HALF : (side + 1) * HALF]
        pairs[side, pl.ds(base, count, stride=2), :] = part
        pairs[side, pl.ds(base + 1, count, stride=2), :] = part
        sides.append(pairs[side, base : base + 2 * count, :])
    return jnp.concatenate(sides, axis=1)


def halved(pairs, base, value):
    count = value.shape[0] // 2
    sides = []
    for side in range(FPN_CH // HALF):
        pairs[side, base : base + 2 * count, :] = value[:, side * HALF : (side + 1) * HALF]
        sides.append(
            pairs[side, pl.ds(base, count, stride=2), :]
            + pairs[side, pl.ds(base + 1, count, stride=2), :]
        )
    return jnp.concatenate(sides, axis=1)


class Copies:
    def __init__(self, sends, locals_, ruler):
        self.sends = sends
        self.locals_ = locals_
        self.ruler = ruler
        self.kinds = {}
        self.used = 0

    def remote(self, source, target, arrival, device, kind, when=None, counts=True):
        size = source.dtype.itemsize
        for length in source.shape:
            size *= length
        most = self.ruler.shape[0] * HALF * self.ruler.dtype.itemsize
        while kind in self.kinds and self.kinds[kind][1] + size > most:
            kind = (kind, "more")
        if kind not in self.kinds:
            self.kinds[kind] = [len(self.kinds), 0]
        kept = self.kinds[kind]
        copy = pltpu.make_async_remote_copy(
            src_ref=source,
            dst_ref=target,
            send_sem=self.sends.at[kept[0]],
            recv_sem=arrival,
            device_id=device,
            device_id_type=MESH,
        )
        if counts:
            kept[1] += size
        if when is None:
            copy.start()
        else:
            pl.when(when)(copy.start)

    def settle(self, kind, device, when=None):
        place, size = self.kinds.pop(kind)
        self.kinds[kind, "settled"] = [place, 0]
        wide = size % (16 * FPN_CH) == 0
        lanes = FPN_CH if wide else HALF
        rows = self.ruler.at[pl.ds(0, size // (2 * lanes)), pl.ds(0, lanes)]
        copy = pltpu.make_async_remote_copy(
            src_ref=rows,
            dst_ref=rows,
            send_sem=self.sends.at[place],
            recv_sem=self.sends.at[place],
            device_id=device,
            device_id_type=MESH,
        )
        if when is None:
            copy.wait_send()
        else:
            pl.when(when)(copy.wait_send)

    def local(self, source, target):
        copy = pltpu.make_async_copy(source, target, self.locals_.at[self.used])
        self.used += 1
        copy.start()
        return copy


def arrived(target, semaphore, device):
    pltpu.make_async_remote_copy(
        src_ref=target,
        dst_ref=target,
        send_sem=semaphore,
        recv_sem=semaphore,
        device_id=device,
        device_id_type=MESH,
    ).wait_recv()


class Place:
    def __init__(self, count):
        self.count = count
        self.spans = count // 2
        self.strip = lax.axis_index("rows")
        self.group = lax.axis_index("grp")
        self.a = self.strip // 2
        self.b = self.strip % 2
        self.y = self.group // 2
        self.c = self.group % 2
        self.core = (self.y * 2 + 1 - self.c, self.strip)
        self.across = ((1 - self.y) * 2 + self.c, self.strip)
        self.beside = (self.group, self.a * 2 + 1 - self.b)

    def other(self, spot):
        return spot + (spot - self.a + self.spans) // self.spans

    def strips(self):
        return [(self.group, lax.rem(self.strip + k, self.count)) for k in range(1, self.count)]


def knock(devices):
    for device in devices:
        pl.semaphore_signal(
            pltpu.get_barrier_semaphore(), inc=1, device_id=device, device_id_type=MESH
        )


def answer(devices):
    pl.semaphore_wait(pltpu.get_barrier_semaphore(), len(devices))


class Gather:
    def __init__(self, kind, full, share, place, copies, arrivals, core_arrivals):
        self.kind = kind
        self.full = full
        self.share = share
        self.core_arrivals = core_arrivals
        self.place = place
        self.copies = copies
        self.arrivals = arrivals

    def piece(self, owner, upper, lane):
        half = self.share // 2
        start = pl.multiple_of(owner * self.share + upper * half, 16 if half % 16 == 0 else 8)
        return self.full.at[pl.ds(start, half), pl.ds(pl.multiple_of(lane * HALF, HALF), HALF)]

    def send(self, owner, upper, lane, device):
        part = self.piece(owner, upper, lane)
        arrival = self.core_arrivals if device is self.place.core else self.arrivals.at[owner, upper]
        self.copies.remote(part, part, arrival, device, self.kind)

    def take(self, owner, upper, lane, device):
        arrived(self.piece(owner, upper, lane), self.arrivals.at[owner, upper], device)

    def along(self):
        at = self.place
        for spot in range(at.spans - 1):
            self.send(at.strip, at.y, at.c, (at.group, at.other(spot) * 2 + at.b))

    def aside(self):
        at = self.place
        self.send(at.strip, at.y, at.c, at.beside)

    def from_span(self, spot):
        at = self.place
        owner = at.other(spot) * 2 + at.b
        self.take(owner, at.y, at.c, (at.group, owner))
        for device in (at.across, at.beside, at.core):
            self.send(owner, at.y, at.c, device)

    def mine(self, spot):
        return self.place.other(spot) * 2 + self.place.b

    def facing(self, spot):
        at = self.place
        return (at.a if spot is None else at.other(spot)) * 2 + 1 - at.b

    def from_beside(self, spot, whole=False):
        at = self.place
        owner = self.facing(spot)
        for upper in (at.y, 1 - at.y)[: 2 if whole else 1]:
            self.take(owner, upper, at.c, at.beside)
            self.send(owner, upper, at.c, at.core)
        if not whole:
            self.send(owner, at.y, at.c, at.across)

    def across_first(self, spot):
        at = self.place
        owner = self.mine(spot)
        self.take(owner, 1 - at.y, at.c, at.across)
        for device in (at.beside, at.core):
            self.send(owner, 1 - at.y, at.c, device)

    def from_across(self, spot):
        at = self.place
        for owner in [self.facing(spot)] if spot is None else [self.mine(spot), self.facing(spot)]:
            self.take(owner, 1 - at.y, at.c, at.across)
            self.send(owner, 1 - at.y, at.c, at.core)

    def from_core(self):
        at = self.place
        rows = (at.count - 1) * self.share // 2
        arrived(self.full.at[pl.ds(0, rows)], self.core_arrivals, at.core)


class Scatter:
    def __init__(self, kind, share, aside, own, by_core, by_across, by_beside, by_span, total, place, copies, sems):
        self.kind = kind
        self.share = share
        self.half = share // 2
        self.aside = aside
        self.apart = share if aside else share // 2
        self.own = own
        self.by_core, self.by_across, self.by_beside, self.by_span = by_core, by_across, by_beside, by_span
        self.total = total
        self.place = place
        self.copies = copies
        self.core_sems, self.across_sems, self.beside_sems, self.span_sems, self.last_sems = sems

    def lanes(self, lane):
        return pl.ds(pl.multiple_of(lane * HALF, HALF), HALF)

    def rows_of(self, owner):
        return pl.ds(pl.multiple_of(owner * self.share, 16), self.share)

    def half_rows(self, base, upper):
        step = 16 if self.half % 16 == 0 else 8
        return pl.ds(pl.multiple_of(base + upper * self.half, step), self.half)

    def start(self, span):
        at = self.place
        for owner in (span * 2 + 1 - at.b, span * 2 + at.b):
            self.copies.remote(
                self.own.at[self.rows_of(owner), self.lanes(1 - at.c)],
                self.by_core.at[self.rows_of(owner)],
                self.core_sems.at[owner],
                at.core,
                (self.kind, "core"),
            )

    def to_across_first(self, span):
        at = self.place
        for owner in (span * 2 + 1 - at.b, span * 2 + at.b):
            rows = self.rows_of(owner)
            arrived(self.by_core.at[rows], self.core_sems.at[owner], at.core)
            value = self.own[rows, self.lanes(at.c)].astype(f32) + self.by_core[rows, :].astype(f32)
            self.by_core[rows, :] = value.astype(bf16)
            self.copies.remote(
                self.by_core.at[self.half_rows(owner * self.share, 1 - at.y)],
                self.by_across.at[self.half_rows(owner * self.half, 0)],
                self.across_sems.at[owner],
                at.across,
                self.kind,
            )

    def both_sides(self, owner):
        at = self.place
        mine = self.half_rows(owner * self.share, at.y)
        slot = self.half_rows(owner * self.half, 0)
        arrived(self.by_across.at[slot], self.across_sems.at[owner], at.across)
        return mine, self.by_core[mine, :].astype(f32) + self.by_across[slot, :].astype(f32)

    def to_beside_second(self, span):
        at = self.place
        mine, value = self.both_sides(span * 2 + 1 - at.b)
        self.by_core[mine, :] = value.astype(bf16)
        self.copies.remote(
            self.by_core.at[mine],
            self.by_beside.at[pl.ds(span * self.apart, self.half)],
            self.beside_sems.at[span],
            at.beside,
            self.kind,
        )

    def to_beside_first(self, span):
        at = self.place
        owner = span * 2 + 1 - at.b
        rows = self.rows_of(owner)
        arrived(self.by_core.at[rows], self.core_sems.at[owner], at.core)
        value = self.own[rows, self.lanes(at.c)].astype(f32) + self.by_core[rows, :].astype(f32)
        self.by_core[rows, :] = value.astype(bf16)
        slot = pl.ds(span * self.share, self.share)
        self.copies.remote(
            self.by_core.at[rows],
            self.by_beside.at[slot],
            self.beside_sems.at[span],
            at.beside,
            self.kind,
        )

    def to_across_second(self, span):
        at = self.place
        owner = span * 2 + at.b
        rows = self.rows_of(owner)
        slot = pl.ds(span * self.share, self.share)
        arrived(self.by_core.at[rows], self.core_sems.at[owner], at.core)
        arrived(self.by_beside.at[slot], self.beside_sems.at[span], at.beside)
        value = (
            self.own[rows, self.lanes(at.c)].astype(f32)
            + self.by_core[rows, :].astype(f32)
            + self.by_beside[slot, :].astype(f32)
        )
        self.by_core[rows, :] = value.astype(bf16)
        self.copies.remote(
            self.by_core.at[self.half_rows(owner * self.share, 1 - at.y)],
            self.by_across.at[self.half_rows(owner * self.half, 0)],
            self.across_sems.at[owner],
            at.across,
            self.kind,
        )

    def first(self, span):
        self.to_beside_first(span) if span in self.aside else self.to_across_first(span)

    def second(self, span):
        self.to_across_second(span) if span in self.aside else self.to_beside_second(span)

    def to_span(self, span):
        at = self.place
        owner = span * 2 + at.b
        mine, value = self.both_sides(owner)
        if span not in self.aside:
            slot = pl.ds(span * self.apart, self.half)
            arrived(self.by_beside.at[slot], self.beside_sems.at[span], at.beside)
            value = value + self.by_beside[slot, :].astype(f32)
        self.by_core[mine, :] = value.astype(bf16)
        self.copies.remote(
            self.by_core.at[mine],
            self.by_span.at[self.half_rows(at.a * self.half, 0)],
            self.span_sems.at[at.a],
            (at.group, owner),
            self.kind,
            at.a != span,
            span > 0,
        )

    def finish(self):
        at = self.place
        value = self.by_core[self.half_rows(at.strip * self.share, at.y), :].astype(f32)
        for spot in range(at.spans - 1):
            span = at.other(spot)
            slot = self.half_rows(span * self.half, 0)
            arrived(self.by_span.at[slot], self.span_sems.at[span], (at.group, span * 2 + at.b))
            value = value + self.by_span[slot, :].astype(f32)
        part = self.total.at[self.half_rows(0, at.y), self.lanes(at.c)]
        part[...] = value.astype(bf16)
        self.copies.remote(part, part, self.last_sems.at[at.y, at.c], at.across, self.kind)
        self.copies.remote(part, part, self.last_sems.at[at.y, at.c], at.core, self.kind)

    def join(self):
        at = self.place
        other = self.total.at[self.half_rows(0, 1 - at.y), self.lanes(at.c)]
        arrived(other, self.last_sems.at[1 - at.y, at.c], at.across)
        self.copies.remote(other, other, self.last_sems.at[1 - at.y, at.c], at.core, self.kind)

    def close(self):
        at = self.place
        for upper in (at.y, 1 - at.y):
            part = self.total.at[self.half_rows(0, upper), self.lanes(1 - at.c)]
            arrived(part, self.last_sems.at[upper, 1 - at.c], at.core)


def scatter_shapes(share, count, mixed):
    v = pltpu.VMEM
    dma = pltpu.SemaphoreType.DMA
    spans = count // 2
    return [
        v((share * count, FPN_CH), bf16),
        v((share * count, HALF), bf16),
        v((share // 2 * count, HALF), bf16),
        v((spans * share // (1 if mixed else 2), HALF), bf16),
        v((share // 2 * spans, HALF), bf16),
        dma((count,)),
        dma((count,)),
        dma((spans,)),
        dma((spans,)),
        dma((2, 2)),
    ]


def step_kernel(plan, own_lateral, pinned, *refs):
    refs = list(refs)

    def take(number):
        taken = refs[:number]
        del refs[:number]
        return taken

    features = take(4)
    grads = take(4)
    (coarse_grad, image_heights, lateral_in, conv_in, bias_in) = take(5)
    held = take(9)
    (conv_total, lateral_total, bias_total) = take(3)
    if pinned:
        g_v, p6_new, c_v = held[:4], held[4], held[5:]
    else:
        g_v, p6_new, c_v = take(4), take(1)[0], take(4)
    (p6_v,) = take(1)
    wide = take(4)
    x_v = take(4)
    (t1, t2, t3) = take(3)
    (conv_v, lateral_v, bias_v, bias_low) = take(4)
    (acc, pairs, edge, bias_acc) = take(4)
    g_halo = take(4)
    x_halo = take(4)
    (send_sems, local_sems, core_sems, conv_sems, lateral_sems, bias_sems, halo_sems) = take(7)
    conv_parts = take(10)
    if own_lateral:
        lateral_parts = take(10)
        lateral_grad = lateral_parts[0]
    else:
        (lateral_grad,) = take(1)
    sums = [None, t1, t2, t3]
    rows, width, depth, unit, blocks = plan.rows, plan.width, plan.depth, plan.unit, plan.blocks

    at = Place(plan.count)
    keep = block_keep(image_heights, blocks, at.strip, plan.count)
    copies = Copies(send_sems, local_sems, conv_v)
    conv_own = acc.at[pl.ds(0, plan.conv_rows)]
    lateral_own = acc.at[pl.ds(plan.conv_rows, plan.lateral_rows)]
    lateral_load = copies.local(lateral_in, lateral_own if own_lateral else lateral_v)
    strips = at.strips()
    partners = strips + [at.core, at.across]
    knock(partners)

    conv = Gather("taps", conv_v, plan.conv_rows, at, copies, conv_sems, core_sems.at[0])
    lateral = Gather(
        "laterals", lateral_v, plan.lateral_rows, at, copies, lateral_sems, core_sems.at[1]
    )
    lateral_load.wait()
    if own_lateral:
        start = pl.multiple_of(at.strip * plan.lateral_rows, 16)
        lateral_v[pl.ds(start, plan.lateral_rows), :] = lateral_own[...].astype(bf16)
    conv_load = copies.local(conv_in, conv_own)
    grad_loads = [copies.local(grads[k], g_v[k]) for k in (3, 2, 1, 0)][::-1]
    coarse_load = copies.local(coarse_grad, p6_v)
    answer(partners)
    if own_lateral:
        lateral.along()
        lateral.aside()
    conv_load.wait()
    start = pl.multiple_of(at.strip * plan.conv_rows, 16)
    conv_v[pl.ds(start, plan.conv_rows), :] = conv_own[...].astype(bf16)
    bias_v[at.strip] = jnp.broadcast_to(bias_in[...].astype(bf16).astype(f32), (8, FPN_CH))
    for device in strips:
        copies.remote(
            bias_v.at[at.strip], bias_v.at[at.strip], bias_sems.at[at.strip], device, "bias"
        )

    grad_loads[3].wait()
    coarse_load.wait()
    for r in range(rows[3] // 2):
        quarter = doubled(pairs, 0, 0.25 * p6_v[r].astype(f32))
        for s in range(2):
            whole = g_v[3][2 * r + s].astype(f32) + quarter
            g_v[3][2 * r + s] = whole.astype(bf16)
    bias_acc[...] = jnp.zeros_like(bias_acc)

    def slot_of(k, j):
        return j if k else 0

    def spread(k, j, first_time):
        tile = wide[k].at[slot_of(k, j)]

        def body(i, carry):
            value = g_v[k][j * unit[k] + i]
            put_shifted(tile.at[i + 1], value)
            if first_time:
                bias_acc[LEVELS + k] += row_sum(value)
            return carry

        lax.fori_loop(0, unit[k], body, 0)

    def spread_rims(k, j, saved):
        tile = wide[k].at[slot_of(k, j)]
        up = g_halo[k][0] if j == 0 else g_v[k][j * unit[k] - 1]
        put_shifted(tile.at[0], masked(up, keep[j]))
        if saved:
            down = edge[...]
        else:
            down = g_halo[k][1] if j == blocks - 1 else g_v[k][(j + 1) * unit[k]]
        put_shifted(tile.at[unit[k] + 1], masked(down, keep[j + 1]))

    near_row = [(1 - at.b) * (rows[k] - 1) for k in range(LEVELS)]
    far_row = [at.b * (rows[k] - 1) for k in range(LEVELS)]
    far = (at.group, at.strip - 1 + 2 * at.b)
    has_far = (at.strip - 1 + 2 * at.b + 1) % (at.count + 1) > 0

    def send_near(row, halo, index):
        kind = ("near", index // LEVELS)
        copies.remote(row, halo.at[at.b], halo_sems.at[index, at.b], at.beside, kind)

    def send_far(row, halo, index):
        kind = ("far", index // LEVELS)
        copies.remote(row, halo.at[1 - at.b], halo_sems.at[index, 1 - at.b], far, kind, has_far)

    def take_rims(halo, index):
        arrived(halo.at[1 - at.b], halo_sems.at[index, 1 - at.b], at.beside)
        pl.when(has_far)(lambda: arrived(halo.at[at.b], halo_sems.at[index, at.b], far))

        def clear():
            halo[at.b] = jnp.zeros(halo.shape[1:], bf16)

        pl.when(jnp.logical_not(has_far))(clear)

    places = [None, *range(at.spans - 1)]
    for k in (2, 1, 0):
        grad_loads[k].wait()
    for k in (3, 2, 1, 0):
        send_far(g_v[k].at[far_row[k]], g_halo[k], k)
    conv.along()
    feature_loads = [copies.local(features[k], c_v[k]) for k in (3, 2, 1, 0)][::-1]
    def spread_level(k):
        def body(r, carry):
            value = g_v[k][r]
            put_shifted(wide[k].at[r // unit[k], lax.rem(r, unit[k]) + 1], value)
            bias_acc[LEVELS + k] += row_sum(value)
            return carry

        lax.fori_loop(0, rows[k], body, 0)

    for k in (3, 2, 1):
        spread_level(k)
    spread(0, 0, True)
    if own_lateral:
        for spot in range(at.spans - 1):
            lateral.from_span(spot)
    for k in (3, 2, 1, 0):
        send_near(g_v[k].at[near_row[k]], g_halo[k], k)
    conv.aside()
    if own_lateral:
        for spot in places:
            lateral.from_beside(spot)
        for spot in places:
            lateral.from_across(spot)
        lateral.from_core()
    for k, device in enumerate(strips):
        owner = lax.rem(at.strip + k + 1, at.count)
        arrived(bias_v.at[owner], bias_sems.at[owner], device)
    per = plan.count // 8
    for j in range(8):
        total = bias_v[j * per]
        for other in range(1, per):
            total = total + bias_v[j * per + other]
        bias_low[j] = total

    def top_values(k, r, count):
        pixels = count * width[k]
        value = jnp.dot(
            c_v[k][pl.ds(r, count)].reshape(pixels, depth[k]),
            lateral_v[plan.bounds[k] : plan.bounds[k + 1], :],
            preferred_element_type=f32,
        )
        value = (value + bias_low[k][0:1, :]).reshape(count, width[k], FPN_CH)
        if k == 3:
            return [value[s] for s in range(count)]
        tops = []
        for s in range(count // 2):
            raised = doubled(pairs, s * width[k], sums[k + 1][r // 2 + s])
            tops += [value[2 * s] + raised, value[2 * s + 1] + raised]
        return tops

    def top_level(k):
        count = min(4, unit[k])
        steps = unit[k] // count

        def body(t, carry):
            tops = top_values(k, t * count, count)
            for s in range(count):
                if k:
                    sums[k][t * count + s] = tops[s]
                x_v[k][t // steps, lax.rem(t, steps) * count + s + 1] = tops[s].astype(bf16)
            return carry

        lax.fori_loop(0, rows[k] // count, body, 0)

    for k in (3, 2, 1, 0):
        feature_loads[k].wait()
        top_level(k)
        for j in range(1, blocks):
            x_v[k][j - 1, unit[k] + 1] = masked(x_v[k][j, 1], keep[j])
            x_v[k][j, 0] = masked(x_v[k][j - 1, unit[k]], keep[j])
        if k == 1:
            conv.from_span(0)
    for k in (3, 2, 1, 0):
        take_rims(g_halo[k], k)
        for j in range(blocks if k else 1):
            spread_rims(k, j, False)

    conv_sum = Scatter(
        "tap sums", plan.conv_rows, (), *conv_parts[0:5], conv_total, at, copies, conv_parts[5:10]
    )
    conv_grad = conv_parts[0]
    if own_lateral:
        lateral_sum = Scatter(
            "lateral sums",
            plan.lateral_rows,
            range(at.spans // 2),
            *lateral_parts[0:5],
            lateral_total,
            at,
            copies,
            lateral_parts[5:10],
        )
    quarter = at.spans // LEVELS

    def spans_of(k):
        return range(k * quarter, (k + 1) * quarter)

    def each(step, items):
        for item in items:
            step(item)

    def for_level(step, k):
        for span in spans_of(k):
            step(span)

    def tap_dots(k, chunks):
        for dy in range(3):
            x = jnp.concatenate(
                [x_v[k][j, pl.ds(i + 1, n)].reshape(n * width[k], FPN_CH) for j, i, n in chunks],
                axis=0,
            )
            g = jnp.concatenate(
                [
                    wide[k][slot_of(k, j), pl.ds(i + dy, n)].reshape(n * width[k], 3 * FPN_CH)
                    for j, i, n in chunks
                ],
                axis=0,
            )
            dot = lax.dot_general(x, g, (((0,), (0,)), ((), ())), preferred_element_type=f32)
            for dx in range(3):
                yield 8 - (3 * dy + dx), dot[:, dx * FPN_CH : (dx + 1) * FPN_CH]

    def tap_grads(k):
        for tap, dot in tap_dots(k, [(j, 0, unit[k]) for j in range(blocks)]):
            start = k * TAPS + tap * FPN_CH
            conv_grad[start : start + FPN_CH, :] = dot.astype(bf16)

    def tap_rows(k, j, first, count):
        for tap, dot in tap_dots(k, [(j, first, count)]):
            acc[tap * FPN_CH : (tap + 1) * FPN_CH, :] += dot

    def x_rims():
        for k in (3, 2, 1, 0):
            send_far(x_v[k].at[at.b * (blocks - 1), 1 + at.b * (unit[k] - 1)], x_halo[k], LEVELS + k)
            send_near(
                x_v[k].at[(1 - at.b) * (blocks - 1), 1 + (1 - at.b) * (unit[k] - 1)],
                x_halo[k],
                LEVELS + k,
            )

    tap_grads(3)
    for_level(conv_sum.start, 3)
    tap_grads(2)
    for_level(conv_sum.start, 2)
    for spot in range(1, at.spans - 1):
        conv.from_span(spot)
    tap_grads(1)
    for_level(conv_sum.start, 1)
    conv.from_beside(None)
    acc[...] = jnp.zeros_like(acc)
    final = at.spans - 2

    def pass_on(spots):
        return lambda: each(conv.from_beside, [spot for spot in spots if spot < final])

    between = [
        pass_on([0]),
        lambda: each(
            lambda run: run(),
            [pass_on([1]), lambda: conv.across_first(final)] + [pass_on(range(2, final))],
        ),
        lambda: each(lambda run: run(), [x_rims, lambda: for_level(conv_sum.first, 3)]),
        lambda: each(lambda k: for_level(conv_sum.first, k), (2, 1)),
    ]
    step = unit[0] // 2

    def tap_half(t, carry):
        j, half = t // 2, lax.rem(t, 2)
        for later in range(1, blocks):

            def renew(later=later):
                spread(0, later, True)
                spread_rims(0, later, False)

            pl.when(t == 2 * later)(renew)
        tap_rows(0, j, half * step, step)
        for place, run in enumerate(between):
            pl.when(t == place)(run)
        return carry

    lax.fori_loop(0, 2 * blocks, tap_half, 0)
    conv_grad[0:TAPS, :] = acc[...].astype(bf16)
    for_level(conv_sum.start, 0)
    for spot in places[:-1]:
        conv.from_across(spot)
    conv.from_beside(final, True)
    conv.from_core()

    def top_rows(k, j, i, count):
        pixels = count * width[k]
        value = None
        for dy in range(3):
            for dx in range(3):
                tap = 8 - (3 * dy + dx)
                start = k * TAPS + tap * FPN_CH
                dot = lax.dot_general(
                    wide[k][
                        slot_of(k, j), pl.ds(i + dy, count), :, dx * FPN_CH : (dx + 1) * FPN_CH
                    ].reshape(pixels, FPN_CH),
                    conv_v[start : start + FPN_CH, :],
                    (((1,), (1,)), ((), ())),
                    preferred_element_type=f32,
                )
                value = dot if value is None else value + dot
        value = value.reshape(count, width[k], FPN_CH)
        first = j * unit[k] + i
        if k:
            value = value + sums[k][pl.ds(first, count)]
        low = value.astype(bf16)
        g_v[k][pl.ds(first, count)] = low
        bias_acc[k] += row_sum(low.reshape(pixels, FPN_CH))
        if k < 3:
            for s in range(count // 2):
                sums[k + 1][first // 2 + s] = halved(
                    pairs, s * width[k], value[2 * s] + value[2 * s + 1]
                )

    def top_level_grads(k):
        count = min(4, unit[k])
        steps = unit[k] // count

        def body(t, carry):
            top_rows(k, t // steps, lax.rem(t, steps) * count, count)
            return carry

        lax.fori_loop(0, rows[k] // count, body, 0)

    copies.settle(("near", 0), at.beside)
    copies.settle(("far", 0), far, has_far)
    steps = unit[0] // 4

    def top_four(t, carry):
        for turn in range(blocks):
            j = blocks - 1 - turn

            def renew(j=j):
                if j < blocks - 1:
                    spread(0, j, False)
                    spread_rims(0, j, True)
                if j:
                    edge[...] = g_v[0][j * unit[0]]

            pl.when(t == turn * steps)(renew)
        top_rows(0, blocks - 1 - t // steps, lax.rem(t, steps) * 4, 4)

        pl.when(t == steps - 1)(lambda: for_level(conv_sum.first, 0))
        pl.when(t == steps)(lambda: for_level(conv_sum.second, 3))
        pl.when(t == blocks * steps - 2)(lambda: for_level(conv_sum.second, 2))
        return carry

    lax.fori_loop(0, blocks * steps, top_four, 0)
    for k in range(1, LEVELS):
        top_level_grads(k)
        if k == 1:
            for_level(conv_sum.second, 1)
            for_level(conv_sum.to_span, 3)
    for_level(conv_sum.to_span, 2)

    for k in (3, 2, 1):
        value = lax.dot_general(
            c_v[k][...].reshape(rows[k] * width[k], depth[k]),
            g_v[k][...].reshape(rows[k] * width[k], FPN_CH),
            (((0,), (0,)), ((), ())),
            preferred_element_type=f32,
        )
        lateral_grad[plan.bounds[k] : plan.bounds[k + 1], :] = value.astype(bf16)
    for_level(conv_sum.second, 0)
    across, core = plan.count, plan.count + 1
    own_bias = jnp.concatenate(
        [jnp.sum(bias_acc[j], axis=0, keepdims=True) for j in range(8)], axis=0
    )
    bias_v[across + 4] = own_bias
    for device in strips:
        copies.remote(
            bias_v.at[across + 4],
            bias_grad_slot(bias_v, plan, at.strip),
            bias_sems.at[across + 2 + at.strip],
            device,
            "bias",
        )
    bias_v[across + 5 + at.strip] = own_bias
    count = min(8, rows[0])
    acc[0 : depth[0], :] = jnp.zeros((depth[0], FPN_CH), f32)

    def lateral_block(i, carry):
        acc[0 : depth[0], :] += lax.dot_general(
            c_v[0][pl.ds(i * count, count)].reshape(count * width[0], depth[0]),
            g_v[0][pl.ds(i * count, count)].reshape(count * width[0], FPN_CH),
            (((0,), (0,)), ((), ())),
            preferred_element_type=f32,
        )
        return carry

    spans = range(at.spans)
    late = [span for span in spans if span * 2 * plan.lateral_rows < depth[0]]
    if own_lateral:
        for span in spans:
            if span not in late:
                lateral_sum.start(span)
    lax.fori_loop(0, rows[0] // count, lateral_block, 0)
    lateral_grad[0 : depth[0], :] = acc[0 : depth[0], :].astype(bf16)
    if own_lateral:
        for span in late:
            lateral_sum.start(span)
        for span in spans:
            if span not in late:
                lateral_sum.first(span)

    for_level(conv_sum.to_span, 1)

    outs = []
    for k in range(LEVELS):
        count = max(1, min(rows[k], 1024 // width[k]))

        def feature_block(i, carry, k=k, count=count):
            value = lax.dot_general(
                g_v[k][pl.ds(i * count, count)].reshape(count * width[k], FPN_CH),
                lateral_v[plan.bounds[k] : plan.bounds[k + 1], :],
                (((1,), (1,)), ((), ())),
                preferred_element_type=f32,
            )
            c_v[k][pl.ds(i * count, count)] = value.astype(bf16).reshape(count, width[k], depth[k])
            return carry

        lax.fori_loop(0, rows[k] // count, feature_block, 0)
        if k == 0:
            if own_lateral:
                for span in late:
                    lateral_sum.first(span)
            for_level(conv_sum.to_span, 0)

    for k in range(LEVELS):
        take_rims(x_halo[k], LEVELS + k)
        x_v[k][0, 0] = masked(x_halo[k][0], keep[0])
        x_v[k][blocks - 1, unit[k] + 1] = masked(x_halo[k][1], keep[blocks])

    def widen(k, j):
        tile = wide[k].at[slot_of(k, j)]

        def body(i, carry):
            put_shifted(tile.at[i], x_v[k][j, i])
            return carry

        lax.fori_loop(0, unit[k] + 2, body, 0)

    def pyramid_rows(k, j, i, count):
        pixels = count * width[k]
        value = jnp.dot(
            jnp.concatenate(
                [
                    wide[k][slot_of(k, j), pl.ds(i + dy, count)].reshape(pixels, 3 * FPN_CH)
                    for dy in range(3)
                ],
                axis=1,
            ),
            conv_v[k * TAPS : (k + 1) * TAPS, :],
            preferred_element_type=f32,
        )
        value = (value + bias_low[LEVELS + k][0:1, :]).reshape(count, width[k], FPN_CH)
        first = j * unit[k] + i
        g_v[k][pl.ds(first, count)] = value.astype(bf16)
        if k == 3:
            for s in range(count // 2):
                mean = 0.25 * halved(pairs, 0, value[2 * s] + value[2 * s + 1])
                p6_new[first // 2 + s] = mean.astype(bf16)

    def pyramid_block(k):
        count = min(4, unit[k])
        steps = unit[k] // count

        def widen_block(j, carry):
            widen(k, j)
            return carry

        def body(t, carry):
            pyramid_rows(k, t // steps, lax.rem(t, steps) * count, count)
            return carry

        lax.fori_loop(0, blocks, widen_block, 0)
        lax.fori_loop(0, rows[k] // count, body, 0)

    def end_close():
        conv_sum.close()

    def end_bias():
        arrived(bias_v.at[core], bias_sems.at[core], at.core)
        own = pl.ds(at.strip // per, 1)
        bias_total[...] = bias_v[across + 3, own, :] + bias_v[core, own, :]

    def end_drain():
        if not pinned:
            for source, target in zip([*g_v, p6_new, *c_v], held):
                outs.append(copies.local(source, target))
        for copy in outs:
            copy.wait()
        copies.settle(("far", 1), far, has_far)
        for kind in [kind for kind, (place, size) in copies.kinds.items() if size]:
            copies.settle(kind, at.core)

    pyramid_block(1)
    if own_lateral:
        for span in spans:
            lateral_sum.second(span)
    for k in range(2, LEVELS):
        pyramid_block(k)
    def end_first():
        conv_sum.finish()
        for k, device in enumerate(strips):
            owner = lax.rem(at.strip + k + 1, at.count)
            arrived(bias_grad_slot(bias_v, plan, owner), bias_sems.at[across + 2 + owner], device)
        total = bias_v[across + 5]
        for k in range(1, plan.count):
            total = total + bias_v[across + 5 + k]
        bias_v[across + 2] = total
        copies.remote(
            bias_v.at[across + 2], bias_v.at[across], bias_sems.at[across], at.across, "bias"
        )
        if own_lateral:
            for span in spans:
                lateral_sum.to_span(span)

    def end_second():
        conv_sum.join()
        arrived(bias_v.at[across], bias_sems.at[across], at.across)
        total = bias_v[across + 2] + bias_v[across]
        bias_v[across + 3] = total
        copies.remote(
            bias_v.at[across + 3], bias_v.at[core], bias_sems.at[core], at.core, "bias"
        )

    def end_third():
        if own_lateral:
            lateral_sum.finish()

    def pyramid_four(t, carry):
        j, i = t // steps, lax.rem(t, steps)
        pl.when(i == 0)(lambda: widen(0, j))
        pyramid_rows(0, j, i * 4, 4)
        pl.when(t == 1)(end_first)
        pl.when(t == (blocks - 1) * steps)(end_second)
        pl.when(t == (blocks - 1) * steps + 1)(end_third)
        return carry

    lax.fori_loop(0, blocks * steps, pyramid_four, 0)
    end_close()
    end_bias()
    if own_lateral:
        lateral_sum.join()
        lateral_sum.close()
    else:
        outs.append(copies.local(lateral_grad, lateral_total))
    end_drain()


def bias_grad_slot(bias_v, plan, owner):
    return bias_v.at[plan.count + 5 + owner]


def whole_step(plan, own_lateral, features, grads, coarse_grad, image_heights, lateral, conv, bias):
    rows, width, depth, unit, blocks = plan.rows, plan.width, plan.depth, plan.unit, plan.blocks
    shape = jax.ShapeDtypeStruct
    v = pltpu.VMEM
    total = plan.bounds[LEVELS]
    coarse = (rows[3] // 2, width[3] // 2, FPN_CH)
    pinned = own_lateral
    shapes = [(rows[k], width[k], FPN_CH) for k in range(LEVELS)] + [coarse]
    shapes += [(rows[k], width[k], depth[k]) for k in range(LEVELS)]
    out_shape = (
        [(v if pinned else shape)(s, bf16) for s in shapes]
        + [(v if pinned else shape)((plan.conv_rows, FPN_CH), bf16)]
        + [v((plan.lateral_rows, FPN_CH), bf16) if pinned else shape((total, FPN_CH), bf16)]
        + [shape((1, FPN_CH), f32)]
    )
    dma = pltpu.SemaphoreType.DMA
    scratch = (
        ([] if pinned else [v(s, bf16) for s in shapes])
        + [v(coarse, bf16)]
        + [v((blocks if k else 1, unit[k] + 2, width[k], 3 * FPN_CH), bf16) for k in range(LEVELS)]
        + [v((blocks, unit[k] + 2, width[k], FPN_CH), bf16) for k in range(LEVELS)]
        + [v((rows[k], width[k], FPN_CH), f32) for k in (1, 2, 3)]
        + [v((LEVELS * TAPS, FPN_CH), bf16), v((total, FPN_CH), bf16)]
        + [v((2 * plan.count + 5, 8, FPN_CH), f32), v((8, 8, FPN_CH), f32)]
        + [v((TAPS, FPN_CH), f32), v((FPN_CH // HALF, 2 * width[0], HALF), f32)]
        + [v((width[0], FPN_CH), bf16), v((8, 8, FPN_CH), f32)]
        + [v((2, width[k], FPN_CH), bf16) for k in range(LEVELS)] * 2
        + [dma((16 + plan.count // 2,)), dma((24,)), dma((2,))]
        + [dma((plan.count, 2)), dma((plan.count, 2))]
        + [dma((2 * plan.count + 2,)), dma((2 * LEVELS, 2))]
        + scatter_shapes(plan.conv_rows, plan.count, False)
        + (
            scatter_shapes(plan.lateral_rows, plan.count, True)
            if own_lateral
            else [v((total, FPN_CH), bf16)]
        )
    )
    return pl.pallas_call(
        functools.partial(step_kernel, plan, own_lateral, pinned),
        out_shape=out_shape,
        in_specs=[ANY] * 9 + [pl.BlockSpec(memory_space=pltpu.SMEM), ANY, ANY, VMEM],
        out_specs=[VMEM if pinned else ANY] * 9 + [VMEM, VMEM if own_lateral else ANY, VMEM],
        scratch_shapes=scratch,
        name="step",
        cost_estimate=pl.CostEstimate(
            flops=45 << 30, bytes_accessed=60 << 20, transcendentals=0
        ),
        compiler_params=pltpu.CompilerParams(
            collective_id=0, has_side_effects=True, vmem_limit_bytes=ROOM if pinned else WHOLE_ROOM
        ),
    )(*features, *grads, coarse_grad, image_heights, lateral, conv, bias)


def update_kernel(count, *refs):
    refs = list(refs)

    def take(number):
        taken = refs[:number]
        del refs[:number]
        return taken

    held = take(count)
    sums = take(3)
    given = [take(3), take(3), take(3)]
    held_out = take(count)
    results = [take(3), take(3), take(3)]
    work = [take(3), take(3)]
    (sems,) = take(1)
    used = [0]

    def begin(source, target):
        copy = pltpu.make_async_copy(source, target, sems.at[used[0]])
        used[0] += 1
        copy.start()
        return copy

    loads = [[begin(given[i][j], work[i][j]) for j in range(3)] for i in range(2)]
    outs = [begin(source, target) for source, target in zip(held, held_out)]
    rates = ((conv_rate, decay_rate), (lateral_rate, decay_rate), (bias_rate, 0.0))
    for i in range(2):
        for load in loads[i]:
            load.wait()
        rows = work[i][0].shape[0]
        step = next(size for size in (96, 48, 16, rows) if rows % size == 0)

        def update(r, carry, i=i, step=step):
            part = pl.ds(r * step, step)
            weight, moment, average = (work[i][j][part, :] for j in range(3))
            total = sums[i][part, :].astype(f32)
            new = nesterov(weight, total, moment, average, *rates[i])
            for j in range(3):
                work[i][j][part, :] = new[j]
            return carry

        lax.fori_loop(0, rows // step, update, 0)
        outs += [begin(work[i][j], results[i][j]) for j in range(3)]
    weight, moment, average = (given[2][j][...] for j in range(3))
    new = nesterov(weight, sums[2][...], moment, average, *rates[2])
    for j in range(3):
        results[2][j][...] = new[j]
    for copy in outs:
        copy.wait()


def update(held, sums, given):
    shape = jax.ShapeDtypeStruct
    place = pltpu.with_memory_space_constraint
    kept = [place(x, pltpu.VMEM) for x in held]
    far = [place(x, pltpu.HBM) for g in given[:2] for x in g]
    results = [shape(g[0].shape, f32) for g in given for _ in range(3)]
    return pl.pallas_call(
        functools.partial(update_kernel, len(held)),
        out_shape=[shape(x.shape, x.dtype) for x in held] + results,
        in_specs=[ANY] * len(held) + [VMEM] * 3 + [HBM] * 6 + [VMEM] * 3,
        out_specs=[HBM] * (len(held) + 6) + [VMEM] * 3,
        scratch_shapes=[pltpu.VMEM(g[0].shape, f32) for g in given[:2] for _ in range(3)]
        + [pltpu.SemaphoreType.DMA((len(held) + 12,))],
        name="update",
        cost_estimate=pl.CostEstimate(flops=8 << 20, bytes_accessed=25 << 20, transcendentals=0),
        compiler_params=pltpu.CompilerParams(vmem_limit_bytes=24 << 20),
    )(*kept, *sums, *far, *given[2])


def shards(
    feature_c2,
    feature_c3,
    feature_c4,
    feature_c5,
    cotangent_p2,
    cotangent_p3,
    cotangent_p4,
    cotangent_p5,
    cotangent_p6,
    image_heights,
    lateral_weight,
    conv_weight,
    bias_all,
    lateral_momentum,
    conv_momentum,
    bias_momentum,
    lateral_ema,
    conv_ema,
    bias_ema,
):
    features = (feature_c2, feature_c3, feature_c4, feature_c5)
    grads = (cotangent_p2, cotangent_p3, cotangent_p4, cotangent_p5)
    count = lax.axis_size("rows")
    strip = lax.axis_index("rows")
    plan = Plan(features, count, lateral_weight.shape[0], conv_weight.shape[0])
    own_lateral = plan.lateral_rows % 16 == 0
    share = bias_all.shape[0]
    if share == FPN_CH:
        bias_row = bias_all.reshape(1, FPN_CH)
    else:
        place = lax.rem(strip * share, FPN_CH)
        lane = jnp.arange(FPN_CH)
        inside = jnp.logical_and(lane >= place, lane < place + share)
        bias_row = jnp.where(inside, jnp.tile(bias_all, FPN_CH // share), 0.0)[None, :]
    if own_lateral:
        lateral_in = lateral_weight
    else:
        lateral_in = lax.all_gather(lateral_weight.astype(bf16), "rows", axis=0, tiled=True)
    results = whole_step(
        plan,
        own_lateral,
        features,
        grads,
        cotangent_p6,
        image_heights,
        lateral_in,
        conv_weight,
        bias_row,
    )
    sum_conv, sum_lateral, sum_bias = results[9:]
    if not own_lateral:
        sum_lateral = lax.psum(
            lax.psum_scatter(sum_lateral, "rows", scatter_dimension=0, tiled=True), "grp"
        ).astype(f32)
    row = (1, share)
    if share < FPN_CH:
        sum_bias = lax.dynamic_slice_in_dim(sum_bias, place, share, axis=1)
    held = results[:9] if own_lateral else []
    new = update(
        held,
        (sum_conv, sum_lateral, sum_bias),
        (
            (conv_weight, conv_momentum, conv_ema),
            (lateral_weight, lateral_momentum, lateral_ema),
            (bias_all.reshape(row), bias_momentum.reshape(row), bias_ema.reshape(row)),
        ),
    )
    held = new[: len(held)] or results[:9]
    first = len(new) - 9
    conv_new, lateral_new, bias_new = (new[first + i : first + i + 3] for i in (0, 3, 6))
    return (
        *held,
        lateral_new[0],
        conv_new[0],
        bias_new[0].reshape(share),
        lateral_new[1],
        conv_new[1],
        bias_new[1].reshape(share),
        lateral_new[2],
        conv_new[2],
        bias_new[2].reshape(share),
    )


def solution(mesh):
    cut = P(("grp", "rows"), None, None)
    wide = P("rows", None)
    in_specs = (cut,) * 9 + (P("grp", None),) + (wide, wide, P("rows")) * 3
    out_specs = (cut,) * 9 + (wide, wide, P("rows")) * 3
    return jax.shard_map(
        shards,
        mesh=mesh,
        in_specs=in_specs,
        out_specs=out_specs,
        check_vma=False,
    )
```

```python
import functools

import jax
import jax.numpy as jnp
from jax import lax
from jax.experimental import pallas as pl
from jax.experimental.pallas import tpu as pltpu
from jax.sharding import PartitionSpec as P

FPN_CH = 256
C2_CH = 256
C3_CH = 512
C4_CH = 1024
C5_CH = 2048
STEP = 10
LEVELS = 4
TAPS = 9 * FPN_CH
HALF = FPN_CH // 2

momentum_rate = 0.9
decay_rate = 0.0001
lateral_rate = 1.2e-05
conv_rate = 8e-06
bias_rate = 0.00013

MESH = pl.DeviceIdType.MESH
ANY = pl.BlockSpec(memory_space=pl.ANY)
VMEM = pl.BlockSpec(memory_space=pltpu.VMEM)
HBM = pl.BlockSpec(memory_space=pltpu.HBM)
f32 = jnp.float32
bf16 = jnp.bfloat16
ROOM = 49 << 20
WHOLE_ROOM = 63 << 20


def nesterov(weight, grad, moment, average, rate, decay):
    ema_keep = min(0.999, (1.0 + STEP) / (10.0 + STEP))
    step_grad = grad + decay * weight
    moment_new = momentum_rate * moment + step_grad
    weight_new = weight - rate * (step_grad + momentum_rate * moment_new)
    average_new = ema_keep * average + (1.0 - ema_keep) * weight_new
    return (weight_new, moment_new, average_new)


def block_keep(image_heights, blocks, strip, count):
    starts = [0]
    for image in range(image_heights.shape[1] - 1):
        starts.append(starts[-1] + image_heights[0, image])
    keep = []
    for border in range(blocks + 1):
        place = strip * blocks + border
        opening = place == blocks * count
        for start in starts:
            opening = jnp.logical_or(opening, place == start)
        keep.append(jnp.where(opening, 0.0, 1.0).astype(f32))
    return keep


class Plan:
    def __init__(self, features, rows_count, lateral_rows, conv_rows):
        self.count = rows_count
        self.rows = [f.shape[0] for f in features]
        self.width = [f.shape[1] for f in features]
        self.depth = [f.shape[2] for f in features]
        self.unit = [16 >> k for k in range(LEVELS)]
        self.blocks = self.rows[0] // self.unit[0]
        self.lateral_rows = lateral_rows
        self.conv_rows = conv_rows
        self.bounds = [sum(self.depth[:k]) for k in range(LEVELS + 1)]


def put_shifted(target, value):
    wide = value.astype(f32)
    width = wide.shape[0]
    at = lax.broadcasted_iota(jnp.int32, wide.shape, 0)
    zero = jnp.zeros_like(wide)
    target[:, 0:FPN_CH] = jnp.where(at == 0, zero, pltpu.roll(wide, 1, 0)).astype(bf16)
    target[:, FPN_CH : 2 * FPN_CH] = value
    target[:, 2 * FPN_CH : 3 * FPN_CH] = jnp.where(
        at == width - 1, zero, pltpu.roll(wide, width - 1, 0)
    ).astype(bf16)


def masked(value, keep):
    return (value.astype(f32) * keep).astype(bf16)


def row_sum(value):
    wide = value.astype(f32)
    return jnp.sum(wide.reshape(wide.shape[0] // 8, 8, wide.shape[1]), axis=0)


def doubled(pairs, base, value):
    count = value.shape[0]
    sides = []
    for side in range(FPN_CH // HALF):
        part = value[:, side * HALF : (side + 1) * HALF]
        pairs[side, pl.ds(base, count, stride=2), :] = part
        pairs[side, pl.ds(base + 1, count, stride=2), :] = part
        sides.append(pairs[side, base : base + 2 * count, :])
    return jnp.concatenate(sides, axis=1)


def halved(pairs, base, value):
    count = value.shape[0] // 2
    sides = []
    for side in range(FPN_CH // HALF):
        pairs[side, base : base + 2 * count, :] = value[:, side * HALF : (side + 1) * HALF]
        sides.append(
            pairs[side, pl.ds(base, count, stride=2), :]
            + pairs[side, pl.ds(base + 1, count, stride=2), :]
        )
    return jnp.concatenate(sides, axis=1)


class Copies:
    def __init__(self, sends, locals_, ruler):
        self.sends = sends
        self.locals_ = locals_
        self.ruler = ruler
        self.kinds = {}
        self.used = 0

    def remote(self, source, target, arrival, device, kind, when=None, counts=True):
        size = source.dtype.itemsize
        for length in source.shape:
            size *= length
        most = self.ruler.shape[0] * HALF * self.ruler.dtype.itemsize
        while kind in self.kinds and self.kinds[kind][1] + size > most:
            kind = (kind, "more")
        if kind not in self.kinds:
            self.kinds[kind] = [len(self.kinds), 0]
        kept = self.kinds[kind]
        copy = pltpu.make_async_remote_copy(
            src_ref=source,
            dst_ref=target,
            send_sem=self.sends.at[kept[0]],
            recv_sem=arrival,
            device_id=device,
            device_id_type=MESH,
        )
        if counts:
            kept[1] += size
        if when is None:
            copy.start()
        else:
            pl.when(when)(copy.start)

    def settle(self, kind, device, when=None):
        place, size = self.kinds.pop(kind)
        self.kinds[kind, "settled"] = [place, 0]
        wide = size % (16 * FPN_CH) == 0
        lanes = FPN_CH if wide else HALF
        rows = self.ruler.at[pl.ds(0, size // (2 * lanes)), pl.ds(0, lanes)]
        copy = pltpu.make_async_remote_copy(
            src_ref=rows,
            dst_ref=rows,
            send_sem=self.sends.at[place],
            recv_sem=self.sends.at[place],
            device_id=device,
            device_id_type=MESH,
        )
        if when is None:
            copy.wait_send()
        else:
            pl.when(when)(copy.wait_send)

    def local(self, source, target):
        copy = pltpu.make_async_copy(source, target, self.locals_.at[self.used])
        self.used += 1
        copy.start()
        return copy


def arrived(target, semaphore, device):
    pltpu.make_async_remote_copy(
        src_ref=target,
        dst_ref=target,
        send_sem=semaphore,
        recv_sem=semaphore,
        device_id=device,
        device_id_type=MESH,
    ).wait_recv()


class Place:
    def __init__(self, count):
        self.count = count
        self.spans = count // 2
        self.strip = lax.axis_index("rows")
        self.group = lax.axis_index("grp")
        self.a = self.strip // 2
        self.b = self.strip % 2
        self.y = self.group // 2
        self.c = self.group % 2
        self.core = (self.y * 2 + 1 - self.c, self.strip)
        self.across = ((1 - self.y) * 2 + self.c, self.strip)
        self.beside = (self.group, self.a * 2 + 1 - self.b)

    def other(self, spot):
        return spot + (spot - self.a + self.spans) // self.spans

    def strips(self):
        return [(self.group, lax.rem(self.strip + k, self.count)) for k in range(1, self.count)]


def knock(devices):
    for device in devices:
        pl.semaphore_signal(
            pltpu.get_barrier_semaphore(), inc=1, device_id=device, device_id_type=MESH
        )


def answer(devices):
    pl.semaphore_wait(pltpu.get_barrier_semaphore(), len(devices))


class Gather:
    def __init__(self, kind, full, share, place, copies, arrivals, core_arrivals):
        self.kind = kind
        self.full = full
        self.share = share
        self.core_arrivals = core_arrivals
        self.place = place
        self.copies = copies
        self.arrivals = arrivals

    def piece(self, owner, upper, lane):
        half = self.share // 2
        start = pl.multiple_of(owner * self.share + upper * half, 16 if half % 16 == 0 else 8)
        return self.full.at[pl.ds(start, half), pl.ds(pl.multiple_of(lane * HALF, HALF), HALF)]

    def send(self, owner, upper, lane, device):
        part = self.piece(owner, upper, lane)
        arrival = self.core_arrivals if device is self.place.core else self.arrivals.at[owner, upper]
        self.copies.remote(part, part, arrival, device, self.kind)

    def take(self, owner, upper, lane, device):
        arrived(self.piece(owner, upper, lane), self.arrivals.at[owner, upper], device)

    def along(self):
        at = self.place
        for spot in range(at.spans - 1):
            self.send(at.strip, at.y, at.c, (at.group, at.other(spot) * 2 + at.b))

    def aside(self):
        at = self.place
        self.send(at.strip, at.y, at.c, at.beside)

    def from_span(self, spot):
        at = self.place
        owner = at.other(spot) * 2 + at.b
        self.take(owner, at.y, at.c, (at.group, owner))
        for device in (at.across, at.beside, at.core):
            self.send(owner, at.y, at.c, device)

    def mine(self, spot):
        return self.place.other(spot) * 2 + self.place.b

    def facing(self, spot):
        at = self.place
        return (at.a if spot is None else at.other(spot)) * 2 + 1 - at.b

    def from_beside(self, spot, whole=False):
        at = self.place
        owner = self.facing(spot)
        for upper in (at.y, 1 - at.y)[: 2 if whole else 1]:
            self.take(owner, upper, at.c, at.beside)
            self.send(owner, upper, at.c, at.core)
        if not whole:
            self.send(owner, at.y, at.c, at.across)

    def across_first(self, spot):
        at = self.place
        owner = self.mine(spot)
        self.take(owner, 1 - at.y, at.c, at.across)
        for device in (at.beside, at.core):
            self.send(owner, 1 - at.y, at.c, device)

    def from_across(self, spot):
        at = self.place
        for owner in [self.facing(spot)] if spot is None else [self.mine(spot), self.facing(spot)]:
            self.take(owner, 1 - at.y, at.c, at.across)
            self.send(owner, 1 - at.y, at.c, at.core)

    def from_core(self):
        at = self.place
        rows = (at.count - 1) * self.share // 2
        arrived(self.full.at[pl.ds(0, rows)], self.core_arrivals, at.core)


class Scatter:
    def __init__(self, kind, share, aside, own, by_core, by_across, by_beside, by_span, total, place, copies, sems):
        self.kind = kind
        self.share = share
        self.half = share // 2
        self.aside = aside
        self.apart = share if aside else share // 2
        self.own = own
        self.by_core, self.by_across, self.by_beside, self.by_span = by_core, by_across, by_beside, by_span
        self.total = total
        self.place = place
        self.copies = copies
        self.core_sems, self.across_sems, self.beside_sems, self.span_sems, self.last_sems = sems

    def lanes(self, lane):
        return pl.ds(pl.multiple_of(lane * HALF, HALF), HALF)

    def rows_of(self, owner):
        return pl.ds(pl.multiple_of(owner * self.share, 16), self.share)

    def half_rows(self, base, upper):
        step = 16 if self.half % 16 == 0 else 8
        return pl.ds(pl.multiple_of(base + upper * self.half, step), self.half)

    def start(self, span):
        at = self.place
        for owner in (span * 2 + 1 - at.b, span * 2 + at.b):
            self.copies.remote(
                self.own.at[self.rows_of(owner), self.lanes(1 - at.c)],
                self.by_core.at[self.rows_of(owner)],
                self.core_sems.at[owner],
                at.core,
                (self.kind, "core"),
            )

    def to_across_first(self, span):
        at = self.place
        for owner in (span * 2 + 1 - at.b, span * 2 + at.b):
            rows = self.rows_of(owner)
            arrived(self.by_core.at[rows], self.core_sems.at[owner], at.core)
            value = self.own[rows, self.lanes(at.c)].astype(f32) + self.by_core[rows, :].astype(f32)
            self.by_core[rows, :] = value.astype(bf16)
            self.copies.remote(
                self.by_core.at[self.half_rows(owner * self.share, 1 - at.y)],
                self.by_across.at[self.half_rows(owner * self.half, 0)],
                self.across_sems.at[owner],
                at.across,
                self.kind,
            )

    def both_sides(self, owner):
        at = self.place
        mine = self.half_rows(owner * self.share, at.y)
        slot = self.half_rows(owner * self.half, 0)
        arrived(self.by_across.at[slot], self.across_sems.at[owner], at.across)
        return mine, self.by_core[mine, :].astype(f32) + self.by_across[slot, :].astype(f32)

    def to_beside_second(self, span):
        at = self.place
        mine, value = self.both_sides(span * 2 + 1 - at.b)
        self.by_core[mine, :] = value.astype(bf16)
        self.copies.remote(
            self.by_core.at[mine],
            self.by_beside.at[pl.ds(span * self.apart, self.half)],
            self.beside_sems.at[span],
            at.beside,
            self.kind,
        )

    def to_beside_first(self, span):
        at = self.place
        owner = span * 2 + 1 - at.b
        rows = self.rows_of(owner)
        arrived(self.by_core.at[rows], self.core_sems.at[owner], at.core)
        value = self.own[rows, self.lanes(at.c)].astype(f32) + self.by_core[rows, :].astype(f32)
        self.by_core[rows, :] = value.astype(bf16)
        slot = pl.ds(span * self.share, self.share)
        self.copies.remote(
            self.by_core.at[rows],
            self.by_beside.at[slot],
            self.beside_sems.at[span],
            at.beside,
            self.kind,
        )

    def to_across_second(self, span):
        at = self.place
        owner = span * 2 + at.b
        rows = self.rows_of(owner)
        slot = pl.ds(span * self.share, self.share)
        arrived(self.by_core.at[rows], self.core_sems.at[owner], at.core)
        arrived(self.by_beside.at[slot], self.beside_sems.at[span], at.beside)
        value = (
            self.own[rows, self.lanes(at.c)].astype(f32)
            + self.by_core[rows, :].astype(f32)
            + self.by_beside[slot, :].astype(f32)
        )
        self.by_core[rows, :] = value.astype(bf16)
        self.copies.remote(
            self.by_core.at[self.half_rows(owner * self.share, 1 - at.y)],
            self.by_across.at[self.half_rows(owner * self.half, 0)],
            self.across_sems.at[owner],
            at.across,
            self.kind,
        )

    def first(self, span):
        self.to_beside_first(span) if span in self.aside else self.to_across_first(span)

    def second(self, span):
        self.to_across_second(span) if span in self.aside else self.to_beside_second(span)

    def to_span(self, span):
        at = self.place
        owner = span * 2 + at.b
        mine, value = self.both_sides(owner)
        if span not in self.aside:
            slot = pl.ds(span * self.apart, self.half)
            arrived(self.by_beside.at[slot], self.beside_sems.at[span], at.beside)
            value = value + self.by_beside[slot, :].astype(f32)
        self.by_core[mine, :] = value.astype(bf16)
        self.copies.remote(
            self.by_core.at[mine],
            self.by_span.at[self.half_rows(at.a * self.half, 0)],
            self.span_sems.at[at.a],
            (at.group, owner),
            self.kind,
            at.a != span,
            span > 0,
        )

    def finish(self):
        at = self.place
        value = self.by_core[self.half_rows(at.strip * self.share, at.y), :].astype(f32)
        for spot in range(at.spans - 1):
            span = at.other(spot)
            slot = self.half_rows(span * self.half, 0)
            arrived(self.by_span.at[slot], self.span_sems.at[span], (at.group, span * 2 + at.b))
            value = value + self.by_span[slot, :].astype(f32)
        part = self.total.at[self.half_rows(0, at.y), self.lanes(at.c)]
        part[...] = value.astype(bf16)
        self.copies.remote(part, part, self.last_sems.at[at.y, at.c], at.across, self.kind)
        self.copies.remote(part, part, self.last_sems.at[at.y, at.c], at.core, self.kind)

    def join(self):
        at = self.place
        other = self.total.at[self.half_rows(0, 1 - at.y), self.lanes(at.c)]
        arrived(other, self.last_sems.at[1 - at.y, at.c], at.across)
        self.copies.remote(other, other, self.last_sems.at[1 - at.y, at.c], at.core, self.kind)

    def close(self):
        at = self.place
        for upper in (at.y, 1 - at.y):
            part = self.total.at[self.half_rows(0, upper), self.lanes(1 - at.c)]
            arrived(part, self.last_sems.at[upper, 1 - at.c], at.core)


def scatter_shapes(share, count, mixed):
    v = pltpu.VMEM
    dma = pltpu.SemaphoreType.DMA
    spans = count // 2
    return [
        v((share * count, FPN_CH), bf16),
        v((share * count, HALF), bf16),
        v((share // 2 * count, HALF), bf16),
        v((spans * share // (1 if mixed else 2), HALF), bf16),
        v((share // 2 * spans, HALF), bf16),
        dma((count,)),
        dma((count,)),
        dma((spans,)),
        dma((spans,)),
        dma((2, 2)),
    ]


def step_kernel(plan, own_lateral, pinned, *refs):
    refs = list(refs)

    def take(number):
        taken = refs[:number]
        del refs[:number]
        return taken

    features = take(4)
    grads = take(4)
    (coarse_grad, image_heights, lateral_in, conv_in, bias_in) = take(5)
    held = take(9)
    (conv_total, lateral_total, bias_total) = take(3)
    if pinned:
        g_v, p6_new, c_v = held[:4], held[4], held[5:]
    else:
        g_v, p6_new, c_v = take(4), take(1)[0], take(4)
    (p6_v,) = take(1)
    wide = take(4)
    x_v = take(4)
    (t1, t2, t3) = take(3)
    (conv_v, lateral_v, bias_v, bias_low) = take(4)
    (acc, pairs, edge, bias_acc) = take(4)
    g_halo = take(4)
    x_halo = take(4)
    (send_sems, local_sems, core_sems, conv_sems, lateral_sems, bias_sems, halo_sems) = take(7)
    conv_parts = take(10)
    if own_lateral:
        lateral_parts = take(10)
        lateral_grad = lateral_parts[0]
    else:
        (lateral_grad,) = take(1)
    sums = [None, t1, t2, t3]
    rows, width, depth, unit, blocks = plan.rows, plan.width, plan.depth, plan.unit, plan.blocks

    at = Place(plan.count)
    keep = block_keep(image_heights, blocks, at.strip, plan.count)
    copies = Copies(send_sems, local_sems, conv_v)
    conv_own = acc.at[pl.ds(0, plan.conv_rows)]
    lateral_own = acc.at[pl.ds(plan.conv_rows, plan.lateral_rows)]
    lateral_load = copies.local(lateral_in, lateral_own if own_lateral else lateral_v)
    strips = at.strips()
    partners = strips + [at.core, at.across]
    knock(partners)

    conv = Gather("taps", conv_v, plan.conv_rows, at, copies, conv_sems, core_sems.at[0])
    lateral = Gather(
        "laterals", lateral_v, plan.lateral_rows, at, copies, lateral_sems, core_sems.at[1]
    )
    lateral_load.wait()
    if own_lateral:
        start = pl.multiple_of(at.strip * plan.lateral_rows, 16)
        lateral_v[pl.ds(start, plan.lateral_rows), :] = lateral_own[...].astype(bf16)
    conv_load = copies.local(conv_in, conv_own)
    grad_loads = [copies.local(grads[k], g_v[k]) for k in (3, 2, 1, 0)][::-1]
    coarse_load = copies.local(coarse_grad, p6_v)
    answer(partners)
    if own_lateral:
        lateral.along()
        lateral.aside()
    conv_load.wait()
    start = pl.multiple_of(at.strip * plan.conv_rows, 16)
    conv_v[pl.ds(start, plan.conv_rows), :] = conv_own[...].astype(bf16)
    bias_v[at.strip] = jnp.broadcast_to(bias_in[...].astype(bf16).astype(f32), (8, FPN_CH))
    for device in strips:
        copies.remote(
            bias_v.at[at.strip], bias_v.at[at.strip], bias_sems.at[at.strip], device, "bias"
        )

    grad_loads[3].wait()
    coarse_load.wait()
    for r in range(rows[3] // 2):
        quarter = doubled(pairs, 0, 0.25 * p6_v[r].astype(f32))
        for s in range(2):
            whole = g_v[3][2 * r + s].astype(f32) + quarter
            g_v[3][2 * r + s] = whole.astype(bf16)
    bias_acc[...] = jnp.zeros_like(bias_acc)

    def slot_of(k, j):
        return j if k else 0

    def spread(k, j, first_time):
        tile = wide[k].at[slot_of(k, j)]

        def body(i, carry):
            value = g_v[k][j * unit[k] + i]
            put_shifted(tile.at[i + 1], value)
            if first_time:
                bias_acc[LEVELS + k] += row_sum(value)
            return carry

        lax.fori_loop(0, unit[k], body, 0)

    def spread_rims(k, j, saved):
        tile = wide[k].at[slot_of(k, j)]
        up = g_halo[k][0] if j == 0 else g_v[k][j * unit[k] - 1]
        put_shifted(tile.at[0], masked(up, keep[j]))
        if saved:
            down = edge[...]
        else:
            down = g_halo[k][1] if j == blocks - 1 else g_v[k][(j + 1) * unit[k]]
        put_shifted(tile.at[unit[k] + 1], masked(down, keep[j + 1]))

    near_row = [(1 - at.b) * (rows[k] - 1) for k in range(LEVELS)]
    far_row = [at.b * (rows[k] - 1) for k in range(LEVELS)]
    far = (at.group, at.strip - 1 + 2 * at.b)
    has_far = (at.strip - 1 + 2 * at.b + 1) % (at.count + 1) > 0

    def send_near(row, halo, index):
        kind = ("near", index // LEVELS)
        copies.remote(row, halo.at[at.b], halo_sems.at[index, at.b], at.beside, kind)

    def send_far(row, halo, index):
        kind = ("far", index // LEVELS)
        copies.remote(row, halo.at[1 - at.b], halo_sems.at[index, 1 - at.b], far, kind, has_far)

    def take_rims(halo, index):
        arrived(halo.at[1 - at.b], halo_sems.at[index, 1 - at.b], at.beside)
        pl.when(has_far)(lambda: arrived(halo.at[at.b], halo_sems.at[index, at.b], far))

        def clear():
            halo[at.b] = jnp.zeros(halo.shape[1:], bf16)

        pl.when(jnp.logical_not(has_far))(clear)

    places = [None, *range(at.spans - 1)]
    for k in (2, 1, 0):
        grad_loads[k].wait()
    for k in (3, 2, 1, 0):
        send_far(g_v[k].at[far_row[k]], g_halo[k], k)
    conv.along()
    feature_loads = [copies.local(features[k], c_v[k]) for k in (3, 2, 1, 0)][::-1]
    def spread_level(k):
        def body(r, carry):
            value = g_v[k][r]
            put_shifted(wide[k].at[r // unit[k], lax.rem(r, unit[k]) + 1], value)
            bias_acc[LEVELS + k] += row_sum(value)
            return carry

        lax.fori_loop(0, rows[k], body, 0)

    for k in (3, 2, 1):
        spread_level(k)
    spread(0, 0, True)
    if own_lateral:
        for spot in range(at.spans - 1):
            lateral.from_span(spot)
    for k in (3, 2, 1, 0):
        send_near(g_v[k].at[near_row[k]], g_halo[k], k)
    conv.aside()
    if own_lateral:
        for spot in places:
            lateral.from_beside(spot)
        for spot in places:
            lateral.from_across(spot)
        lateral.from_core()
    for k, device in enumerate(strips):
        owner = lax.rem(at.strip + k + 1, at.count)
        arrived(bias_v.at[owner], bias_sems.at[owner], device)
    per = plan.count // 8
    for j in range(8):
        total = bias_v[j * per]
        for other in range(1, per):
            total = total + bias_v[j * per + other]
        bias_low[j] = total

    def top_values(k, r, count):
        pixels = count * width[k]
        value = jnp.dot(
            c_v[k][pl.ds(r, count)].reshape(pixels, depth[k]),
            lateral_v[plan.bounds[k] : plan.bounds[k + 1], :],
            preferred_element_type=f32,
        )
        value = (value + bias_low[k][0:1, :]).reshape(count, width[k], FPN_CH)
        if k == 3:
            return [value[s] for s in range(count)]
        tops = []
        for s in range(count // 2):
            raised = doubled(pairs, s * width[k], sums[k + 1][r // 2 + s])
            tops += [value[2 * s] + raised, value[2 * s + 1] + raised]
        return tops

    def top_level(k):
        count = min(4, unit[k])
        steps = unit[k] // count

        def body(t, carry):
            tops = top_values(k, t * count, count)
            for s in range(count):
                if k:
                    sums[k][t * count + s] = tops[s]
                x_v[k][t // steps, lax.rem(t, steps) * count + s + 1] = tops[s].astype(bf16)
            return carry

        lax.fori_loop(0, rows[k] // count, body, 0)

    for k in (3, 2, 1, 0):
        feature_loads[k].wait()
        top_level(k)
        for j in range(1, blocks):
            x_v[k][j - 1, unit[k] + 1] = masked(x_v[k][j, 1], keep[j])
            x_v[k][j, 0] = masked(x_v[k][j - 1, unit[k]], keep[j])
        if k == 1:
            conv.from_span(0)
    for k in (3, 2, 1, 0):
        take_rims(g_halo[k], k)
        for j in range(blocks if k else 1):
            spread_rims(k, j, False)

    conv_sum = Scatter(
        "tap sums", plan.conv_rows, (), *conv_parts[0:5], conv_total, at, copies, conv_parts[5:10]
    )
    conv_grad = conv_parts[0]
    if own_lateral:
        lateral_sum = Scatter(
            "lateral sums",
            plan.lateral_rows,
            range(at.spans // 2),
            *lateral_parts[0:5],
            lateral_total,
            at,
            copies,
            lateral_parts[5:10],
        )
    quarter = at.spans // LEVELS

    def spans_of(k):
        return range(k * quarter, (k + 1) * quarter)

    def each(step, items):
        for item in items:
            step(item)

    def for_level(step, k):
        for span in spans_of(k):
            step(span)

    def tap_dots(k, chunks):
        for dy in range(3):
            x = jnp.concatenate(
                [x_v[k][j, pl.ds(i + 1, n)].reshape(n * width[k], FPN_CH) for j, i, n in chunks],
                axis=0,
            )
            g = jnp.concatenate(
                [
                    wide[k][slot_of(k, j), pl.ds(i + dy, n)].reshape(n * width[k], 3 * FPN_CH)
                    for j, i, n in chunks
                ],
                axis=0,
            )
            dot = lax.dot_general(x, g, (((0,), (0,)), ((), ())), preferred_element_type=f32)
            for dx in range(3):
                yield 8 - (3 * dy + dx), dot[:, dx * FPN_CH : (dx + 1) * FPN_CH]

    def tap_grads(k):
        for tap, dot in tap_dots(k, [(j, 0, unit[k]) for j in range(blocks)]):
            start = k * TAPS + tap * FPN_CH
            conv_grad[start : start + FPN_CH, :] = dot.astype(bf16)

    def tap_rows(k, j, first, count):
        for tap, dot in tap_dots(k, [(j, first, count)]):
            acc[tap * FPN_CH : (tap + 1) * FPN_CH, :] += dot

    def x_rims():
        for k in (3, 2, 1, 0):
            send_far(x_v[k].at[at.b * (blocks - 1), 1 + at.b * (unit[k] - 1)], x_halo[k], LEVELS + k)
            send_near(
                x_v[k].at[(1 - at.b) * (blocks - 1), 1 + (1 - at.b) * (unit[k] - 1)],
                x_halo[k],
                LEVELS + k,
            )

    tap_grads(3)
    for_level(conv_sum.start, 3)
    tap_grads(2)
    for_level(conv_sum.start, 2)
    for spot in range(1, at.spans - 1):
        conv.from_span(spot)
    tap_grads(1)
    for_level(conv_sum.start, 1)
    conv.from_beside(None)
    acc[...] = jnp.zeros_like(acc)
    final = at.spans - 2

    def pass_on(spots):
        return lambda: each(conv.from_beside, [spot for spot in spots if spot < final])

    between = [
        pass_on([0]),
        lambda: each(
            lambda run: run(),
            [pass_on([1]), lambda: conv.across_first(final)] + [pass_on(range(2, final))],
        ),
        lambda: each(lambda run: run(), [x_rims, lambda: for_level(conv_sum.first, 3)]),
        lambda: each(lambda k: for_level(conv_sum.first, k), (2, 1)),
    ]
    step = unit[0] // 2

    def tap_half(t, carry):
        j, half = t // 2, lax.rem(t, 2)
        for later in range(1, blocks):

            def renew(later=later):
                spread(0, later, True)
                spread_rims(0, later, False)

            pl.when(t == 2 * later)(renew)
        tap_rows(0, j, half * step, step)
        for place, run in enumerate(between):
            pl.when(t == place)(run)
        return carry

    lax.fori_loop(0, 2 * blocks, tap_half, 0)
    conv_grad[0:TAPS, :] = acc[...].astype(bf16)
    for_level(conv_sum.start, 0)
    for spot in places[:-1]:
        conv.from_across(spot)
    conv.from_beside(final, True)
    conv.from_core()

    def top_rows(k, j, i, count):
        pixels = count * width[k]
        value = None
        for dy in range(3):
            for dx in range(3):
                tap = 8 - (3 * dy + dx)
                start = k * TAPS + tap * FPN_CH
                dot = lax.dot_general(
                    wide[k][
                        slot_of(k, j), pl.ds(i + dy, count), :, dx * FPN_CH : (dx + 1) * FPN_CH
                    ].reshape(pixels, FPN_CH),
                    conv_v[start : start + FPN_CH, :],
                    (((1,), (1,)), ((), ())),
                    preferred_element_type=f32,
                )
                value = dot if value is None else value + dot
        value = value.reshape(count, width[k], FPN_CH)
        first = j * unit[k] + i
        if k:
            value = value + sums[k][pl.ds(first, count)]
        low = value.astype(bf16)
        g_v[k][pl.ds(first, count)] = low
        bias_acc[k] += row_sum(low.reshape(pixels, FPN_CH))
        if k < 3:
            for s in range(count // 2):
                sums[k + 1][first // 2 + s] = halved(
                    pairs, s * width[k], value[2 * s] + value[2 * s + 1]
                )

    def top_level_grads(k):
        count = min(8 if k else 4, unit[k])
        steps = unit[k] // count

        def body(t, carry):
            top_rows(k, t // steps, lax.rem(t, steps) * count, count)
            return carry

        lax.fori_loop(0, rows[k] // count, body, 0)

    copies.settle(("near", 0), at.beside)
    copies.settle(("far", 0), far, has_far)
    steps = unit[0] // 4

    def top_four(t, carry):
        for turn in range(blocks):
            j = blocks - 1 - turn

            def renew(j=j):
                if j < blocks - 1:
                    spread(0, j, False)
                    spread_rims(0, j, True)
                if j:
                    edge[...] = g_v[0][j * unit[0]]

            pl.when(t == turn * steps)(renew)
        top_rows(0, blocks - 1 - t // steps, lax.rem(t, steps) * 4, 4)

        pl.when(t == steps - 1)(lambda: for_level(conv_sum.first, 0))
        pl.when(t == steps)(lambda: for_level(conv_sum.second, 3))
        pl.when(t == blocks * steps - 2)(lambda: for_level(conv_sum.second, 2))
        return carry

    lax.fori_loop(0, blocks * steps, top_four, 0)
    for k in range(1, LEVELS):
        top_level_grads(k)
        if k == 1:
            for_level(conv_sum.second, 1)
            for_level(conv_sum.to_span, 3)
    for_level(conv_sum.to_span, 2)

    for k in (3, 2, 1):
        value = lax.dot_general(
            c_v[k][...].reshape(rows[k] * width[k], depth[k]),
            g_v[k][...].reshape(rows[k] * width[k], FPN_CH),
            (((0,), (0,)), ((), ())),
            preferred_element_type=f32,
        )
        lateral_grad[plan.bounds[k] : plan.bounds[k + 1], :] = value.astype(bf16)
    for_level(conv_sum.second, 0)
    across, core = plan.count, plan.count + 1
    own_bias = jnp.concatenate(
        [jnp.sum(bias_acc[j], axis=0, keepdims=True) for j in range(8)], axis=0
    )
    bias_v[across + 4] = own_bias
    for device in strips:
        copies.remote(
            bias_v.at[across + 4],
            bias_grad_slot(bias_v, plan, at.strip),
            bias_sems.at[across + 2 + at.strip],
            device,
            "bias",
        )
    bias_v[across + 5 + at.strip] = own_bias
    count = min(8, rows[0])
    acc[0 : depth[0], :] = jnp.zeros((depth[0], FPN_CH), f32)

    def lateral_block(i, carry):
        acc[0 : depth[0], :] += lax.dot_general(
            c_v[0][pl.ds(i * count, count)].reshape(count * width[0], depth[0]),
            g_v[0][pl.ds(i * count, count)].reshape(count * width[0], FPN_CH),
            (((0,), (0,)), ((), ())),
            preferred_element_type=f32,
        )
        return carry

    spans = range(at.spans)
    late = [span for span in spans if span * 2 * plan.lateral_rows < depth[0]]
    if own_lateral:
        for span in spans:
            if span not in late:
                lateral_sum.start(span)
    lax.fori_loop(0, rows[0] // count, lateral_block, 0)
    lateral_grad[0 : depth[0], :] = acc[0 : depth[0], :].astype(bf16)
    if own_lateral:
        for span in late:
            lateral_sum.start(span)
        for span in spans:
            if span not in late:
                lateral_sum.first(span)

    for_level(conv_sum.to_span, 1)

    outs = []
    for k in range(LEVELS):
        count = max(1, min(rows[k], 1024 // width[k]))

        def feature_block(i, carry, k=k, count=count):
            value = lax.dot_general(
                g_v[k][pl.ds(i * count, count)].reshape(count * width[k], FPN_CH),
                lateral_v[plan.bounds[k] : plan.bounds[k + 1], :],
                (((1,), (1,)), ((), ())),
                preferred_element_type=f32,
            )
            c_v[k][pl.ds(i * count, count)] = value.astype(bf16).reshape(count, width[k], depth[k])
            return carry

        lax.fori_loop(0, rows[k] // count, feature_block, 0)
        if k == 0:
            if own_lateral:
                for span in late:
                    lateral_sum.first(span)
            for_level(conv_sum.to_span, 0)

    for k in range(LEVELS):
        take_rims(x_halo[k], LEVELS + k)
        x_v[k][0, 0] = masked(x_halo[k][0], keep[0])
        x_v[k][blocks - 1, unit[k] + 1] = masked(x_halo[k][1], keep[blocks])

    def widen(k, j):
        tile = wide[k].at[slot_of(k, j)]

        def body(i, carry):
            put_shifted(tile.at[i], x_v[k][j, i])
            return carry

        lax.fori_loop(0, unit[k] + 2, body, 0)

    def pyramid_rows(k, j, i, count):
        pixels = count * width[k]
        value = jnp.dot(
            jnp.concatenate(
                [
                    wide[k][slot_of(k, j), pl.ds(i + dy, count)].reshape(pixels, 3 * FPN_CH)
                    for dy in range(3)
                ],
                axis=1,
            ),
            conv_v[k * TAPS : (k + 1) * TAPS, :],
            preferred_element_type=f32,
        )
        value = (value + bias_low[LEVELS + k][0:1, :]).reshape(count, width[k], FPN_CH)
        first = j * unit[k] + i
        g_v[k][pl.ds(first, count)] = value.astype(bf16)
        if k == 3:
            for s in range(count // 2):
                mean = 0.25 * halved(pairs, 0, value[2 * s] + value[2 * s + 1])
                p6_new[first // 2 + s] = mean.astype(bf16)

    def pyramid_block(k):
        count = min(8 if k else 4, unit[k])
        steps = unit[k] // count

        def widen_block(j, carry):
            widen(k, j)
            return carry

        def body(t, carry):
            pyramid_rows(k, t // steps, lax.rem(t, steps) * count, count)
            return carry

        lax.fori_loop(0, blocks, widen_block, 0)
        lax.fori_loop(0, rows[k] // count, body, 0)

    def end_close():
        conv_sum.close()

    def end_bias():
        arrived(bias_v.at[core], bias_sems.at[core], at.core)
        own = pl.ds(at.strip // per, 1)
        bias_total[...] = bias_v[across + 3, own, :] + bias_v[core, own, :]

    def end_drain():
        if not pinned:
            for source, target in zip([*g_v, p6_new, *c_v], held):
                outs.append(copies.local(source, target))
        for copy in outs:
            copy.wait()
        copies.settle(("far", 1), far, has_far)
        for kind in [kind for kind, (place, size) in copies.kinds.items() if size]:
            copies.settle(kind, at.core)

    pyramid_block(1)
    if own_lateral:
        for span in spans:
            lateral_sum.second(span)
    for k in range(2, LEVELS):
        pyramid_block(k)
    def end_first():
        conv_sum.finish()
        for k, device in enumerate(strips):
            owner = lax.rem(at.strip + k + 1, at.count)
            arrived(bias_grad_slot(bias_v, plan, owner), bias_sems.at[across + 2 + owner], device)
        total = bias_v[across + 5]
        for k in range(1, plan.count):
            total = total + bias_v[across + 5 + k]
        bias_v[across + 2] = total
        copies.remote(
            bias_v.at[across + 2], bias_v.at[across], bias_sems.at[across], at.across, "bias"
        )
        if own_lateral:
            for span in spans:
                lateral_sum.to_span(span)

    def end_second():
        conv_sum.join()
        arrived(bias_v.at[across], bias_sems.at[across], at.across)
        total = bias_v[across + 2] + bias_v[across]
        bias_v[across + 3] = total
        copies.remote(
            bias_v.at[across + 3], bias_v.at[core], bias_sems.at[core], at.core, "bias"
        )

    def end_third():
        if own_lateral:
            lateral_sum.finish()

    def pyramid_four(t, carry):
        j, i = t // steps, lax.rem(t, steps)
        pl.when(i == 0)(lambda: widen(0, j))
        pyramid_rows(0, j, i * 4, 4)
        pl.when(t == 1)(end_first)
        pl.when(t == (blocks - 1) * steps)(end_second)
        pl.when(t == (blocks - 1) * steps + 1)(end_third)
        return carry

    lax.fori_loop(0, blocks * steps, pyramid_four, 0)
    end_close()
    end_bias()
    if own_lateral:
        lateral_sum.join()
        lateral_sum.close()
    else:
        outs.append(copies.local(lateral_grad, lateral_total))
    end_drain()


def bias_grad_slot(bias_v, plan, owner):
    return bias_v.at[plan.count + 5 + owner]


def whole_step(plan, own_lateral, features, grads, coarse_grad, image_heights, lateral, conv, bias):
    rows, width, depth, unit, blocks = plan.rows, plan.width, plan.depth, plan.unit, plan.blocks
    shape = jax.ShapeDtypeStruct
    v = pltpu.VMEM
    total = plan.bounds[LEVELS]
    coarse = (rows[3] // 2, width[3] // 2, FPN_CH)
    pinned = own_lateral
    shapes = [(rows[k], width[k], FPN_CH) for k in range(LEVELS)] + [coarse]
    shapes += [(rows[k], width[k], depth[k]) for k in range(LEVELS)]
    out_shape = (
        [(v if pinned else shape)(s, bf16) for s in shapes]
        + [(v if pinned else shape)((plan.conv_rows, FPN_CH), bf16)]
        + [v((plan.lateral_rows, FPN_CH), bf16) if pinned else shape((total, FPN_CH), bf16)]
        + [shape((1, FPN_CH), f32)]
    )
    dma = pltpu.SemaphoreType.DMA
    scratch = (
        ([] if pinned else [v(s, bf16) for s in shapes])
        + [v(coarse, bf16)]
        + [v((blocks if k else 1, unit[k] + 2, width[k], 3 * FPN_CH), bf16) for k in range(LEVELS)]
        + [v((blocks, unit[k] + 2, width[k], FPN_CH), bf16) for k in range(LEVELS)]
        + [v((rows[k], width[k], FPN_CH), f32) for k in (1, 2, 3)]
        + [v((LEVELS * TAPS, FPN_CH), bf16), v((total, FPN_CH), bf16)]
        + [v((2 * plan.count + 5, 8, FPN_CH), f32), v((8, 8, FPN_CH), f32)]
        + [v((TAPS, FPN_CH), f32), v((FPN_CH // HALF, 2 * width[0], HALF), f32)]
        + [v((width[0], FPN_CH), bf16), v((8, 8, FPN_CH), f32)]
        + [v((2, width[k], FPN_CH), bf16) for k in range(LEVELS)] * 2
        + [dma((16 + plan.count // 2,)), dma((24,)), dma((2,))]
        + [dma((plan.count, 2)), dma((plan.count, 2))]
        + [dma((2 * plan.count + 2,)), dma((2 * LEVELS, 2))]
        + scatter_shapes(plan.conv_rows, plan.count, False)
        + (
            scatter_shapes(plan.lateral_rows, plan.count, True)
            if own_lateral
            else [v((total, FPN_CH), bf16)]
        )
    )
    return pl.pallas_call(
        functools.partial(step_kernel, plan, own_lateral, pinned),
        out_shape=out_shape,
        in_specs=[ANY] * 9 + [pl.BlockSpec(memory_space=pltpu.SMEM), ANY, ANY, VMEM],
        out_specs=[VMEM if pinned else ANY] * 9 + [VMEM, VMEM if own_lateral else ANY, VMEM],
        scratch_shapes=scratch,
        name="step",
        cost_estimate=pl.CostEstimate(
            flops=45 << 30, bytes_accessed=60 << 20, transcendentals=0
        ),
        compiler_params=pltpu.CompilerParams(
            collective_id=0, has_side_effects=True, vmem_limit_bytes=ROOM if pinned else WHOLE_ROOM
        ),
    )(*features, *grads, coarse_grad, image_heights, lateral, conv, bias)


def update_kernel(count, *refs):
    refs = list(refs)

    def take(number):
        taken = refs[:number]
        del refs[:number]
        return taken

    held = take(count)
    sums = take(3)
    given = [take(3), take(3), take(3)]
    held_out = take(count)
    results = [take(3), take(3), take(3)]
    work = [take(3), take(3)]
    (sems,) = take(1)
    used = [0]

    def begin(source, target):
        copy = pltpu.make_async_copy(source, target, sems.at[used[0]])
        used[0] += 1
        copy.start()
        return copy

    loads = [[begin(given[i][j], work[i][j]) for j in range(3)] for i in range(2)]
    outs = [begin(source, target) for source, target in zip(held, held_out)]
    rates = ((conv_rate, decay_rate), (lateral_rate, decay_rate), (bias_rate, 0.0))
    for i in range(2):
        for load in loads[i]:
            load.wait()
        rows = work[i][0].shape[0]
        step = next(size for size in (96, 48, 16, rows) if rows % size == 0)

        def update(r, carry, i=i, step=step):
            part = pl.ds(r * step, step)
            weight, moment, average = (work[i][j][part, :] for j in range(3))
            total = sums[i][part, :].astype(f32)
            new = nesterov(weight, total, moment, average, *rates[i])
            for j in range(3):
                work[i][j][part, :] = new[j]
            return carry

        lax.fori_loop(0, rows // step, update, 0)
        outs += [begin(work[i][j], results[i][j]) for j in range(3)]
    weight, moment, average = (given[2][j][...] for j in range(3))
    new = nesterov(weight, sums[2][...], moment, average, *rates[2])
    for j in range(3):
        results[2][j][...] = new[j]
    for copy in outs:
        copy.wait()


def update(held, sums, given):
    shape = jax.ShapeDtypeStruct
    place = pltpu.with_memory_space_constraint
    kept = [place(x, pltpu.VMEM) for x in held]
    far = [place(x, pltpu.HBM) for g in given[:2] for x in g]
    results = [shape(g[0].shape, f32) for g in given for _ in range(3)]
    return pl.pallas_call(
        functools.partial(update_kernel, len(held)),
        out_shape=[shape(x.shape, x.dtype) for x in held] + results,
        in_specs=[ANY] * len(held) + [VMEM] * 3 + [HBM] * 6 + [VMEM] * 3,
        out_specs=[HBM] * (len(held) + 6) + [VMEM] * 3,
        scratch_shapes=[pltpu.VMEM(g[0].shape, f32) for g in given[:2] for _ in range(3)]
        + [pltpu.SemaphoreType.DMA((len(held) + 12,))],
        name="update",
        cost_estimate=pl.CostEstimate(flops=8 << 20, bytes_accessed=25 << 20, transcendentals=0),
        compiler_params=pltpu.CompilerParams(vmem_limit_bytes=24 << 20),
    )(*kept, *sums, *far, *given[2])


def shards(
    feature_c2,
    feature_c3,
    feature_c4,
    feature_c5,
    cotangent_p2,
    cotangent_p3,
    cotangent_p4,
    cotangent_p5,
    cotangent_p6,
    image_heights,
    lateral_weight,
    conv_weight,
    bias_all,
    lateral_momentum,
    conv_momentum,
    bias_momentum,
    lateral_ema,
    conv_ema,
    bias_ema,
):
    features = (feature_c2, feature_c3, feature_c4, feature_c5)
    grads = (cotangent_p2, cotangent_p3, cotangent_p4, cotangent_p5)
    count = lax.axis_size("rows")
    strip = lax.axis_index("rows")
    plan = Plan(features, count, lateral_weight.shape[0], conv_weight.shape[0])
    own_lateral = plan.lateral_rows % 16 == 0
    share = bias_all.shape[0]
    if share == FPN_CH:
        bias_row = bias_all.reshape(1, FPN_CH)
    else:
        place = lax.rem(strip * share, FPN_CH)
        lane = jnp.arange(FPN_CH)
        inside = jnp.logical_and(lane >= place, lane < place + share)
        bias_row = jnp.where(inside, jnp.tile(bias_all, FPN_CH // share), 0.0)[None, :]
    if own_lateral:
        lateral_in = lateral_weight
    else:
        lateral_in = lax.all_gather(lateral_weight.astype(bf16), "rows", axis=0, tiled=True)
    results = whole_step(
        plan,
        own_lateral,
        features,
        grads,
        cotangent_p6,
        image_heights,
        lateral_in,
        conv_weight,
        bias_row,
    )
    sum_conv, sum_lateral, sum_bias = results[9:]
    if not own_lateral:
        sum_lateral = lax.psum(
            lax.psum_scatter(sum_lateral, "rows", scatter_dimension=0, tiled=True), "grp"
        ).astype(f32)
    row = (1, share)
    if share < FPN_CH:
        sum_bias = lax.dynamic_slice_in_dim(sum_bias, place, share, axis=1)
    held = results[:9] if own_lateral else []
    new = update(
        held,
        (sum_conv, sum_lateral, sum_bias),
        (
            (conv_weight, conv_momentum, conv_ema),
            (lateral_weight, lateral_momentum, lateral_ema),
            (bias_all.reshape(row), bias_momentum.reshape(row), bias_ema.reshape(row)),
        ),
    )
    held = new[: len(held)] or results[:9]
    first = len(new) - 9
    conv_new, lateral_new, bias_new = (new[first + i : first + i + 3] for i in (0, 3, 6))
    return (
        *held,
        lateral_new[0],
        conv_new[0],
        bias_new[0].reshape(share),
        lateral_new[1],
        conv_new[1],
        bias_new[1].reshape(share),
        lateral_new[2],
        conv_new[2],
        bias_new[2].reshape(share),
    )


def solution(mesh):
    cut = P(("grp", "rows"), None, None)
    wide = P("rows", None)
    in_specs = (cut,) * 9 + (P("grp", None),) + (wide, wide, P("rows")) * 3
    out_specs = (cut,) * 9 + (wide, wide, P("rows")) * 3
    return jax.shard_map(
        shards,
        mesh=mesh,
        in_specs=in_specs,
        out_specs=out_specs,
        check_vma=False,
    )
```
